512 devices in a mesh: gx: 128 (over y, z, core), gy: 4 (over x).
Axes of the slice: x: 4, y: 4, z: 16, core: 2. Of those that a mesh axis runs over, the one named last changes fastest.
Arguments:
- populations: float32 [256, 19, 64, 256], P('gx', None, 'gy'), may hold values from 0.013 to 0.5, as said below
- cotangent: bfloat16 [256, 19, 64, 256], P('gx', None, 'gy'), may hold values from -12 to 12
- flags: int32 [256, 64, 256], P('gx', 'gy'), may hold values 0 or 1
- w_in: bfloat16 [128, 19], replicated, may hold values from -4 to 4
- b_in: float32 [128], replicated, may hold values from -3 to 3
- w_out: bfloat16 [19, 128], replicated, may hold values from -0.02734375 to 0.02734375
Outputs:
- adjoint_pops: bfloat16 [256, 19, 64, 256], P('gx', None, 'gy')
- grad_w_in: float32 [128, 19], replicated
- grad_b_in: float32 [128], replicated
- grad_w_out: float32 [19, 128], replicated
The draws below stay inside these ranges and needn't reach their ends.
Inputs may be any that keep to these rules, and one draw needn't show every extreme that they name: populations are positive at every cell and velocity.
All inputs are finite; a program needn't handle non-finite values. No bound on the sum of `flags` on one device may be relied on, other than what follows from the above.
Results may differ from the reference program's by a relative error of at most 0.012.
The reference program's roundings to bfloat16 on the way count: a program that leaves them out, or rounds other values in their place, can miss the bound.
Values sent between devices are 32-bit elements; how exact they have to be, the bound alone decides.
A program may use at most 64 MiB of HBM per device.

```python
import jax
import jax.numpy as jnp
from jax import lax

Q = 19
UNITS = 128
NZ = 256
NX = 256
NY = 64


LATTICE_WEIGHTS = [1.0 / 3.0] + [1.0 / 18.0] * 6 + [1.0 / 36.0] * 12


POPULATION_SALT = 11


COTANGENT_SALT = 29


def draw_populations(key, part):
    own_key = jax.random.fold_in(key, POPULATION_SALT)
    shape = (NX, Q, NY, NZ)
    weights = jnp.asarray(LATTICE_WEIGHTS, jnp.float32)[None, :, None, None]
    spread = jax.random.uniform(own_key, shape, jnp.float32, -0.5, 0.5)
    return weights * (1.0 + spread)


def draw_cotangent(key, part):
    own_key = jax.random.fold_in(key, COTANGENT_SALT)
    shape = (NX, Q, NY, NZ)
    rising = 1.0 + 2.0 * jnp.arange(NX, dtype=jnp.float32) / max(NX - 1, 1)
    base = jnp.clip(jax.random.normal(own_key, shape, jnp.float32), -4.0, 4.0)
    return (base * rising[:, None, None, None]).astype(jnp.bfloat16)


def set_ends(values, stream_key, smallest, largest):
    longest = values.shape.index(max(values.shape))
    spots = []
    for shift in (0, 1):
        where = [jax.random.randint(jax.random.fold_in(stream_key, axis), (), 0, length) for axis, length in enumerate(values.shape)]
        where[longest] = (where[longest] + shift) % values.shape[longest]
        spots.append(tuple(where))
    return values.at[spots[0]].set(smallest).at[spots[1]].set(largest)


def scatter_about(rng, extent, scale, reach, held_as=jnp.bfloat16):
    return jnp.clip(scale * jax.random.normal(rng, extent, jnp.float32), -reach, reach).astype(held_as)


def setup_inputs(seed: int = 0) -> dict:
    splits = jax.random.split(jax.random.key(seed), 7)
    return {
        "populations": draw_populations(jax.random.fold_in(splits[6], 71), 0),
        "cotangent": draw_cotangent(jax.random.fold_in(splits[6], 71), 0),
        "flags": set_ends((jax.random.randint(splits[2], (NX, NY, NZ), 0, 4) < 3).astype(jnp.int32), jax.random.fold_in(splits[2], 1), 0, 1),
        "w_in": scatter_about(splits[3], (UNITS, Q), 2 ** -0.5, 4.0),
        "b_in": scatter_about(splits[4], (UNITS,), 0.5, 3.0, jnp.float32),
        "w_out": scatter_about(splits[5], (Q, UNITS), (UNITS * 400) ** -0.5, 0.02734375),
    }


VELOCITY = [(0, 0, 0), (1, 0, 0), (-1, 0, 0), (0, 1, 0), (0, -1, 0), (0, 0, 1), (0, 0, -1), (1, 1, 0), (-1, -1, 0), (1, -1, 0), (-1, 1, 0), (1, 0, 1), (-1, 0, -1), (1, 0, -1), (-1, 0, 1), (0, 1, 1), (0, -1, -1), (0, 1, -1), (0, -1, 1)]
OPPOSITE = [0, 2, 1, 4, 3, 6, 5, 8, 7, 10, 9, 12, 11, 14, 13, 16, 15, 18, 17]
LATTICE_WEIGHTS = [1.0 / 3.0] + [1.0 / 18.0] * 6 + [1.0 / 36.0] * 12
TAU_INV = 1.25
BUOYANCY = 0.05

def lattice_tables():
    vel_x = jnp.asarray([float(v[0]) for v in VELOCITY], jnp.float32)[:, None]
    vel_y = jnp.asarray([float(v[1]) for v in VELOCITY], jnp.float32)[:, None]
    vel_z = jnp.asarray([float(v[2]) for v in VELOCITY], jnp.float32)[:, None]
    weights = jnp.asarray(LATTICE_WEIGHTS, jnp.float32)[:, None]
    return (vel_x, vel_y, vel_z, weights)

def equilibrium_parts(pops):
    vel_x, vel_y, vel_z, weights = lattice_tables()
    density = lax.optimization_barrier(jnp.sum(pops, axis=0))
    momentum_x = lax.optimization_barrier(jnp.sum(vel_x * pops, axis=0))
    momentum_y = lax.optimization_barrier(jnp.sum(vel_y * pops, axis=0))
    momentum_z = lax.optimization_barrier(jnp.sum(vel_z * pops, axis=0))
    projected = vel_x * momentum_x + vel_y * momentum_y + vel_z * momentum_z
    momentum_sq = momentum_x * momentum_x + momentum_y * momentum_y + momentum_z * momentum_z
    equilibrium = weights * (density + 3.0 * projected + 4.5 * projected * projected - 1.5 * momentum_sq)
    return (density, (momentum_x, momentum_y, momentum_z), projected, equilibrium)

def network_front(pops, equilibrium, w_in, b_in):
    weights = lattice_tables()[3]
    features = ((pops - equilibrium) / weights).astype(jnp.bfloat16)
    preact = jnp.dot(w_in, features, preferred_element_type=jnp.float32) + b_in[:, None]
    return (features, preact)

def collide_plane(pops, melt, w_in, b_in, w_out):
    vel_x, vel_y, vel_z, weights = lattice_tables()
    density, momentum, projected, equilibrium = equilibrium_parts(pops)
    features, preact = network_front(pops, equilibrium, w_in, b_in)
    hidden = jnp.tanh(preact).astype(jnp.bfloat16)
    learned = jnp.dot(w_out, hidden, preferred_element_type=jnp.float32)
    lift = 3.0 * BUOYANCY * weights * vel_z
    relaxed = pops - TAU_INV * (pops - equilibrium) + learned + lift * (density - 1.0)
    bounced = jnp.stack([pops[k] for k in OPPOSITE], axis=0)
    return jnp.where(melt > 0.5, relaxed, bounced)

def adjoint_plane(pops, melt, incoming, w_in, b_in, w_out):
    vel_x, vel_y, vel_z, weights = lattice_tables()
    density, momentum, projected, equilibrium = equilibrium_parts(pops)
    features, preact = network_front(pops, equilibrium, w_in, b_in)
    activity = jnp.tanh(preact)
    hidden = activity.astype(jnp.bfloat16)
    melt_adj = incoming * melt
    solid_adj = incoming - melt_adj
    grad_out = melt_adj.astype(jnp.bfloat16)
    contract = (((1,), (1,)), ((), ()))
    grad_w_out = lax.dot_general(grad_out, hidden, contract, preferred_element_type=jnp.float32)
    grad_hidden = jnp.dot(w_out.T, grad_out, preferred_element_type=jnp.float32)
    grad_preact = (grad_hidden * (1.0 - activity * activity)).astype(jnp.bfloat16)
    grad_w_in = lax.dot_general(grad_preact, features, contract, preferred_element_type=jnp.float32)
    grad_b_in = lax.optimization_barrier(jnp.sum(grad_preact, axis=1, dtype=jnp.float32))
    grad_noneq = jnp.dot(w_in.T, grad_preact, preferred_element_type=jnp.float32) / weights
    grad_equil = TAU_INV * melt_adj - grad_noneq
    weighted = weights * grad_equil
    lift = 3.0 * BUOYANCY * weights * vel_z
    grad_density = lax.optimization_barrier(jnp.sum(weighted, axis=0)) + lax.optimization_barrier(jnp.sum(lift * melt_adj, axis=0))
    slope_terms = weighted * (3.0 + 9.0 * projected)
    weighted_total = lax.optimization_barrier(jnp.sum(weighted, axis=0))
    grad_mx = lax.optimization_barrier(jnp.sum(vel_x * slope_terms, axis=0)) - 3.0 * momentum[0] * weighted_total
    grad_my = lax.optimization_barrier(jnp.sum(vel_y * slope_terms, axis=0)) - 3.0 * momentum[1] * weighted_total
    grad_mz = lax.optimization_barrier(jnp.sum(vel_z * slope_terms, axis=0)) - 3.0 * momentum[2] * weighted_total
    bounced = jnp.stack([solid_adj[k] for k in OPPOSITE], axis=0)
    grad_pops = (1.0 - TAU_INV) * melt_adj + grad_noneq + grad_density + vel_x * grad_mx + vel_y * grad_my + vel_z * grad_mz + bounced
    return (grad_pops, (grad_w_in, grad_b_in, grad_w_out))

def collide_field(field, flags, w_in, b_in, w_out):

    def one_plane(inputs):
        plane, flag_plane = inputs
        result = collide_plane(plane.reshape(plane.shape[0], -1), flag_plane.reshape(-1).astype(jnp.float32), w_in, b_in, w_out)
        return result.reshape(plane.shape)
    return lax.map(one_plane, (field, flags))

def adjoint_field(field, flags, incoming, w_in, b_in, w_out):
    units = w_in.shape[0]
    width = w_in.shape[1]
    start = (jnp.zeros((units, width), jnp.float32), jnp.zeros((units,), jnp.float32), jnp.zeros((width, units), jnp.float32))

    def one_plane(carry, inputs):
        plane, flag_plane, grad_plane = inputs
        grad_pops, grads = adjoint_plane(plane.reshape(plane.shape[0], -1), flag_plane.reshape(-1).astype(jnp.float32), grad_plane.reshape(plane.shape[0], -1), w_in, b_in, w_out)
        return (tuple((c + g for c, g in zip(carry, grads))), grad_pops.reshape(plane.shape))
    totals, grad_field = lax.scan(one_plane, start, (field, flags, incoming))
    return (totals, grad_field)

def stream_global(field, sign):
    comps = []
    for comp in range(len(VELOCITY)):
        step_x, step_y, step_z = [sign * v for v in VELOCITY[comp]]
        comps.append(jnp.roll(field[:, comp], (step_x, step_y, step_z), axis=(0, 1, 2)))
    return jnp.stack(comps, axis=1)

def normalized(total):
    return total / jnp.sqrt(jnp.mean(total * total) + 1e-06)

def reference(populations, cotangent, flags, w_in, b_in, w_out):
    post = collide_field(populations, flags, w_in, b_in, w_out)
    shifted = stream_global(post, 1)
    incoming = stream_global(cotangent.astype(jnp.float32), -1)
    grads_late, back_late = adjoint_field(shifted, flags, incoming, w_in, b_in, w_out)
    before = stream_global(back_late, -1)
    grads_early, back_early = adjoint_field(populations, flags, before, w_in, b_in, w_out)
    totals = [a + b for a, b in zip(grads_early, grads_late)]
    return (back_early.astype(jnp.bfloat16), normalized(totals[0]), normalized(totals[1]), normalized(totals[2]))
```

```python
import functools

import jax
import jax.numpy as jnp
from jax import lax
from jax.experimental import pallas as pl
from jax.experimental.pallas import tpu as pltpu
from jax.sharding import PartitionSpec as P

VELOCITY = [
    (0, 0, 0),
    (1, 0, 0),
    (-1, 0, 0),
    (0, 1, 0),
    (0, -1, 0),
    (0, 0, 1),
    (0, 0, -1),
    (1, 1, 0),
    (-1, -1, 0),
    (1, -1, 0),
    (-1, 1, 0),
    (1, 0, 1),
    (-1, 0, -1),
    (1, 0, -1),
    (-1, 0, 1),
    (0, 1, 1),
    (0, -1, -1),
    (0, 1, -1),
    (0, -1, 1),
]
OPPOSITE = [0, 2, 1, 4, 3, 6, 5, 8, 7, 10, 9, 12, 11, 14, 13, 16, 15, 18, 17]
INV_W = [3.0] + [18.0] * 6 + [36.0] * 12
W = [1.0 / 3.0] + [1.0 / 18.0] * 6 + [1.0 / 36.0] * 12
PAIRS = [(i, i + 1) for i in range(1, 19, 2)]
Q = 19
UNITS = 128
ROWS = 160
DEPTH = 256
HID = 8 * UNITS
LANES = 256
GROUPS = 4

X_PLUS = [1, 7, 9, 11, 13]
X_MINUS = [2, 8, 10, 12, 14]
Y_PLUS = [(3, 0), (3, 1), (15, 0), (15, 1), (17, 0), (17, 1), (7, 0), (10, 1)]
Y_MINUS = [(4, 0), (4, 1), (16, 0), (16, 1), (18, 0), (18, 1), (9, 0), (8, 1)]
CORNERS = [7, 10, 8, 9]
MESH = pl.DeviceIdType.MESH
BF = jnp.bfloat16
F32 = jnp.float32
NT = (((1,), (1,)), ((), ()))
TN = (((0,), (0,)), ((), ()))


class Exchange:
    def __init__(self, refs):
        (self.own, self.sxp, self.sxm, self.syp, self.sym, self.rxl, self.rxr,
         self.ryl, self.ryu, self.rc, self.send, self.recv) = refs

    def put(self, j, p, s, val):
        cx, cy, cz = VELOCITY[j]
        if cz:
            val = pltpu.roll(val, cz % LANES, 1)
        rows = pl.ds(8 * s, 8)
        if cx == 1 and p == 1:
            self.sxp[X_PLUS.index(j), rows, :] = val
        elif cx == -1 and p == 0:
            self.sxm[X_MINUS.index(j), rows, :] = val
        else:
            self.own[p, j, rows, :] = val
        if cy == 1 and s == 1 and (j, p) in Y_PLUS:
            k = Y_PLUS.index((j, p))
            self.syp[k : k + 1, :] = val[7:8, :]
        if cy == -1 and s == 0 and (j, p) in Y_MINUS:
            k = Y_MINUS.index((j, p))
            self.sym[k : k + 1, :] = val[0:1, :]

    def copies(self, gx, gy):
        xr, xl = lax.rem(gx + 1, 128), lax.rem(gx + 127, 128)
        yu, yd = lax.rem(gy + 1, 4), lax.rem(gy + 3, 4)
        plan = [
            (self.sxp.at[:, :, :], self.rxl.at[:, :, :], (xr, gy)),
            (self.sxm.at[:, :, :], self.rxr.at[:, :, :], (xl, gy)),
            (self.syp.at[:, :], self.ryl.at[:, :], (gx, yu)),
            (self.sym.at[:, :], self.ryu.at[:, :], (gx, yd)),
            (self.sxp.at[1, pl.ds(8, 8), :], self.rc.at[0], (xr, yu)),
            (self.sxm.at[2, pl.ds(8, 8), :], self.rc.at[1], (xl, yu)),
            (self.sxm.at[1, pl.ds(0, 8), :], self.rc.at[2], (xl, yd)),
            (self.sxp.at[2, pl.ds(0, 8), :], self.rc.at[3], (xr, yd)),
        ]
        return [
            pltpu.make_async_remote_copy(
                src_ref=src, dst_ref=dst, send_sem=self.send.at[k], recv_sem=self.recv.at[k],
                device_id=dev, device_id_type=MESH,
            )
            for k, (src, dst, dev) in enumerate(plan)
        ]

    def get(self, j, p, s):
        cx, cy, cz = VELOCITY[j]
        q = p - cx
        if q == -1:
            src = self.rxl.at[X_PLUS.index(j)]
        elif q == 2:
            src = self.rxr.at[X_MINUS.index(j)]
        else:
            src = self.own.at[q, j]
        if cy == 0:
            return src[8 * s : 8 * s + 8, :]
        row = lax.broadcasted_iota(jnp.int32, (8, LANES), 0)
        if cy == 1:
            if s == 1:
                return src[7:15, :]
            if q in (0, 1):
                k = Y_PLUS.index((j, q))
                halo = self.ryl[k : k + 1, :]
            else:
                halo = self.rc[CORNERS.index(j), 7:8, :]
            return jnp.where(row == 0, halo, pltpu.roll(src[0:8, :], 1, 0))
        if s == 0:
            return src[1:9, :]
        if q in (0, 1):
            k = Y_MINUS.index((j, q))
            halo = self.ryu[k : k + 1, :]
        else:
            halo = self.rc[CORNERS.index(j), 0:1, :]
        return jnp.where(row == 7, halo, pltpu.roll(src[8:16, :], 7, 0))


EX_SCRATCH = [
    pltpu.VMEM((2, Q, 16, LANES), F32),
    pltpu.VMEM((5, 16, LANES), F32),
    pltpu.VMEM((5, 16, LANES), F32),
    pltpu.VMEM((8, LANES), F32),
    pltpu.VMEM((8, LANES), F32),
    pltpu.VMEM((5, 16, LANES), F32),
    pltpu.VMEM((5, 16, LANES), F32),
    pltpu.VMEM((8, LANES), F32),
    pltpu.VMEM((8, LANES), F32),
    pltpu.VMEM((4, 8, LANES), F32),
    pltpu.SemaphoreType.DMA((8,)),
    pltpu.SemaphoreType.DMA((8,)),
]
N_EX = len(EX_SCRATCH)


def dot(a, b, dims=None):
    if dims is None:
        return jnp.dot(a, b, preferred_element_type=F32)
    return lax.dot_general(a, b, dims, preferred_element_type=F32)


def moments(f):
    rho = f[0]
    for a, b in PAIRS:
        rho = rho + (f[a] + f[b])
    mom = []
    for d in range(3):
        acc = None
        for a, b in PAIRS:
            c = VELOCITY[a][d]
            if c == 0:
                continue
            diff = f[a] - f[b] if c == 1 else f[b] - f[a]
            acc = diff if acc is None else acc + diff
        mom.append(acc)
    return rho, mom


def along(i, vec):
    out = None
    for d in range(3):
        c = VELOCITY[i][d]
        if c == 0:
            continue
        if out is None:
            out = vec[d] if c == 1 else -vec[d]
        else:
            out = out + vec[d] if c == 1 else out - vec[d]
    return out


def equilibrium(rho, mom):
    base = rho - 1.5 * (mom[0] * mom[0] + mom[1] * mom[1] + mom[2] * mom[2])
    eq = [base]
    for a, b in PAIRS:
        u = along(a, mom)
        even = base + 4.5 * (u * u)
        odd = 3.0 * u
        eq.append(even + odd)
        eq.append(even - odd)
    return eq


def store_features(dst, lanes, vals):
    for k in range(0, len(vals), 2):
        two = jnp.concatenate([vals[k], vals[k + 1]], axis=0)
        dst[8 * k : 8 * k + 16, lanes] = two.astype(BF)


def build_weights(w_in, b_in, w_out, w1, w1t, w2, w2t):
    comp_of = lax.broadcasted_iota(jnp.int32, (Q, DEPTH), 1) // 8
    expand = (lax.broadcasted_iota(jnp.int32, (Q, DEPTH), 0) == comp_of).astype(F32).astype(BF)
    comp_of_t = lax.broadcasted_iota(jnp.int32, (ROWS, Q), 0) // 8
    expand_t = (lax.broadcasted_iota(jnp.int32, (ROWS, Q), 1) == comp_of_t).astype(F32).astype(BF)
    hi = b_in[...].astype(BF)
    rest = b_in[...] - hi.astype(F32)
    mid = rest.astype(BF)
    low = (rest - mid.astype(F32)).astype(BF)
    row = lax.broadcasted_iota(jnp.int32, (8, UNITS), 0)
    parts = jnp.where(
        row == 0, hi.astype(F32),
        jnp.where(row == 1, mid.astype(F32), jnp.where(row == 2, low.astype(F32), 0.0)),
    ).astype(BF)
    place = (
        lax.broadcasted_iota(jnp.int32, (8, DEPTH), 1)
        == lax.broadcasted_iota(jnp.int32, (8, DEPTH), 0) + 8 * Q
    ).astype(F32).astype(BF)
    in_rep = dot(w_in[...], expand)
    bias_rep = dot(parts, place, TN)
    out_rep = dot(w_out[...], expand, TN)
    in_rep_t = dot(expand_t, w_in[...], NT)
    out_rep_t = dot(expand_t, w_out[...])
    lane = lax.broadcasted_iota(jnp.int32, (UNITS, DEPTH), 1) % 8
    sub = lax.broadcasted_iota(jnp.int32, (ROWS, UNITS), 0) % 8
    for y in range(8):
        block = pl.ds(UNITS * y, UNITS)
        w1[block, :] = (jnp.where(lane == y, in_rep, 0.0) + bias_rep).astype(BF)
        w2t[block, :] = jnp.where(lane == y, out_rep, 0.0).astype(BF)
        w1t[:, block] = jnp.where(sub == y, in_rep_t, 0.0).astype(BF)
        w2[:, block] = jnp.where(sub == y, out_rep_t, 0.0).astype(BF)


def kernel(pops, cot, flags, w_in, b_in, w_out, d0_ref, grads_ref, *scratch):
    gx, gy = lax.axis_index("gx"), lax.axis_index("gy")
    ex_c = Exchange(scratch[:N_EX])
    ex_p = Exchange(scratch[N_EX : 2 * N_EX])
    ex_d = Exchange(scratch[2 * N_EX : 3 * N_EX])
    (w1, w1t, w2, w2t, feat0, feat1, qa, qb, hid0, hid1, ra, rb, t0, t1, gh, field, grad,
     mom0, post) = scratch[3 * N_EX :]

    barrier = pltpu.get_barrier_semaphore()
    for dx in (1, 0, 127):
        for dy in (1, 0, 3):
            if dx == 0 and dy == 0:
                continue
            pl.semaphore_signal(
                barrier, inc=1,
                device_id=(lax.rem(gx + dx, 128), lax.rem(gy + dy, 4)), device_id_type=MESH,
            )

    for p in range(2):
        for i in range(Q):
            wide = cot[p, i].astype(F32)
            for s in range(2):
                ex_c.put(OPPOSITE[i], p, s, wide[8 * s : 8 * s + 8, :])
    build_weights(w_in, b_in, w_out, w1, w1t, w2, w2t)
    zero = jnp.zeros((DEPTH - ROWS, GROUPS * LANES), BF)
    for ref in (feat0, feat1, qa, qb):
        ref[ROWS:, :] = zero
    pl.semaphore_wait(barrier, 8)
    copies_c = ex_c.copies(gx, gy)
    for c in copies_c:
        c.start()

    one = jnp.ones((8, LANES), F32)
    nil = jnp.zeros((8, LANES), F32)

    def lanes_of(g):
        return pl.ds(pl.multiple_of(g * LANES, LANES), LANES)

    def melt_of(g):
        rows = pl.ds(pl.multiple_of((g % 2) * 8, 8), 8)
        return flags[g // 2, rows, :].astype(F32)

    def front(f, g, feat, hid, act):
        rho, mom = moments(f)
        eq = equilibrium(rho, mom)
        lanes = lanes_of(g)
        store_features(feat, lanes, [f[i] * INV_W[i] - eq[i] for i in range(Q)] + [one])
        for c in range(4):
            block = pl.ds(256 * c, 256)
            t = jnp.tanh(dot(w1[block, :], feat[:, lanes]))
            act[block, lanes] = t
            hid[block, lanes] = t.astype(BF)
        return rho, mom, eq

    def step_a(g, carry):
        p = g // 2
        rows = pl.ds(pl.multiple_of((g % 2) * 8, 8), 8)
        lanes = lanes_of(g)
        f = [pops[p, i, rows, :] for i in range(Q)]
        rho, mom, eq = front(f, g, feat0, hid0, t0)
        for d in range(3):
            mom0[g, d] = mom[d]
        learned = dot(w2[...], hid0[:, lanes])
        melt = melt_of(g) > 0.5
        excess = rho - 1.0
        for i in range(Q):
            val = -0.25 * f[i] + (1.25 * W[i]) * eq[i] + learned[8 * i : 8 * i + 8, :]
            cz = VELOCITY[i][2]
            if cz:
                val = val + (0.15 * W[i] * cz) * excess
            post[g, i] = jnp.where(melt, val, f[OPPOSITE[i]])
        return carry

    lax.fori_loop(0, GROUPS, step_a, 0)

    for g in range(GROUPS):
        for i in range(Q):
            ex_p.put(i, g // 2, g % 2, post[g, i])
    copies_p = ex_p.copies(gx, gy)
    for c in copies_p:
        c.start()

    for c in copies_c:
        c.wait()
    for g in range(GROUPS):
        for i in range(Q):
            grad[g, i] = ex_c.get(OPPOSITE[i], g // 2, g % 2)

    def hidden_grad(g, q):
        melt = melt_of(g)
        lanes = lanes_of(g)
        m = [grad[g, i] * melt for i in range(Q)]
        store_features(q, lanes, m + [nil])
        for c in range(4):
            block = pl.ds(256 * c, 256)
            gh[block, lanes] = dot(w2t[block, :], q[:, lanes])

    def step_q(g, carry):
        hidden_grad(g, qb)
        return carry

    lax.fori_loop(0, GROUPS, step_q, 0)

    for c in copies_p:
        c.wait()
    for g in range(GROUPS):
        for i in range(Q):
            field[g, i] = ex_p.get(i, g // 2, g % 2)

    def back(g, mom, act, r, put):
        lanes = lanes_of(g)
        melt = melt_of(g)
        for c in range(4):
            block = pl.ds(256 * c, 256)
            t = act[block, lanes]
            r[block, lanes] = (gh[block, lanes] * (1.0 - t * t)).astype(BF)
        prod = dot(w1t[...], r[:, lanes])
        m, wd = [], []
        for i in range(Q):
            m.append(grad[g, i] * melt)
            wd.append((1.25 * W[i]) * m[i] - prod[8 * i : 8 * i + 8, :])
        total = wd[0]
        lift = None
        dj = [None, None, None]
        for a, b in PAIRS:
            both = wd[a] + wd[b]
            total = total + both
            cz = VELOCITY[a][2]
            if cz:
                term = (0.15 * W[a] * cz) * (m[a] - m[b])
                lift = term if lift is None else lift + term
            slope = 3.0 * (wd[a] - wd[b]) + 9.0 * along(a, mom) * both
            for d in range(3):
                c = VELOCITY[a][d]
                if c == 0:
                    continue
                if dj[d] is None:
                    dj[d] = slope if c == 1 else -slope
                else:
                    dj[d] = dj[d] + slope if c == 1 else dj[d] - slope
        drho = total + lift
        dj = [dj[d] - 3.0 * mom[d] * total for d in range(3)]
        for i in range(Q):
            o = OPPOSITE[i]
            val = (-0.25) * m[i] + INV_W[i] * prod[8 * i : 8 * i + 8, :] + drho
            if i:
                val = val + along(i, dj)
            put(i, val + (grad[g, o] - m[o]))

    def step_b(g, carry):
        f = [field[g, i] for i in range(Q)]
        rho, mom, eq = front(f, g, feat1, hid1, t1)

        def put(i, val):
            post[g, i] = val

        back(g, mom, t1, rb, put)
        return carry

    lax.fori_loop(0, GROUPS, step_b, 0)
    for g in range(GROUPS):
        for i in range(Q):
            ex_d.put(OPPOSITE[i], g // 2, g % 2, post[g, i])
    copies_d = ex_d.copies(gx, gy)
    for c in copies_d:
        c.start()

    acc_out = dot(qb[:ROWS, :], hid1[...], NT)
    acc_in = dot(feat1[:ROWS, :], rb[...], NT)

    for c in copies_d:
        c.wait()
    for g in range(GROUPS):
        for i in range(Q):
            grad[g, i] = ex_d.get(OPPOSITE[i], g // 2, g % 2)

    def step_c(g, carry):
        hidden_grad(g, qa)
        p = g // 2
        rows = pl.ds(pl.multiple_of((g % 2) * 8, 8), 8)

        def put(i, val):
            d0_ref[p, i, rows, :] = val

        back(g, [mom0[g, d] for d in range(3)], t0, ra, put)
        return carry

    lax.fori_loop(0, GROUPS, step_c, 0)
    acc_out = acc_out + dot(qa[:ROWS, :], hid0[...], NT)
    acc_in = acc_in + dot(feat0[:ROWS, :], ra[...], NT)
    sub = lax.broadcasted_iota(jnp.int32, (ROWS, UNITS), 0) % 8
    for k, acc in enumerate((acc_in, acc_out)):
        tot = jnp.zeros((ROWS, UNITS), F32)
        for y in range(8):
            tot = tot + jnp.where(sub == y, acc[:, UNITS * y : UNITS * (y + 1)], 0.0)
        grads_ref[k] = jnp.sum(tot.reshape(20, 8, UNITS), axis=1)


def local_step(populations, cotangent, flags, w_in, b_in, w_out):
    vmem = pl.BlockSpec(memory_space=pltpu.VMEM)
    cells = GROUPS * LANES
    return pl.pallas_call(
        kernel,
        out_shape=(
            jax.ShapeDtypeStruct((2, Q, 16, LANES), F32),
            jax.ShapeDtypeStruct((2, 20, UNITS), F32),
        ),
        in_specs=[vmem] * 6,
        out_specs=(vmem, vmem),
        scratch_shapes=EX_SCRATCH * 3
        + [
            pltpu.VMEM((HID, DEPTH), BF),
            pltpu.VMEM((ROWS, HID), BF),
            pltpu.VMEM((ROWS, HID), BF),
            pltpu.VMEM((HID, DEPTH), BF),
            pltpu.VMEM((DEPTH, cells), BF),
            pltpu.VMEM((DEPTH, cells), BF),
            pltpu.VMEM((DEPTH, cells), BF),
            pltpu.VMEM((DEPTH, cells), BF),
            pltpu.VMEM((HID, cells), BF),
            pltpu.VMEM((HID, cells), BF),
            pltpu.VMEM((HID, cells), BF),
            pltpu.VMEM((HID, cells), BF),
            pltpu.VMEM((HID, cells), F32),
            pltpu.VMEM((HID, cells), F32),
            pltpu.VMEM((HID, cells), F32),
            pltpu.VMEM((GROUPS, Q, 8, LANES), F32),
            pltpu.VMEM((GROUPS, Q, 8, LANES), F32),
            pltpu.VMEM((GROUPS, 3, 8, LANES), F32),
            pltpu.VMEM((GROUPS, Q, 8, LANES), F32),
        ],
        compiler_params=pltpu.CompilerParams(
            collective_id=0, has_side_effects=True, vmem_limit_bytes=60 * 1024 * 1024
        ),
    )(populations, cotangent, flags, w_in, b_in.reshape(1, UNITS), w_out)


def normalized(total):
    return total / jnp.sqrt(jnp.mean(total * total) + 1e-06)


def shards(populations, cotangent, flags, w_in, b_in, w_out):
    d0, grads = local_step(populations, cotangent, flags, w_in, b_in, w_out)
    totals = lax.psum(grads, ("gx", "gy"))
    return (
        d0.astype(BF),
        normalized(totals[0, :Q].T),
        normalized(totals[0, Q]),
        normalized(totals[1, :Q]),
    )


def solution(mesh):
    placed = (
        P("gx", None, "gy", None),
        P("gx", None, "gy", None),
        P("gx", "gy", None),
        P(),
        P(),
        P(),
    )
    return jax.shard_map(
        shards,
        mesh=mesh,
        in_specs=placed,
        out_specs=(P("gx", None, "gy", None), P(), P(), P()),
        check_vma=False,
    )
```

```python
import functools

import jax
import jax.numpy as jnp
from jax import lax
from jax.experimental import pallas as pl
from jax.experimental.pallas import tpu as pltpu
from jax.sharding import PartitionSpec as P

VELOCITY = [
    (0, 0, 0),
    (1, 0, 0),
    (-1, 0, 0),
    (0, 1, 0),
    (0, -1, 0),
    (0, 0, 1),
    (0, 0, -1),
    (1, 1, 0),
    (-1, -1, 0),
    (1, -1, 0),
    (-1, 1, 0),
    (1, 0, 1),
    (-1, 0, -1),
    (1, 0, -1),
    (-1, 0, 1),
    (0, 1, 1),
    (0, -1, -1),
    (0, 1, -1),
    (0, -1, 1),
]
OPPOSITE = [0, 2, 1, 4, 3, 6, 5, 8, 7, 10, 9, 12, 11, 14, 13, 16, 15, 18, 17]
INV_W = [3.0] + [18.0] * 6 + [36.0] * 12
W = [1.0 / 3.0] + [1.0 / 18.0] * 6 + [1.0 / 36.0] * 12
PAIRS = [(i, i + 1) for i in range(1, 19, 2)]
Q = 19
UNITS = 128
ROWS = 160
DEPTH = 256
HID = 8 * UNITS
LANES = 256
GROUPS = 4

X_PLUS = [1, 7, 9, 11, 13]
X_MINUS = [2, 8, 10, 12, 14]
Y_PLUS = [(3, 0), (3, 1), (15, 0), (15, 1), (17, 0), (17, 1), (7, 0), (10, 1)]
Y_MINUS = [(4, 0), (4, 1), (16, 0), (16, 1), (18, 0), (18, 1), (9, 0), (8, 1)]
CORNERS = [7, 10, 8, 9]
MESH = pl.DeviceIdType.MESH
DEV_Z = 16
PLANE = 32
BF = jnp.bfloat16
F32 = jnp.float32
NT = (((1,), (1,)), ((), ()))
TN = (((0,), (0,)), ((), ()))


class Exchange:
    def __init__(self, refs):
        (self.own, self.sxp, self.sxm, self.syp, self.sym, self.rxl, self.rxr,
         self.ryl, self.ryu, self.rc, self.send, self.recv) = refs

    def put(self, j, p, s, val):
        cx, cy, cz = VELOCITY[j]
        if cz:
            val = pltpu.roll(val, cz % LANES, 1)
        rows = pl.ds(8 * s, 8)
        if cx == 1 and p == 1:
            self.sxp[X_PLUS.index(j), rows, :] = val
        elif cx == -1 and p == 0:
            self.sxm[X_MINUS.index(j), rows, :] = val
        else:
            self.own[p, j, rows, :] = val
        if cy == 1 and s == 1 and (j, p) in Y_PLUS:
            k = Y_PLUS.index((j, p))
            self.syp[k : k + 1, :] = val[7:8, :]
        if cy == -1 and s == 0 and (j, p) in Y_MINUS:
            k = Y_MINUS.index((j, p))
            self.sym[k : k + 1, :] = val[0:1, :]

    def copies(self, gx, gy):
        xr, xl = lax.rem(gx + 1, 128), lax.rem(gx + 127, 128)
        yu, yd = lax.rem(gy + 1, 4), lax.rem(gy + 3, 4)
        plan = [
            (self.sxp.at[:, :, :], self.rxl.at[:, :, :], (xr, gy)),
            (self.sxm.at[:, :, :], self.rxr.at[:, :, :], (xl, gy)),
            (self.syp.at[:, :], self.ryl.at[:, :], (gx, yu)),
            (self.sym.at[:, :], self.ryu.at[:, :], (gx, yd)),
            (self.sxp.at[1, pl.ds(8, 8), :], self.rc.at[0], (xr, yu)),
            (self.sxm.at[2, pl.ds(8, 8), :], self.rc.at[1], (xl, yu)),
            (self.sxm.at[1, pl.ds(0, 8), :], self.rc.at[2], (xl, yd)),
            (self.sxp.at[2, pl.ds(0, 8), :], self.rc.at[3], (xr, yd)),
        ]
        return [
            pltpu.make_async_remote_copy(
                src_ref=src, dst_ref=dst, send_sem=self.send.at[k], recv_sem=self.recv.at[k],
                device_id=dev, device_id_type=MESH,
            )
            for k, (src, dst, dev) in enumerate(plan)
        ]

    def get(self, j, p, s):
        cx, cy, cz = VELOCITY[j]
        q = p - cx
        if q == -1:
            src = self.rxl.at[X_PLUS.index(j)]
        elif q == 2:
            src = self.rxr.at[X_MINUS.index(j)]
        else:
            src = self.own.at[q, j]
        if cy == 0:
            return src[8 * s : 8 * s + 8, :]
        row = lax.broadcasted_iota(jnp.int32, (8, LANES), 0)
        if cy == 1:
            if s == 1:
                return src[7:15, :]
            if q in (0, 1):
                k = Y_PLUS.index((j, q))
                halo = self.ryl[k : k + 1, :]
            else:
                halo = self.rc[CORNERS.index(j), 7:8, :]
            return jnp.where(row == 0, halo, pltpu.roll(src[0:8, :], 1, 0))
        if s == 0:
            return src[1:9, :]
        if q in (0, 1):
            k = Y_MINUS.index((j, q))
            halo = self.ryu[k : k + 1, :]
        else:
            halo = self.rc[CORNERS.index(j), 0:1, :]
        return jnp.where(row == 7, halo, pltpu.roll(src[8:16, :], 7, 0))


EX_SCRATCH = [
    pltpu.VMEM((2, Q, 16, LANES), F32),
    pltpu.VMEM((5, 16, LANES), F32),
    pltpu.VMEM((5, 16, LANES), F32),
    pltpu.VMEM((8, LANES), F32),
    pltpu.VMEM((8, LANES), F32),
    pltpu.VMEM((5, 16, LANES), F32),
    pltpu.VMEM((5, 16, LANES), F32),
    pltpu.VMEM((8, LANES), F32),
    pltpu.VMEM((8, LANES), F32),
    pltpu.VMEM((4, 8, LANES), F32),
    pltpu.SemaphoreType.DMA((8,)),
    pltpu.SemaphoreType.DMA((8,)),
]
N_EX = len(EX_SCRATCH)


def dot(a, b, dims=None):
    if dims is None:
        return jnp.dot(a, b, preferred_element_type=F32)
    return lax.dot_general(a, b, dims, preferred_element_type=F32)


def moments(f):
    rho = f[0]
    for a, b in PAIRS:
        rho = rho + (f[a] + f[b])
    mom = []
    for d in range(3):
        acc = None
        for a, b in PAIRS:
            c = VELOCITY[a][d]
            if c == 0:
                continue
            diff = f[a] - f[b] if c == 1 else f[b] - f[a]
            acc = diff if acc is None else acc + diff
        mom.append(acc)
    return rho, mom


def along(i, vec):
    out = None
    for d in range(3):
        c = VELOCITY[i][d]
        if c == 0:
            continue
        if out is None:
            out = vec[d] if c == 1 else -vec[d]
        else:
            out = out + vec[d] if c == 1 else out - vec[d]
    return out


def equilibrium(rho, mom):
    base = rho - 1.5 * (mom[0] * mom[0] + mom[1] * mom[1] + mom[2] * mom[2])
    eq = [base]
    for a, b in PAIRS:
        u = along(a, mom)
        even = base + 4.5 * (u * u)
        odd = 3.0 * u
        eq.append(even + odd)
        eq.append(even - odd)
    return eq


def store_features(dst, lanes, vals):
    for k in range(0, len(vals), 2):
        two = jnp.concatenate([vals[k], vals[k + 1]], axis=0)
        dst[8 * k : 8 * k + 16, lanes] = two.astype(BF)


def build_weights(w_in_t, b_in, w_out, w1, w1t, w2, w2t):
    comp_of = lax.broadcasted_iota(jnp.int32, (Q, DEPTH), 1) // 8
    expand = (lax.broadcasted_iota(jnp.int32, (Q, DEPTH), 0) == comp_of).astype(F32).astype(BF)
    comp_of_t = lax.broadcasted_iota(jnp.int32, (ROWS, Q), 0) // 8
    expand_t = (lax.broadcasted_iota(jnp.int32, (ROWS, Q), 1) == comp_of_t).astype(F32).astype(BF)
    hi = b_in[...].astype(BF)
    rest = b_in[...] - hi.astype(F32)
    mid = rest.astype(BF)
    low = (rest - mid.astype(F32)).astype(BF)
    row = lax.broadcasted_iota(jnp.int32, (8, UNITS), 0)
    parts = jnp.where(
        row == 0, hi.astype(F32),
        jnp.where(row == 1, mid.astype(F32), jnp.where(row == 2, low.astype(F32), 0.0)),
    ).astype(BF)
    place = (
        lax.broadcasted_iota(jnp.int32, (8, DEPTH), 1)
        == lax.broadcasted_iota(jnp.int32, (8, DEPTH), 0) + 8 * Q
    ).astype(F32).astype(BF)
    in_rep = dot(w_in_t[...], expand, TN)
    bias_rep = dot(parts, place, TN)
    out_rep = dot(w_out[...], expand, TN)
    in_rep_t = dot(expand_t, w_in_t[...])
    out_rep_t = dot(expand_t, w_out[...])
    lane = lax.broadcasted_iota(jnp.int32, (UNITS, DEPTH), 1) % 8
    sub = lax.broadcasted_iota(jnp.int32, (ROWS, UNITS), 0) % 8
    for y in range(8):
        block = pl.ds(UNITS * y, UNITS)
        w1[block, :] = (jnp.where(lane == y, in_rep, 0.0) + bias_rep).astype(BF)
        w2t[block, :] = jnp.where(lane == y, out_rep, 0.0).astype(BF)
        w1t[:, block] = jnp.where(sub == y, in_rep_t, 0.0).astype(BF)
        w2[:, block] = jnp.where(sub == y, out_rep_t, 0.0).astype(BF)


class Reduction:
    def __init__(self, refs, gx, gy):
        (self.pay, self.rs_in, self.z_own, self.z_in, self.ag_own, self.ag, self.send,
         self.recv) = refs
        self.core = lax.rem(gx, 2)
        self.z = lax.rem(gx // 2, DEV_Z)
        self.y = gx // (2 * DEV_Z)
        self.x = gy
        self.me = (self.y * 4 + self.x) * 2 + self.core

    def plane_peer(self, k):
        m = lax.rem(self.me + k, PLANE)
        return m, (((m // 8) * DEV_Z + self.z) * 2 + lax.rem(m, 2), lax.rem(m // 2, 4))

    def line_peer(self, k):
        z = lax.rem(self.z + k, DEV_Z)
        return ((self.y * DEV_Z + z) * 2 + self.core, self.x)

    def greet(self, barrier):
        @pl.loop(1, PLANE)
        def _(k):
            pl.semaphore_signal(
                barrier, inc=1, device_id=self.plane_peer(k)[1], device_id_type=MESH
            )

        @pl.loop(1, DEV_Z)
        def _(k):
            pl.semaphore_signal(barrier, inc=1, device_id=self.line_peer(k), device_id_type=MESH)

        return PLANE + DEV_Z - 2

    def remote(self, src, dst, phase, dev):
        return pltpu.make_async_remote_copy(
            src_ref=src, dst_ref=dst, send_sem=self.send.at[phase], recv_sem=self.recv.at[phase],
            device_id=dev, device_id_type=MESH,
        )

    def wait(self, src, dst, phase):
        dev = self.plane_peer(1)[1]
        both = self.remote(src, dst, phase, dev)
        both.wait_send()
        both.wait_recv()

    def scatter(self):
        @pl.loop(1, PLANE)
        def _(k):
            m, dev = self.plane_peer(k)
            self.remote(self.pay.at[m], self.rs_in.at[k - 1], 0, dev).start()

    def finish(self):
        self.wait(self.pay.at[0 : PLANE - 1], self.rs_in.at[:], 0)
        part = self.pay[self.me] + jnp.sum(self.rs_in[...], axis=0)
        self.z_own[...] = part
        self.z_in[self.z] = part

        @pl.loop(1, DEV_Z)
        def _(k):
            self.remote(self.z_own.at[:], self.z_in.at[self.z], 1, self.line_peer(k)).start()

        sized = self.z_in.at[0 : DEV_Z - 1]
        self.wait(sized, sized, 1)
        total = jnp.sum(self.z_in[...], axis=0)
        self.ag_own[...] = total
        self.ag[self.me] = total

        @pl.loop(1, PLANE)
        def _(k):
            dev = self.plane_peer(k)[1]
            self.remote(self.ag_own.at[:], self.ag.at[self.me], 2, dev).start()

        sized = self.ag.at[0 : PLANE - 1]
        self.wait(sized, sized, 2)


RED_SCRATCH = [
    pltpu.VMEM((PLANE, 2, UNITS), F32),
    pltpu.VMEM((PLANE - 1, 2, UNITS), F32),
    pltpu.VMEM((2, UNITS), F32),
    pltpu.VMEM((DEV_Z, 2, UNITS), F32),
    pltpu.VMEM((2, UNITS), F32),
    pltpu.VMEM((PLANE, 2, UNITS), F32),
    pltpu.SemaphoreType.DMA((3,)),
    pltpu.SemaphoreType.DMA((3,)),
]
N_RED = len(RED_SCRATCH)


def kernel(pops, cot, flags, w_in_t, b_in, w_out, d0_ref, gin_ref, gb_ref, gout_ref, *scratch):
    gx, gy = lax.axis_index("gx"), lax.axis_index("gy")
    reduction = Reduction(scratch[:N_RED], gx, gy)
    scratch = scratch[N_RED:]
    ex_c = Exchange(scratch[:N_EX])
    ex_p = Exchange(scratch[N_EX : 2 * N_EX])
    ex_d = Exchange(scratch[2 * N_EX : 3 * N_EX])
    (w1, w1t, w2, w2t, feat0, feat1, qa, qb, hid0, hid1, ra, rb, t0, t1, gh, field, grad,
     mom0, post, out, out_sem) = scratch[3 * N_EX :]

    barrier = pltpu.get_barrier_semaphore()
    for dx in (1, 0, 127):
        for dy in (1, 0, 3):
            if dx == 0 and dy == 0:
                continue
            pl.semaphore_signal(
                barrier, inc=1,
                device_id=(lax.rem(gx + dx, 128), lax.rem(gy + dy, 4)), device_id_type=MESH,
            )

    greeted = 8 + reduction.greet(barrier)
    for p in range(2):
        for i in range(Q):
            wide = cot[p, i].astype(F32)
            for s in range(2):
                ex_c.put(OPPOSITE[i], p, s, wide[8 * s : 8 * s + 8, :])
    build_weights(w_in_t, b_in, w_out, w1, w1t, w2, w2t)
    zero = jnp.zeros((DEPTH - ROWS, GROUPS * LANES), BF)
    for ref in (feat0, feat1, qa, qb):
        ref[ROWS:, :] = zero
    reduction.pay[...] = jnp.zeros((PLANE, 2, UNITS), F32)

    one = jnp.ones((8, LANES), F32)
    nil = jnp.zeros((8, LANES), F32)

    def lanes_of(g):
        return pl.ds(pl.multiple_of(g * LANES, LANES), LANES)

    def melt_of(g):
        rows = pl.ds(pl.multiple_of((g % 2) * 8, 8), 8)
        return flags[g // 2, rows, :].astype(F32)

    def front(f, g, feat, hid, act):
        rho, mom = moments(f)
        eq = equilibrium(rho, mom)
        lanes = lanes_of(g)
        store_features(feat, lanes, [f[i] * INV_W[i] - eq[i] for i in range(Q)] + [one])
        for c in range(4):
            block = pl.ds(256 * c, 256)
            t = jnp.tanh(dot(w1[block, :], feat[:, lanes]))
            act[block, lanes] = t
            hid[block, lanes] = t.astype(BF)
        return rho, mom, eq

    def step_a(g, carry):
        p = g // 2
        rows = pl.ds(pl.multiple_of((g % 2) * 8, 8), 8)
        lanes = lanes_of(g)
        f = [pops[p, i, rows, :] for i in range(Q)]
        rho, mom, eq = front(f, g, feat0, hid0, t0)
        for d in range(3):
            mom0[g, d] = mom[d]
        learned = dot(w2[...], hid0[:, lanes])
        melt = melt_of(g) > 0.5
        excess = rho - 1.0
        for i in range(Q):
            val = -0.25 * f[i] + (1.25 * W[i]) * eq[i] + learned[8 * i : 8 * i + 8, :]
            cz = VELOCITY[i][2]
            if cz:
                val = val + (0.15 * W[i] * cz) * excess
            post[g, i] = jnp.where(melt, val, f[OPPOSITE[i]])
        return carry

    lax.fori_loop(0, GROUPS, step_a, 0)

    pl.semaphore_wait(barrier, greeted)
    copies_c = ex_c.copies(gx, gy)
    for c in copies_c:
        c.start()
    for g in range(GROUPS):
        for i in range(Q):
            ex_p.put(i, g // 2, g % 2, post[g, i])
    copies_p = ex_p.copies(gx, gy)
    for c in copies_p:
        c.start()

    for c in copies_c:
        c.wait()
    for g in range(GROUPS):
        for i in range(Q):
            grad[g, i] = ex_c.get(OPPOSITE[i], g // 2, g % 2)

    def hidden_grad(g, q):
        melt = melt_of(g)
        lanes = lanes_of(g)
        m = [grad[g, i] * melt for i in range(Q)]
        store_features(q, lanes, m + [nil])
        for c in range(4):
            block = pl.ds(256 * c, 256)
            gh[block, lanes] = dot(w2t[block, :], q[:, lanes])

    def step_q(g, carry):
        hidden_grad(g, qb)
        return carry

    lax.fori_loop(0, GROUPS, step_q, 0)

    for c in copies_p:
        c.wait()
    for g in range(GROUPS):
        for i in range(Q):
            field[g, i] = ex_p.get(i, g // 2, g % 2)

    def preact_grad(g, act, r):
        lanes = lanes_of(g)
        for c in range(4):
            block = pl.ds(256 * c, 256)
            t = act[block, lanes]
            r[block, lanes] = (gh[block, lanes] * (1.0 - t * t)).astype(BF)

    def back(g, mom, r):
        lanes = lanes_of(g)
        melt = melt_of(g)
        prod = dot(w1t[...], r[:, lanes])
        m, wd = [], []
        for i in range(Q):
            m.append(grad[g, i] * melt)
            wd.append((1.25 * W[i]) * m[i] - prod[8 * i : 8 * i + 8, :])
        total = wd[0]
        lift = None
        dj = [None, None, None]
        for a, b in PAIRS:
            both = wd[a] + wd[b]
            total = total + both
            cz = VELOCITY[a][2]
            if cz:
                term = (0.15 * W[a] * cz) * (m[a] - m[b])
                lift = term if lift is None else lift + term
            slope = 3.0 * (wd[a] - wd[b]) + 9.0 * along(a, mom) * both
            for d in range(3):
                c = VELOCITY[a][d]
                if c == 0:
                    continue
                if dj[d] is None:
                    dj[d] = slope if c == 1 else -slope
                else:
                    dj[d] = dj[d] + slope if c == 1 else dj[d] - slope
        drho = total + lift
        dj = [dj[d] - 3.0 * mom[d] * total for d in range(3)]
        for i in range(Q):
            o = OPPOSITE[i]
            val = (-0.25) * m[i] + INV_W[i] * prod[8 * i : 8 * i + 8, :] + drho
            if i:
                val = val + along(i, dj)
            post[g, i] = val + (grad[g, o] - m[o])

    def step_b(g, carry):
        f = [field[g, i] for i in range(Q)]
        rho, mom, eq = front(f, g, feat1, hid1, t1)
        preact_grad(g, t1, rb)
        back(g, mom, rb)
        return carry

    lax.fori_loop(0, GROUPS, step_b, 0)
    for g in range(GROUPS):
        for i in range(Q):
            ex_d.put(OPPOSITE[i], g // 2, g % 2, post[g, i])
    copies_d = ex_d.copies(gx, gy)
    for c in copies_d:
        c.start()

    acc_out = dot(qb[:ROWS, :], hid1[...], NT)
    acc_in = dot(feat1[:ROWS, :], rb[...], NT)

    for c in copies_d:
        c.wait()
    for g in range(GROUPS):
        for i in range(Q):
            grad[g, i] = ex_d.get(OPPOSITE[i], g // 2, g % 2)

    def step_r(g, carry):
        hidden_grad(g, qa)
        preact_grad(g, t0, ra)
        return carry

    lax.fori_loop(0, GROUPS, step_r, 0)
    acc_out = acc_out + dot(qa[:ROWS, :], hid0[...], NT)
    acc_in = acc_in + dot(feat0[:ROWS, :], ra[...], NT)
    sub = lax.broadcasted_iota(jnp.int32, (ROWS, UNITS), 0) % 8
    for k, acc in enumerate((acc_in, acc_out)):
        tot = jnp.zeros((ROWS, UNITS), F32)
        for y in range(8):
            tot = tot + jnp.where(sub == y, acc[:, UNITS * y : UNITS * (y + 1)], 0.0)
        tot = jnp.sum(tot.reshape(20, 8, UNITS), axis=1)
        for j in range(10):
            reduction.pay[10 * k + j] = tot[2 * j : 2 * j + 2, :]
    reduction.scatter()

    def step_c(g, carry):
        back(g, [mom0[g, d] for d in range(3)], ra)
        return carry

    lax.fori_loop(0, GROUPS, step_c, 0)
    for p in range(2):
        for i in range(Q):
            out[p, i] = jnp.concatenate([post[2 * p, i], post[2 * p + 1, i]], axis=0).astype(BF)
    write = pltpu.make_async_copy(out, d0_ref, out_sem)
    write.start()
    reduction.finish()

    def normalized(rows):
        total = jnp.concatenate(rows, axis=0)
        scale = jnp.sum(total * total) / (total.shape[0] * UNITS) + 1e-06
        return total / jnp.sqrt(scale)

    row = [reduction.ag[k // 2, k % 2 : k % 2 + 1, :] for k in range(2 * 20)]
    gin_ref[...] = normalized(row[:Q])
    gb_ref[...] = normalized(row[Q : Q + 1])
    gout_ref[...] = normalized(row[Q + 1 : 2 * Q + 1])
    write.wait()


def local_step(populations, cotangent, flags, w_in, b_in, w_out):
    vmem = pl.BlockSpec(memory_space=pltpu.VMEM)
    cells = GROUPS * LANES
    return pl.pallas_call(
        kernel,
        out_shape=(
            jax.ShapeDtypeStruct((2, Q, 16, LANES), BF),
            jax.ShapeDtypeStruct((Q, UNITS), F32),
            jax.ShapeDtypeStruct((1, UNITS), F32),
            jax.ShapeDtypeStruct((Q, UNITS), F32),
        ),
        in_specs=[vmem] * 6,
        out_specs=(pl.BlockSpec(memory_space=pl.ANY), vmem, vmem, vmem),
        scratch_shapes=RED_SCRATCH
        + EX_SCRATCH * 3
        + [
            pltpu.VMEM((HID, DEPTH), BF),
            pltpu.VMEM((ROWS, HID), BF),
            pltpu.VMEM((ROWS, HID), BF),
            pltpu.VMEM((HID, DEPTH), BF),
            pltpu.VMEM((DEPTH, cells), BF),
            pltpu.VMEM((DEPTH, cells), BF),
            pltpu.VMEM((DEPTH, cells), BF),
            pltpu.VMEM((DEPTH, cells), BF),
            pltpu.VMEM((HID, cells), BF),
            pltpu.VMEM((HID, cells), BF),
            pltpu.VMEM((HID, cells), BF),
            pltpu.VMEM((HID, cells), BF),
            pltpu.VMEM((HID, cells), F32),
            pltpu.VMEM((HID, cells), F32),
            pltpu.VMEM((HID, cells), F32),
            pltpu.VMEM((GROUPS, Q, 8, LANES), F32),
            pltpu.VMEM((GROUPS, Q, 8, LANES), F32),
            pltpu.VMEM((GROUPS, 3, 8, LANES), F32),
            pltpu.VMEM((GROUPS, Q, 8, LANES), F32),
            pltpu.VMEM((2, Q, 16, LANES), BF),
            pltpu.SemaphoreType.DMA,
        ],
        compiler_params=pltpu.CompilerParams(
            collective_id=0, has_side_effects=True, vmem_limit_bytes=60 * 1024 * 1024
        ),
    )(populations, cotangent, flags, w_in.T, b_in.reshape(1, UNITS), w_out)


def shards(populations, cotangent, flags, w_in, b_in, w_out):
    d0, grad_in, grad_b, grad_out = local_step(populations, cotangent, flags, w_in, b_in, w_out)
    return d0, grad_in.T, grad_b.reshape(UNITS), grad_out


def solution(mesh):
    placed = (
        P("gx", None, "gy", None),
        P("gx", None, "gy", None),
        P("gx", "gy", None),
        P(),
        P(),
        P(),
    )
    return jax.shard_map(
        shards,
        mesh=mesh,
        in_specs=placed,
        out_specs=(P("gx", None, "gy", None), P(), P(), P()),
        check_vma=False,
    )
```

```python
import functools

import jax
import jax.numpy as jnp
from jax import lax
from jax.experimental import pallas as pl
from jax.experimental.pallas import tpu as pltpu
from jax.sharding import PartitionSpec as P

VELOCITY = [
    (0, 0, 0),
    (1, 0, 0),
    (-1, 0, 0),
    (0, 1, 0),
    (0, -1, 0),
    (0, 0, 1),
    (0, 0, -1),
    (1, 1, 0),
    (-1, -1, 0),
    (1, -1, 0),
    (-1, 1, 0),
    (1, 0, 1),
    (-1, 0, -1),
    (1, 0, -1),
    (-1, 0, 1),
    (0, 1, 1),
    (0, -1, -1),
    (0, 1, -1),
    (0, -1, 1),
]
OPPOSITE = [0, 2, 1, 4, 3, 6, 5, 8, 7, 10, 9, 12, 11, 14, 13, 16, 15, 18, 17]
INV_W = [3.0] + [18.0] * 6 + [36.0] * 12
W = [1.0 / 3.0] + [1.0 / 18.0] * 6 + [1.0 / 36.0] * 12
PAIRS = [(i, i + 1) for i in range(1, 19, 2)]
Q = 19
UNITS = 128
ROWS = 160
DEPTH = 256
HID = 8 * UNITS
LANES = 256
GROUPS = 4

X_PLUS = [1, 7, 9, 11, 13]
X_MINUS = [2, 8, 10, 12, 14]
Y_PLUS = [(3, 0), (3, 1), (15, 0), (15, 1), (17, 0), (17, 1), (7, 0), (10, 1)]
Y_MINUS = [(4, 0), (4, 1), (16, 0), (16, 1), (18, 0), (18, 1), (9, 0), (8, 1)]
CORNERS = [7, 10, 8, 9]
MESH = pl.DeviceIdType.MESH
DEV_Z = 16
PLANE = 32
CHUNK = 256
BF = jnp.bfloat16
F32 = jnp.float32
NT = (((1,), (1,)), ((), ()))
TN = (((0,), (0,)), ((), ()))


class Exchange:
    def __init__(self, refs):
        (self.own, self.sxp, self.sxm, self.syp, self.sym, self.rxl, self.rxr,
         self.ryl, self.ryu, self.rc, self.send, self.recv) = refs

    def put(self, j, p, s, val):
        cx, cy, cz = VELOCITY[j]
        if cz:
            val = pltpu.roll(val, cz % LANES, 1)
        rows = pl.ds(8 * s, 8)
        if cx == 1 and p == 1:
            self.sxp[X_PLUS.index(j), rows, :] = val
        elif cx == -1 and p == 0:
            self.sxm[X_MINUS.index(j), rows, :] = val
        else:
            self.own[p, j, rows, :] = val
        if cy == 1 and s == 1 and (j, p) in Y_PLUS:
            k = Y_PLUS.index((j, p))
            self.syp[k : k + 1, :] = val[7:8, :]
        if cy == -1 and s == 0 and (j, p) in Y_MINUS:
            k = Y_MINUS.index((j, p))
            self.sym[k : k + 1, :] = val[0:1, :]

    def send_half(self, s, near):
        rows = pl.ds(8 * s, 8)
        dy = 1 if s else -1
        plan = [
            (self.sxp.at[1 if s else 2, rows, :], self.rc.at[0 if s else 3], near(1, dy)),
            (self.sxm.at[2 if s else 1, rows, :], self.rc.at[1 if s else 2], near(-1, dy)),
            (self.sxp.at[:, rows, :], self.rxl.at[:, rows, :], near(1, 0)),
            (self.sxm.at[:, rows, :], self.rxr.at[:, rows, :], near(-1, 0)),
            (self.syp, self.ryl, near(0, 1)) if s else (self.sym, self.ryu, near(0, -1)),
        ]
        made = [
            pltpu.make_async_remote_copy(
                src_ref=src, dst_ref=dst, send_sem=self.send.at[5 * s + k],
                recv_sem=self.recv.at[5 * s + k], device_id=dev, device_id_type=MESH,
            )
            for k, (src, dst, dev) in enumerate(plan)
        ]
        for c in made:
            c.start()
        return made

    def get(self, j, p, s):
        cx, cy, cz = VELOCITY[j]
        q = p - cx
        if q == -1:
            src = self.rxl.at[X_PLUS.index(j)]
        elif q == 2:
            src = self.rxr.at[X_MINUS.index(j)]
        else:
            src = self.own.at[q, j]
        if cy == 0:
            return src[8 * s : 8 * s + 8, :]
        row = lax.broadcasted_iota(jnp.int32, (8, LANES), 0)
        if cy == 1:
            if s == 1:
                return src[7:15, :]
            if q in (0, 1):
                k = Y_PLUS.index((j, q))
                halo = self.ryl[k : k + 1, :]
            else:
                halo = self.rc[CORNERS.index(j), 7:8, :]
            return jnp.where(row == 0, halo, pltpu.roll(src[0:8, :], 1, 0))
        if s == 0:
            return src[1:9, :]
        if q in (0, 1):
            k = Y_MINUS.index((j, q))
            halo = self.ryu[k : k + 1, :]
        else:
            halo = self.rc[CORNERS.index(j), 0:1, :]
        return jnp.where(row == 7, halo, pltpu.roll(src[8:16, :], 7, 0))


EX_SCRATCH = [
    pltpu.VMEM((2, Q, 16, LANES), F32),
    pltpu.VMEM((5, 16, LANES), F32),
    pltpu.VMEM((5, 16, LANES), F32),
    pltpu.VMEM((8, LANES), F32),
    pltpu.VMEM((8, LANES), F32),
    pltpu.VMEM((5, 16, LANES), F32),
    pltpu.VMEM((5, 16, LANES), F32),
    pltpu.VMEM((8, LANES), F32),
    pltpu.VMEM((8, LANES), F32),
    pltpu.VMEM((4, 8, LANES), F32),
    pltpu.SemaphoreType.DMA((10,)),
    pltpu.SemaphoreType.DMA((10,)),
]
N_EX = len(EX_SCRATCH)


def dot(a, b, dims=None):
    if dims is None:
        return jnp.dot(a, b, preferred_element_type=F32)
    return lax.dot_general(a, b, dims, preferred_element_type=F32)


def moments(f):
    rho = f[0]
    for a, b in PAIRS:
        rho = rho + (f[a] + f[b])
    mom = []
    for d in range(3):
        acc = None
        for a, b in PAIRS:
            c = VELOCITY[a][d]
            if c == 0:
                continue
            diff = f[a] - f[b] if c == 1 else f[b] - f[a]
            acc = diff if acc is None else acc + diff
        mom.append(acc)
    return rho, mom


def along(i, vec):
    out = None
    for d in range(3):
        c = VELOCITY[i][d]
        if c == 0:
            continue
        if out is None:
            out = vec[d] if c == 1 else -vec[d]
        else:
            out = out + vec[d] if c == 1 else out - vec[d]
    return out


def equilibrium(rho, mom):
    base = rho - 1.5 * (mom[0] * mom[0] + mom[1] * mom[1] + mom[2] * mom[2])
    eq = [base]
    for a, b in PAIRS:
        u = along(a, mom)
        even = base + 4.5 * (u * u)
        odd = 3.0 * u
        eq.append(even + odd)
        eq.append(even - odd)
    return eq


def store_features(dst, lanes, vals):
    for k in range(0, len(vals), 2):
        two = jnp.concatenate([vals[k], vals[k + 1]], axis=0)
        dst[8 * k : 8 * k + 16, lanes] = two.astype(BF)


def one_hot(hit):
    return hit.astype(F32).astype(BF)


def iota(shape, dim):
    return lax.broadcasted_iota(jnp.int32, shape, dim)


def tall(w_t, masked, extra=None):
    expand = one_hot(iota((Q, DEPTH), 0) == iota((Q, DEPTH), 1) // 8)
    wide = dot(w_t, expand, TN)
    lane = iota((UNITS, DEPTH), 1) % 8
    for y in range(8):
        val = jnp.where(lane == y, wide, 0.0)
        if extra is not None:
            val = val + extra
        masked[pl.ds(UNITS * y, UNITS), :] = val.astype(BF)


def flat(w_t, masked):
    expand = one_hot(iota((ROWS, Q), 1) == iota((ROWS, Q), 0) // 8)
    wide = dot(expand, w_t)
    sub = iota((ROWS, UNITS), 0) % 8
    for y in range(8):
        masked[:, pl.ds(UNITS * y, UNITS)] = jnp.where(sub == y, wide, 0.0).astype(BF)


def bias_columns(b_in):
    hi = b_in.astype(BF)
    rest = b_in - hi.astype(F32)
    mid = rest.astype(BF)
    low = (rest - mid.astype(F32)).astype(BF)
    row = iota((8, UNITS), 0)
    parts = jnp.where(
        row == 0, hi.astype(F32),
        jnp.where(row == 1, mid.astype(F32), jnp.where(row == 2, low.astype(F32), 0.0)),
    ).astype(BF)
    place = one_hot(iota((8, DEPTH), 1) == iota((8, DEPTH), 0) + 8 * Q)
    return dot(parts, place, TN)


class Reduction:
    def __init__(self, refs, gx, gy):
        (self.pay, self.rs_in, self.z_own, self.z_in, self.ag_own, self.ag, self.send,
         self.recv) = refs
        self.z = lax.rem(gx // 2, DEV_Z)
        core, y = lax.rem(gx, 2), gx // (2 * DEV_Z)
        self.me = y * 8 + gy * 2 + core
        cs = [core, 1 - core]
        xs = [gy] + [lax.rem(gy + k, 4) for k in range(1, 4)]
        ys = [y] + [lax.rem(y + k, 4) for k in range(1, 4)]
        self.plane = []
        for dy in range(4):
            base, mbase = ys[dy] * (2 * DEV_Z) + self.z * 2, ys[dy] * 8
            for dc in range(2):
                for dx in range(4):
                    if dx or dy or dc:
                        dev = (base + cs[dc], xs[dx])
                        self.plane.append((mbase + (xs[dx] * 2 + cs[dc]), dev))
        line = gx - 2 * self.z
        self.line = []
        for k in range(1, DEV_Z):
            self.line.append((line + 2 * lax.rem(self.z + k, DEV_Z), gy))

    def greet(self, barrier):
        for dev in [d for _, d in self.plane] + self.line:
            pl.semaphore_signal(barrier, inc=1, device_id=dev, device_id_type=MESH)
        return PLANE + DEV_Z - 2

    def remote(self, src, dst, phase, dev):
        return pltpu.make_async_remote_copy(
            src_ref=src, dst_ref=dst, send_sem=self.send.at[phase], recv_sem=self.recv.at[phase],
            device_id=dev, device_id_type=MESH,
        )

    def wait(self, src, dst, phase):
        dev = self.plane[0][1]
        both = self.remote(src, dst, phase, dev)
        both.wait_send()
        both.wait_recv()

    def scatter(self):
        for k, (m, dev) in enumerate(self.plane):
            self.remote(self.pay.at[m], self.rs_in.at[k], 0, dev).start()

    def finish(self):
        self.wait(self.pay.at[0 : PLANE - 1], self.rs_in.at[:], 0)
        part = self.pay[self.me] + jnp.sum(self.rs_in[...], axis=0)
        self.z_own[...] = part
        self.z_in[self.z] = part

        for dev in self.line:
            self.remote(self.z_own.at[:], self.z_in.at[self.z], 1, dev).start()

        sized = self.z_in.at[0 : DEV_Z - 1]
        self.wait(sized, sized, 1)
        total = jnp.sum(self.z_in[...], axis=0)
        self.ag_own[...] = total
        self.ag[self.me] = total

        for _, dev in self.plane:
            self.remote(self.ag_own.at[:], self.ag.at[self.me], 2, dev).start()

        sized = self.ag.at[0 : PLANE - 1]
        self.wait(sized, sized, 2)


RED_SCRATCH = [
    pltpu.VMEM((PLANE, 2, UNITS), F32),
    pltpu.VMEM((PLANE - 1, 2, UNITS), F32),
    pltpu.VMEM((2, UNITS), F32),
    pltpu.VMEM((DEV_Z, 2, UNITS), F32),
    pltpu.VMEM((2, UNITS), F32),
    pltpu.VMEM((PLANE, 2, UNITS), F32),
    pltpu.SemaphoreType.DMA((3,)),
    pltpu.SemaphoreType.DMA((3,)),
]
N_RED = len(RED_SCRATCH)


def kernel(pops_hbm, cot_hbm, flags, w_in_t, b_in, w_out, d0_ref, gin_ref, gb_ref, gout_ref, *scratch):
    gx, gy = lax.axis_index("gx"), lax.axis_index("gy")
    (w1, w1t, w2, w2t, feat0, feat1, qa, qb, hid0, hid1, ra, rb, t0, t1, gh, field, grad,
     mom0, post, out, fold_out, pops, cot, out_sem, in_sem) = scratch[N_RED + 3 * N_EX :]
    get_cot = pltpu.make_async_copy(cot_hbm, cot, in_sem.at[0])
    get_pops = pltpu.make_async_copy(pops_hbm, pops, in_sem.at[1])
    get_cot.start()
    get_pops.start()
    reduction = Reduction(scratch[:N_RED], gx, gy)
    ex_c, ex_p, ex_d = [
        Exchange(scratch[N_RED + k * N_EX : N_RED + (k + 1) * N_EX]) for k in range(3)
    ]
    step_x = {0: gx, 1: lax.rem(gx + 1, 128), -1: lax.rem(gx + 127, 128)}
    step_y = {0: gy, 1: lax.rem(gy + 1, 4), -1: lax.rem(gy + 3, 4)}

    def near(dx, dy):
        return (step_x[dx], step_y[dy])

    barrier = pltpu.get_barrier_semaphore()
    for dx in (1, 0, -1):
        for dy in (1, 0, -1):
            if dx or dy:
                pl.semaphore_signal(
                    barrier, inc=1, device_id=near(dx, dy), device_id_type=MESH
                )
    greeted = 8 + reduction.greet(barrier)
    tall(w_in_t[...], w1, bias_columns(b_in[...]))
    flat(w_out[...], w2)
    zero = jnp.zeros((DEPTH - ROWS, GROUPS * LANES), BF)
    for ref in (feat0, feat1, qa, qb):
        ref[ROWS:, :] = zero
    reduction.pay[...] = jnp.zeros((PLANE, 2, UNITS), F32)
    get_cot.wait()
    for p in range(2):
        for i in range(Q):
            wide = cot[p, i].astype(F32)
            for s in range(2):
                ex_c.put(OPPOSITE[i], p, s, wide[8 * s : 8 * s + 8, :])
    one = jnp.ones((8, LANES), F32)
    nil = jnp.zeros((8, LANES), F32)
    get_pops.wait()

    def lanes_of(p, s):
        return pl.ds((2 * p + s) * LANES, LANES)

    def rows_of(s):
        return pl.ds(8 * s, 8)

    def melt_of(p, s):
        return flags[p, rows_of(s), :].astype(F32)

    def front(f, p, s, feat, hid, act):
        rho, mom = moments(f)
        eq = equilibrium(rho, mom)
        lanes = lanes_of(p, s)
        store_features(feat, lanes, [f[i] * INV_W[i] - eq[i] for i in range(Q)] + [one])
        for c in range(0, HID, CHUNK):
            block = pl.ds(c, CHUNK)
            t = jnp.tanh(dot(w1[block, :], feat[:, lanes]))
            act[block, lanes] = t
            hid[block, lanes] = t.astype(BF)
        return rho, mom, eq

    def step_a(p, s):
        f = [pops[p, i, rows_of(s), :] for i in range(Q)]
        rho, mom, eq = front(f, p, s, feat0, hid0, t0)
        for d in range(3):
            mom0[2 * p + s, d] = mom[d]
        learned = dot(w2[...], hid0[:, lanes_of(p, s)])
        melt = melt_of(p, s) > 0.5
        excess = rho - 1.0
        for i in range(Q):
            val = -0.25 * f[i] + (1.25 * W[i]) * eq[i] + learned[8 * i : 8 * i + 8, :]
            cz = VELOCITY[i][2]
            if cz:
                val = val + (0.15 * W[i] * cz) * excess
            ex_p.put(i, p, s, jnp.where(melt, val, f[OPPOSITE[i]]))

    copies_c, copies_p, copies_d = [], [], []
    for p in range(2):
        step_a(p, 1)
    pl.semaphore_wait(barrier, greeted)
    copies_c += ex_c.send_half(1, near)
    copies_c += ex_c.send_half(0, near)
    copies_p += ex_p.send_half(1, near)
    for p in range(2):
        step_a(p, 0)
    copies_p += ex_p.send_half(0, near)

    tall(w_out[...], w2t)
    flat(w_in_t[...], w1t)
    for c in copies_c:
        c.wait()

    def hidden_grad(p, s, q):
        melt = melt_of(p, s)
        m = [grad[2 * p + s, i] * melt for i in range(Q)]
        store_features(q, lanes_of(p, s), m + [nil])

    for p in range(2):
        for s in range(2):
            for i in range(Q):
                grad[2 * p + s, i] = ex_c.get(OPPOSITE[i], p, s)
            hidden_grad(p, s, qb)
            for c in range(0, HID, CHUNK):
                block = pl.ds(c, CHUNK)
                gh[block, lanes_of(p, s)] = dot(w2t[block, :], qb[:, lanes_of(p, s)])

    for c in copies_p:
        c.wait()

    def back(p, s, mom, r, put):
        g = 2 * p + s
        melt = melt_of(p, s)
        prod = dot(w1t[...], r[:, lanes_of(p, s)])
        m, wd = [], []
        for i in range(Q):
            m.append(grad[g, i] * melt)
            wd.append((1.25 * W[i]) * m[i] - prod[8 * i : 8 * i + 8, :])
        total = wd[0]
        lift = None
        dj = [None, None, None]
        for a, b in PAIRS:
            both = wd[a] + wd[b]
            total = total + both
            cz = VELOCITY[a][2]
            if cz:
                term = (0.15 * W[a] * cz) * (m[a] - m[b])
                lift = term if lift is None else lift + term
            slope = 3.0 * (wd[a] - wd[b]) + 9.0 * along(a, mom) * both
            for d in range(3):
                c = VELOCITY[a][d]
                if c == 0:
                    continue
                if dj[d] is None:
                    dj[d] = slope if c == 1 else -slope
                else:
                    dj[d] = dj[d] + slope if c == 1 else dj[d] - slope
        drho = total + lift
        dj = [dj[d] - 3.0 * mom[d] * total for d in range(3)]
        for i in range(Q):
            o = OPPOSITE[i]
            val = (-0.25) * m[i] + INV_W[i] * prod[8 * i : 8 * i + 8, :] + drho
            if i:
                val = val + along(i, dj)
            put(i, val + (grad[g, o] - m[o]))

    def step_b(p, s):
        f = [ex_p.get(i, p, s) for i in range(Q)]
        _, mom, _ = front(f, p, s, feat1, hid1, t1)
        lanes = lanes_of(p, s)
        for c in range(0, HID, CHUNK):
            block = pl.ds(c, CHUNK)
            t = t1[block, lanes]
            rb[block, lanes] = (gh[block, lanes] * (1.0 - t * t)).astype(BF)
        back(p, s, mom, rb, lambda i, val: ex_d.put(OPPOSITE[i], p, s, val))

    for s in (1, 0):
        for p in range(2):
            step_b(p, s)
        copies_d += ex_d.send_half(s, near)

    def weight_sums(feat, r, q, hid):
        sub = iota((ROWS, UNITS), 0) % 8
        sums = []
        for left, right in ((feat, r), (q, hid)):
            tot = None
            for c in range(0, HID, 256):
                acc = dot(left[:ROWS, :], right[pl.ds(c, 256), :], NT)
                for k in range(2):
                    hit = jnp.where(sub == c // UNITS + k, acc[:, UNITS * k : UNITS * (k + 1)], 0.0)
                    tot = hit if tot is None else tot + hit
            sums.append(jnp.sum(tot.reshape(20, 8, UNITS), axis=1))
        return sums

    for k, val in enumerate(weight_sums(feat1, rb, qb, hid1)):
        fold_out[0, k] = val
    for c in range(0, HID, CHUNK):
        block = pl.ds(c, CHUNK)
        t = t0[block, :]
        t0[block, :] = 1.0 - t * t

    for c in copies_d:
        c.wait()
    for p in range(2):
        for s in range(2):
            for i in range(Q):
                grad[2 * p + s, i] = ex_d.get(OPPOSITE[i], p, s)
            hidden_grad(p, s, qa)
            lanes = lanes_of(p, s)
            for c in range(0, HID, CHUNK):
                block = pl.ds(c, CHUNK)
                ra[block, lanes] = (dot(w2t[block, :], qa[:, lanes]) * t0[block, lanes]).astype(BF)

    for k, val in enumerate(weight_sums(feat0, ra, qa, hid0)):
        tot = val + fold_out[0, k]
        for j in range(10):
            reduction.pay[10 * k + j] = tot[2 * j : 2 * j + 2, :]
    reduction.scatter()

    def keep(p, s):
        def put(i, val):
            post[2 * p + s, i] = val

        return put

    for p in range(2):
        for s in range(2):
            back(p, s, [mom0[2 * p + s, d] for d in range(3)], ra, keep(p, s))
        for i in range(Q):
            out[p, i] = jnp.concatenate([post[2 * p, i], post[2 * p + 1, i]], axis=0).astype(BF)
    write = pltpu.make_async_copy(out, d0_ref, out_sem)
    write.start()
    reduction.finish()

    def normalized(rows):
        total = jnp.concatenate(rows, axis=0)
        scale = jnp.sum(total * total) / (total.shape[0] * UNITS) + 1e-06
        return total / jnp.sqrt(scale)

    row = [reduction.ag[k // 2, k % 2 : k % 2 + 1, :] for k in range(2 * 20)]
    gin_ref[...] = normalized(row[:Q])
    gb_ref[...] = normalized(row[Q : Q + 1])
    gout_ref[...] = normalized(row[Q + 1 : 2 * Q + 1])
    write.wait()


def local_step(populations, cotangent, flags, w_in, b_in, w_out):
    vmem = pl.BlockSpec(memory_space=pltpu.VMEM)
    hbm = pl.BlockSpec(memory_space=pl.ANY)
    cells = GROUPS * LANES
    return pl.pallas_call(
        kernel,
        out_shape=(
            jax.ShapeDtypeStruct((2, Q, 16, LANES), BF),
            jax.ShapeDtypeStruct((Q, UNITS), F32),
            jax.ShapeDtypeStruct((1, UNITS), F32),
            jax.ShapeDtypeStruct((Q, UNITS), F32),
        ),
        in_specs=[hbm] * 2 + [vmem] * 4,
        out_specs=(pl.BlockSpec(memory_space=pl.ANY), vmem, vmem, vmem),
        scratch_shapes=RED_SCRATCH
        + EX_SCRATCH * 3
        + [
            pltpu.VMEM((HID, DEPTH), BF),
            pltpu.VMEM((ROWS, HID), BF),
            pltpu.VMEM((ROWS, HID), BF),
            pltpu.VMEM((HID, DEPTH), BF),
            pltpu.VMEM((DEPTH, cells), BF),
            pltpu.VMEM((DEPTH, cells), BF),
            pltpu.VMEM((DEPTH, cells), BF),
            pltpu.VMEM((DEPTH, cells), BF),
            pltpu.VMEM((HID, cells), BF),
            pltpu.VMEM((HID, cells), BF),
            pltpu.VMEM((HID, cells), BF),
            pltpu.VMEM((HID, cells), BF),
            pltpu.VMEM((HID, cells), F32),
            pltpu.VMEM((HID, cells), F32),
            pltpu.VMEM((HID, cells), F32),
            pltpu.VMEM((GROUPS, Q, 8, LANES), F32),
            pltpu.VMEM((GROUPS, Q, 8, LANES), F32),
            pltpu.VMEM((GROUPS, 3, 8, LANES), F32),
            pltpu.VMEM((GROUPS, Q, 8, LANES), F32),
            pltpu.VMEM((2, Q, 16, LANES), BF),
            pltpu.VMEM((2, 2, 20, UNITS), F32),
            pltpu.VMEM((2, Q, 16, LANES), F32),
            pltpu.VMEM((2, Q, 16, LANES), BF),
            pltpu.SemaphoreType.DMA,
            pltpu.SemaphoreType.DMA((2,)),
        ],
        compiler_params=pltpu.CompilerParams(
            collective_id=0, has_side_effects=True, vmem_limit_bytes=60 * 1024 * 1024
        ),
    )(populations, cotangent, flags, w_in.T, b_in.reshape(1, UNITS), w_out)


def shards(populations, cotangent, flags, w_in, b_in, w_out):
    d0, grad_in, grad_b, grad_out = local_step(populations, cotangent, flags, w_in, b_in, w_out)
    return d0, grad_in.T, grad_b.reshape(UNITS), grad_out


def solution(mesh):
    placed = (
        P("gx", None, "gy", None),
        P("gx", None, "gy", None),
        P("gx", "gy", None),
        P(),
        P(),
        P(),
    )
    return jax.shard_map(
        shards,
        mesh=mesh,
        in_specs=placed,
        out_specs=(P("gx", None, "gy", None), P(), P(), P()),
        check_vma=False,
    )
```

```python
import functools

import jax
import jax.numpy as jnp
from jax import lax
from jax.experimental import pallas as pl
from jax.experimental.pallas import tpu as pltpu
from jax.sharding import PartitionSpec as P

VELOCITY = [
    (0, 0, 0),
    (1, 0, 0),
    (-1, 0, 0),
    (0, 1, 0),
    (0, -1, 0),
    (0, 0, 1),
    (0, 0, -1),
    (1, 1, 0),
    (-1, -1, 0),
    (1, -1, 0),
    (-1, 1, 0),
    (1, 0, 1),
    (-1, 0, -1),
    (1, 0, -1),
    (-1, 0, 1),
    (0, 1, 1),
    (0, -1, -1),
    (0, 1, -1),
    (0, -1, 1),
]
OPPOSITE = [0, 2, 1, 4, 3, 6, 5, 8, 7, 10, 9, 12, 11, 14, 13, 16, 15, 18, 17]
INV_W = [3.0] + [18.0] * 6 + [36.0] * 12
W = [1.0 / 3.0] + [1.0 / 18.0] * 6 + [1.0 / 36.0] * 12
PAIRS = [(i, i + 1) for i in range(1, 19, 2)]
Q = 19
UNITS = 128
ROWS = 160
DEPTH = 256
HID = 8 * UNITS
LANES = 256
GROUPS = 4

X_PLUS = [1, 7, 9, 11, 13]
X_MINUS = [2, 8, 10, 12, 14]
Y_PLUS = [(3, 0), (3, 1), (15, 0), (15, 1), (17, 0), (17, 1), (7, 0), (10, 1)]
Y_MINUS = [(4, 0), (4, 1), (16, 0), (16, 1), (18, 0), (18, 1), (9, 0), (8, 1)]
CORNERS = [7, 10, 8, 9]
MESH = pl.DeviceIdType.MESH
DEV_Z = 16
PLANE = 32
CHUNK = 256
BF = jnp.bfloat16
F32 = jnp.float32
NT = (((1,), (1,)), ((), ()))
TN = (((0,), (0,)), ((), ()))


class Exchange:
    def __init__(self, refs):
        (self.own, self.sxp, self.sxm, self.syp, self.sym, self.rxl, self.rxr,
         self.ryl, self.ryu, self.rc, self.send, self.recv) = refs

    def put(self, j, p, s, val):
        cx, cy, cz = VELOCITY[j]
        if cz:
            val = pltpu.roll(val, cz % LANES, 1)
        rows = pl.ds(8 * s, 8)
        if cx == 1 and p == 1:
            self.sxp[X_PLUS.index(j), rows, :] = val
        elif cx == -1 and p == 0:
            self.sxm[X_MINUS.index(j), rows, :] = val
        else:
            self.own[p, j, rows, :] = val
        if cy == 1 and s == 1 and (j, p) in Y_PLUS:
            k = Y_PLUS.index((j, p))
            self.syp[k : k + 1, :] = val[7:8, :]
        if cy == -1 and s == 0 and (j, p) in Y_MINUS:
            k = Y_MINUS.index((j, p))
            self.sym[k : k + 1, :] = val[0:1, :]

    def send_half(self, s, near):
        rows = pl.ds(8 * s, 8)
        dy = 1 if s else -1
        plan = [
            (self.sxp.at[1 if s else 2, rows, :], self.rc.at[0 if s else 3], near(1, dy)),
            (self.sxm.at[2 if s else 1, rows, :], self.rc.at[1 if s else 2], near(-1, dy)),
            (self.sxp.at[:, rows, :], self.rxl.at[:, rows, :], near(1, 0)),
            (self.sxm.at[:, rows, :], self.rxr.at[:, rows, :], near(-1, 0)),
            (self.syp, self.ryl, near(0, 1)) if s else (self.sym, self.ryu, near(0, -1)),
        ]
        made = [
            pltpu.make_async_remote_copy(
                src_ref=src, dst_ref=dst, send_sem=self.send.at[5 * s + k],
                recv_sem=self.recv.at[5 * s + k], device_id=dev, device_id_type=MESH,
            )
            for k, (src, dst, dev) in enumerate(plan)
        ]
        for c in made:
            c.start()
        return made

    def get(self, j, p, s):
        cx, cy, cz = VELOCITY[j]
        q = p - cx
        if q == -1:
            src = self.rxl.at[X_PLUS.index(j)]
        elif q == 2:
            src = self.rxr.at[X_MINUS.index(j)]
        else:
            src = self.own.at[q, j]
        if cy == 0:
            return src[8 * s : 8 * s + 8, :]
        row = lax.broadcasted_iota(jnp.int32, (8, LANES), 0)
        if cy == 1:
            if s == 1:
                return src[7:15, :]
            if q in (0, 1):
                k = Y_PLUS.index((j, q))
                halo = self.ryl[k : k + 1, :]
            else:
                halo = self.rc[CORNERS.index(j), 7:8, :]
            return jnp.where(row == 0, halo, pltpu.roll(src[0:8, :], 1, 0))
        if s == 0:
            return src[1:9, :]
        if q in (0, 1):
            k = Y_MINUS.index((j, q))
            halo = self.ryu[k : k + 1, :]
        else:
            halo = self.rc[CORNERS.index(j), 0:1, :]
        return jnp.where(row == 7, halo, pltpu.roll(src[8:16, :], 7, 0))


EX_SCRATCH = [
    pltpu.VMEM((2, Q, 16, LANES), F32),
    pltpu.VMEM((5, 16, LANES), F32),
    pltpu.VMEM((5, 16, LANES), F32),
    pltpu.VMEM((8, LANES), F32),
    pltpu.VMEM((8, LANES), F32),
    pltpu.VMEM((5, 16, LANES), F32),
    pltpu.VMEM((5, 16, LANES), F32),
    pltpu.VMEM((8, LANES), F32),
    pltpu.VMEM((8, LANES), F32),
    pltpu.VMEM((4, 8, LANES), F32),
    pltpu.SemaphoreType.DMA((10,)),
    pltpu.SemaphoreType.DMA((10,)),
]
N_EX = len(EX_SCRATCH)


def dot(a, b, dims=None):
    if dims is None:
        return jnp.dot(a, b, preferred_element_type=F32)
    return lax.dot_general(a, b, dims, preferred_element_type=F32)


def moments(f):
    rho = f[0]
    for a, b in PAIRS:
        rho = rho + (f[a] + f[b])
    mom = []
    for d in range(3):
        acc = None
        for a, b in PAIRS:
            c = VELOCITY[a][d]
            if c == 0:
                continue
            diff = f[a] - f[b] if c == 1 else f[b] - f[a]
            acc = diff if acc is None else acc + diff
        mom.append(acc)
    return rho, mom


def along(i, vec):
    out = None
    for d in range(3):
        c = VELOCITY[i][d]
        if c == 0:
            continue
        if out is None:
            out = vec[d] if c == 1 else -vec[d]
        else:
            out = out + vec[d] if c == 1 else out - vec[d]
    return out


def equilibrium(rho, mom):
    base = rho - 1.5 * (mom[0] * mom[0] + mom[1] * mom[1] + mom[2] * mom[2])
    eq = [base]
    for a, b in PAIRS:
        u = along(a, mom)
        even = base + 4.5 * (u * u)
        odd = 3.0 * u
        eq.append(even + odd)
        eq.append(even - odd)
    return eq


def store_features(dst, lanes, vals):
    for k in range(0, len(vals), 2):
        two = jnp.concatenate([vals[k], vals[k + 1]], axis=0)
        dst[8 * k : 8 * k + 16, lanes] = two.astype(BF)


def one_hot(hit):
    return hit.astype(F32).astype(BF)


def iota(shape, dim):
    return lax.broadcasted_iota(jnp.int32, shape, dim)


def tall(w_t, masked, extra=None):
    expand = one_hot(iota((Q, DEPTH), 0) == iota((Q, DEPTH), 1) // 8)
    wide = dot(w_t, expand, TN)
    lane = iota((UNITS, DEPTH), 1) % 8
    for y in range(8):
        val = jnp.where(lane == y, wide, 0.0)
        if extra is not None:
            val = val + extra
        masked[pl.ds(UNITS * y, UNITS), :] = val.astype(BF)


def flat(w_t, masked):
    expand = one_hot(iota((ROWS, Q), 1) == iota((ROWS, Q), 0) // 8)
    wide = dot(expand, w_t)
    sub = iota((ROWS, UNITS), 0) % 8
    for y in range(8):
        masked[:, pl.ds(UNITS * y, UNITS)] = jnp.where(sub == y, wide, 0.0).astype(BF)


def bias_columns(b_in):
    hi = b_in.astype(BF)
    rest = b_in - hi.astype(F32)
    mid = rest.astype(BF)
    low = (rest - mid.astype(F32)).astype(BF)
    row = iota((8, UNITS), 0)
    parts = jnp.where(
        row == 0, hi.astype(F32),
        jnp.where(row == 1, mid.astype(F32), jnp.where(row == 2, low.astype(F32), 0.0)),
    ).astype(BF)
    place = one_hot(iota((8, DEPTH), 1) == iota((8, DEPTH), 0) + 8 * Q)
    return dot(parts, place, TN)


class Reduction:
    def __init__(self, refs, ag, gx, gy):
        (self.pay, self.rs_in, self.z_own, self.z_in, self.ag_own, self.send, self.recv) = refs
        self.ag = ag
        self.z = lax.rem(gx // 2, DEV_Z)
        core, y = lax.rem(gx, 2), gx // (2 * DEV_Z)
        self.me = y * 8 + gy * 2 + core
        cs = [core, 1 - core]
        xs = [gy] + [lax.rem(gy + k, 4) for k in range(1, 4)]
        ys = [y] + [lax.rem(y + k, 4) for k in range(1, 4)]
        self.plane = []
        for dy in range(4):
            base, mbase = ys[dy] * (2 * DEV_Z) + self.z * 2, ys[dy] * 8
            for dc in range(2):
                for dx in range(4):
                    if dx or dy or dc:
                        dev = (base + cs[dc], xs[dx])
                        self.plane.append((mbase + (xs[dx] * 2 + cs[dc]), dev))
        line = gx - 2 * self.z
        self.line = []
        for k in range(1, DEV_Z):
            self.line.append((line + 2 * lax.rem(self.z + k, DEV_Z), gy))

    def greet(self, barrier):
        for dev in [d for _, d in self.plane] + self.line:
            pl.semaphore_signal(barrier, inc=1, device_id=dev, device_id_type=MESH)
        return PLANE + DEV_Z - 2

    def remote(self, src, dst, phase, dev):
        return pltpu.make_async_remote_copy(
            src_ref=src, dst_ref=dst, send_sem=self.send.at[phase], recv_sem=self.recv.at[phase],
            device_id=dev, device_id_type=MESH,
        )

    def wait(self, src, dst, phase):
        dev = self.plane[0][1]
        both = self.remote(src, dst, phase, dev)
        both.wait_send()
        both.wait_recv()

    def scatter(self):
        for k, (m, dev) in enumerate(self.plane):
            self.remote(self.pay.at[m], self.rs_in.at[k], 0, dev).start()

    def finish(self):
        self.wait(self.pay.at[0 : PLANE - 1], self.rs_in.at[:], 0)
        part = self.pay[self.me] + jnp.sum(self.rs_in[...], axis=0)
        self.z_own[...] = part
        self.z_in[self.z] = part

        for dev in self.line:
            self.remote(self.z_own.at[:], self.z_in.at[self.z], 1, dev).start()

        sized = self.z_in.at[0 : DEV_Z - 1]
        self.wait(sized, sized, 1)
        total = jnp.sum(self.z_in[...], axis=0)
        self.ag_own[...] = total
        self.ag[self.me] = total

        for _, dev in self.plane:
            self.remote(self.ag_own.at[:], self.ag.at[self.me], 2, dev).start()

        sized = self.ag.at[0 : PLANE - 1]
        self.wait(sized, sized, 2)


RED_SCRATCH = [
    pltpu.VMEM((PLANE, 2, UNITS), F32),
    pltpu.VMEM((PLANE - 1, 2, UNITS), F32),
    pltpu.VMEM((2, UNITS), F32),
    pltpu.VMEM((DEV_Z, 2, UNITS), F32),
    pltpu.VMEM((2, UNITS), F32),
    pltpu.SemaphoreType.DMA((3,)),
    pltpu.SemaphoreType.DMA((3,)),
]
N_RED = len(RED_SCRATCH)


def kernel(pops_hbm, cot_hbm, *refs):
    small_hbm, (out, ag), scratch = refs[:4], refs[4:6], refs[6:]
    gx, gy = lax.axis_index("gx"), lax.axis_index("gy")
    (w1, w1t, w2, w2t, feat0, feat1, qa, qb, hid0, hid1, ra, rb, t0, t1, gh, field, grad,
     mom0, post, fold_out, pops, cot, flags, w_in_t, b_in, w_out, in_sem) = scratch[N_RED + 3 * N_EX :]
    get_cot = pltpu.make_async_copy(cot_hbm, cot, in_sem.at[0])
    get_pops = pltpu.make_async_copy(pops_hbm, pops, in_sem.at[1])
    gets = [
        pltpu.make_async_copy(src, dst, in_sem.at[2 + k])
        for k, (src, dst) in enumerate(zip(small_hbm, (flags, w_in_t, b_in, w_out)))
    ]
    for c in gets[1:] + [get_cot, get_pops, gets[0]]:
        c.start()
    reduction = Reduction(scratch[:N_RED], ag, gx, gy)
    ex_c, ex_p, ex_d = [
        Exchange(scratch[N_RED + k * N_EX : N_RED + (k + 1) * N_EX]) for k in range(3)
    ]
    step_x = {0: gx, 1: lax.rem(gx + 1, 128), -1: lax.rem(gx + 127, 128)}
    step_y = {0: gy, 1: lax.rem(gy + 1, 4), -1: lax.rem(gy + 3, 4)}

    def near(dx, dy):
        return (step_x[dx], step_y[dy])

    barrier = pltpu.get_barrier_semaphore()
    for dx in (1, 0, -1):
        for dy in (1, 0, -1):
            if dx or dy:
                pl.semaphore_signal(
                    barrier, inc=1, device_id=near(dx, dy), device_id_type=MESH
                )
    greeted = 8 + reduction.greet(barrier)
    for c in gets[1:]:
        c.wait()
    tall(w_in_t[...], w1, bias_columns(b_in[...]))
    flat(w_out[...], w2)
    zero = jnp.zeros((DEPTH - ROWS, GROUPS * LANES), BF)
    for ref in (feat0, feat1, qa, qb):
        ref[ROWS:, :] = zero
    reduction.pay[...] = jnp.zeros((PLANE, 2, UNITS), F32)
    get_cot.wait()
    for p in range(2):
        for i in range(Q):
            wide = cot[p, i].astype(F32)
            for s in range(2):
                ex_c.put(OPPOSITE[i], p, s, wide[8 * s : 8 * s + 8, :])
    one = jnp.ones((8, LANES), F32)
    nil = jnp.zeros((8, LANES), F32)
    get_pops.wait()
    gets[0].wait()

    def lanes_of(p, s):
        return pl.ds((2 * p + s) * LANES, LANES)

    def rows_of(s):
        return pl.ds(8 * s, 8)

    def melt_of(p, s):
        return flags[p, rows_of(s), :].astype(F32)

    def front(f, p, s, feat, hid, act):
        rho, mom = moments(f)
        eq = equilibrium(rho, mom)
        lanes = lanes_of(p, s)
        store_features(feat, lanes, [f[i] * INV_W[i] - eq[i] for i in range(Q)] + [one])
        for c in range(0, HID, CHUNK):
            block = pl.ds(c, CHUNK)
            t = jnp.tanh(dot(w1[block, :], feat[:, lanes]))
            act[block, lanes] = t
            hid[block, lanes] = t.astype(BF)
        return rho, mom, eq

    def step_a(p, s):
        f = [pops[p, i, rows_of(s), :] for i in range(Q)]
        rho, mom, eq = front(f, p, s, feat0, hid0, t0)
        for d in range(3):
            mom0[2 * p + s, d] = mom[d]
        learned = dot(w2[...], hid0[:, lanes_of(p, s)])
        melt = melt_of(p, s) > 0.5
        excess = rho - 1.0
        for i in range(Q):
            val = -0.25 * f[i] + (1.25 * W[i]) * eq[i] + learned[8 * i : 8 * i + 8, :]
            cz = VELOCITY[i][2]
            if cz:
                val = val + (0.15 * W[i] * cz) * excess
            ex_p.put(i, p, s, jnp.where(melt, val, f[OPPOSITE[i]]))

    copies_c, copies_p, copies_d = [], [], []
    for p in range(2):
        step_a(p, 1)
    pl.semaphore_wait(barrier, greeted)
    copies_c += ex_c.send_half(1, near)
    copies_c += ex_c.send_half(0, near)
    copies_p += ex_p.send_half(1, near)
    for p in range(2):
        step_a(p, 0)
    copies_p += ex_p.send_half(0, near)

    tall(w_out[...], w2t)
    flat(w_in_t[...], w1t)
    for c in copies_c:
        c.wait()

    def hidden_grad(p, s, q):
        melt = melt_of(p, s)
        m = [grad[2 * p + s, i] * melt for i in range(Q)]
        store_features(q, lanes_of(p, s), m + [nil])

    for p in range(2):
        for s in range(2):
            for i in range(Q):
                grad[2 * p + s, i] = ex_c.get(OPPOSITE[i], p, s)
            hidden_grad(p, s, qb)
            for c in range(0, HID, CHUNK):
                block = pl.ds(c, CHUNK)
                gh[block, lanes_of(p, s)] = dot(w2t[block, :], qb[:, lanes_of(p, s)])

    for c in copies_p:
        c.wait()

    def back(p, s, mom, r, put):
        g = 2 * p + s
        melt = melt_of(p, s)
        prod = dot(w1t[...], r[:, lanes_of(p, s)])
        m, wd = [], []
        for i in range(Q):
            m.append(grad[g, i] * melt)
            wd.append((1.25 * W[i]) * m[i] - prod[8 * i : 8 * i + 8, :])
        total = wd[0]
        lift = None
        dj = [None, None, None]
        for a, b in PAIRS:
            both = wd[a] + wd[b]
            total = total + both
            cz = VELOCITY[a][2]
            if cz:
                term = (0.15 * W[a] * cz) * (m[a] - m[b])
                lift = term if lift is None else lift + term
            slope = 3.0 * (wd[a] - wd[b]) + 9.0 * along(a, mom) * both
            for d in range(3):
                c = VELOCITY[a][d]
                if c == 0:
                    continue
                if dj[d] is None:
                    dj[d] = slope if c == 1 else -slope
                else:
                    dj[d] = dj[d] + slope if c == 1 else dj[d] - slope
        drho = total + lift
        dj = [dj[d] - 3.0 * mom[d] * total for d in range(3)]
        for i in range(Q):
            o = OPPOSITE[i]
            val = (-0.25) * m[i] + INV_W[i] * prod[8 * i : 8 * i + 8, :] + drho
            if i:
                val = val + along(i, dj)
            put(i, val + (grad[g, o] - m[o]))

    def step_b(p, s):
        f = [ex_p.get(i, p, s) for i in range(Q)]
        _, mom, _ = front(f, p, s, feat1, hid1, t1)
        lanes = lanes_of(p, s)
        for c in range(0, HID, CHUNK):
            block = pl.ds(c, CHUNK)
            t = t1[block, lanes]
            rb[block, lanes] = (gh[block, lanes] * (1.0 - t * t)).astype(BF)
        back(p, s, mom, rb, lambda i, val: ex_d.put(OPPOSITE[i], p, s, val))

    for s in (1, 0):
        for p in range(2):
            step_b(p, s)
        copies_d += ex_d.send_half(s, near)

    def weight_sums(feat, r, q, hid):
        sub = iota((ROWS, UNITS), 0) % 8
        sums = []
        for left, right in ((feat, r), (q, hid)):
            tot = None
            for c in range(0, HID, 256):
                acc = dot(left[:ROWS, :], right[pl.ds(c, 256), :], NT)
                for k in range(2):
                    hit = jnp.where(sub == c // UNITS + k, acc[:, UNITS * k : UNITS * (k + 1)], 0.0)
                    tot = hit if tot is None else tot + hit
            sums.append(jnp.sum(tot.reshape(20, 8, UNITS), axis=1))
        return sums

    for k, val in enumerate(weight_sums(feat1, rb, qb, hid1)):
        fold_out[0, k] = val
    for c in range(0, HID, CHUNK):
        block = pl.ds(c, CHUNK)
        t = t0[block, :]
        t0[block, :] = 1.0 - t * t

    for c in copies_d:
        c.wait()
    for p in range(2):
        for s in range(2):
            for i in range(Q):
                grad[2 * p + s, i] = ex_d.get(OPPOSITE[i], p, s)
            hidden_grad(p, s, qa)
            lanes = lanes_of(p, s)
            for c in range(0, HID, CHUNK):
                block = pl.ds(c, CHUNK)
                ra[block, lanes] = (dot(w2t[block, :], qa[:, lanes]) * t0[block, lanes]).astype(BF)

    for k, val in enumerate(weight_sums(feat0, ra, qa, hid0)):
        tot = val + fold_out[0, k]
        for j in range(10):
            reduction.pay[10 * k + j] = tot[2 * j : 2 * j + 2, :]
    reduction.scatter()

    def keep(p, s):
        def put(i, val):
            post[2 * p + s, i] = val

        return put

    for p in range(2):
        for s in range(2):
            back(p, s, [mom0[2 * p + s, d] for d in range(3)], ra, keep(p, s))
        for i in range(Q):
            out[p, i] = jnp.concatenate([post[2 * p, i], post[2 * p + 1, i]], axis=0).astype(BF)
    reduction.finish()


def finish_kernel(d0, ag, d0_ref, gin_ref, gb_ref, gout_ref, sem):
    write = pltpu.make_async_copy(d0, d0_ref, sem)
    write.start()

    def normalized(rows):
        total = jnp.concatenate(rows, axis=0)
        scale = jnp.sum(total * total) / (total.shape[0] * UNITS) + 1e-06
        return total / jnp.sqrt(scale)

    row = [ag[k // 2, k % 2 : k % 2 + 1, :] for k in range(2 * 20)]
    gin_ref[...] = normalized(row[:Q])
    gb_ref[...] = normalized(row[Q : Q + 1])
    gout_ref[...] = normalized(row[Q + 1 : 2 * Q + 1])
    write.wait()


def local_step(populations, cotangent, flags, w_in, b_in, w_out):
    vmem = pl.BlockSpec(memory_space=pltpu.VMEM)
    hbm = pl.BlockSpec(memory_space=pltpu.HBM)
    cells = GROUPS * LANES
    d0, ag = pl.pallas_call(
        kernel,
        out_shape=(
            pltpu.VMEM((2, Q, 16, LANES), BF),
            pltpu.VMEM((PLANE, 2, UNITS), F32),
        ),
        in_specs=[hbm] * 6,
        out_specs=(vmem, vmem),
        scratch_shapes=RED_SCRATCH
        + EX_SCRATCH * 3
        + [
            pltpu.VMEM((HID, DEPTH), BF),
            pltpu.VMEM((ROWS, HID), BF),
            pltpu.VMEM((ROWS, HID), BF),
            pltpu.VMEM((HID, DEPTH), BF),
            pltpu.VMEM((DEPTH, cells), BF),
            pltpu.VMEM((DEPTH, cells), BF),
            pltpu.VMEM((DEPTH, cells), BF),
            pltpu.VMEM((DEPTH, cells), BF),
            pltpu.VMEM((HID, cells), BF),
            pltpu.VMEM((HID, cells), BF),
            pltpu.VMEM((HID, cells), BF),
            pltpu.VMEM((HID, cells), BF),
            pltpu.VMEM((HID, cells), F32),
            pltpu.VMEM((HID, cells), F32),
            pltpu.VMEM((HID, cells), F32),
            pltpu.VMEM((GROUPS, Q, 8, LANES), F32),
            pltpu.VMEM((GROUPS, Q, 8, LANES), F32),
            pltpu.VMEM((GROUPS, 3, 8, LANES), F32),
            pltpu.VMEM((GROUPS, Q, 8, LANES), F32),
            pltpu.VMEM((2, 2, 20, UNITS), F32),
            pltpu.VMEM((2, Q, 16, LANES), F32),
            pltpu.VMEM((2, Q, 16, LANES), BF),
            pltpu.VMEM((2, 16, LANES), jnp.int32),
            pltpu.VMEM((Q, UNITS), BF),
            pltpu.VMEM((1, UNITS), F32),
            pltpu.VMEM((Q, UNITS), BF),
            pltpu.SemaphoreType.DMA((6,)),
        ],
        compiler_params=pltpu.CompilerParams(
            collective_id=0, has_side_effects=True, vmem_limit_bytes=66650112
        ),
    )(populations, cotangent, flags, w_in.T, b_in.reshape(1, UNITS), w_out)
    return pl.pallas_call(
        finish_kernel,
        out_shape=(
            jax.ShapeDtypeStruct((2, Q, 16, LANES), BF),
            jax.ShapeDtypeStruct((Q, UNITS), F32),
            jax.ShapeDtypeStruct((1, UNITS), F32),
            jax.ShapeDtypeStruct((Q, UNITS), F32),
        ),
        in_specs=[vmem] * 2,
        out_specs=(hbm, vmem, vmem, vmem),
        scratch_shapes=[pltpu.SemaphoreType.DMA],
        compiler_params=pltpu.CompilerParams(vmem_limit_bytes=1024 * 1024),
    )(d0, ag)


def shards(populations, cotangent, flags, w_in, b_in, w_out):
    d0, grad_in, grad_b, grad_out = local_step(populations, cotangent, flags, w_in, b_in, w_out)
    return d0, grad_in.T, grad_b.reshape(UNITS), grad_out


def solution(mesh):
    placed = (
        P("gx", None, "gy", None),
        P("gx", None, "gy", None),
        P("gx", "gy", None),
        P(),
        P(),
        P(),
    )
    return jax.shard_map(
        shards,
        mesh=mesh,
        in_specs=placed,
        out_specs=(P("gx", None, "gy", None), P(), P(), P()),
        check_vma=False,
    )
```

```python
import functools

import jax
import jax.numpy as jnp
from jax import lax
from jax.experimental import pallas as pl
from jax.experimental.pallas import tpu as pltpu
from jax.sharding import PartitionSpec as P

VELOCITY = [
    (0, 0, 0),
    (1, 0, 0),
    (-1, 0, 0),
    (0, 1, 0),
    (0, -1, 0),
    (0, 0, 1),
    (0, 0, -1),
    (1, 1, 0),
    (-1, -1, 0),
    (1, -1, 0),
    (-1, 1, 0),
    (1, 0, 1),
    (-1, 0, -1),
    (1, 0, -1),
    (-1, 0, 1),
    (0, 1, 1),
    (0, -1, -1),
    (0, 1, -1),
    (0, -1, 1),
]
OPPOSITE = [0, 2, 1, 4, 3, 6, 5, 8, 7, 10, 9, 12, 11, 14, 13, 16, 15, 18, 17]
INV_W = [3.0] + [18.0] * 6 + [36.0] * 12
W = [1.0 / 3.0] + [1.0 / 18.0] * 6 + [1.0 / 36.0] * 12
PAIRS = [(i, i + 1) for i in range(1, 19, 2)]
Q = 19
UNITS = 128
ROWS = 160
DEPTH = 256
HID = 8 * UNITS
LANES = 256
GROUPS = 4

X_PLUS = [1, 7, 9, 11, 13]
X_MINUS = [2, 8, 10, 12, 14]
Y_PLUS = [(3, 0), (3, 1), (15, 0), (15, 1), (17, 0), (17, 1), (7, 0), (10, 1)]
Y_MINUS = [(4, 0), (4, 1), (16, 0), (16, 1), (18, 0), (18, 1), (9, 0), (8, 1)]
CORNERS = [7, 10, 8, 9]
MESH = pl.DeviceIdType.MESH
DEV_Z = 16
PLANE = 32
CHUNK = 256
HALF = 128
BF = jnp.bfloat16
F32 = jnp.float32
NT = (((1,), (1,)), ((), ()))
TN = (((0,), (0,)), ((), ()))


class Exchange:
    def __init__(self, refs):
        (self.own, self.sxp, self.sxm, self.syp, self.sym, self.rxl, self.rxr,
         self.ryl, self.ryu, self.rc, self.send, self.recv) = refs

    def put(self, j, p, s, val, lanes=slice(None)):
        cx, cy, cz = VELOCITY[j]
        if cz:
            val = pltpu.roll(val, cz % LANES, 1)
        rows = pl.ds(8 * s, 8)
        if cx == 1 and p == 1:
            self.sxp[X_PLUS.index(j), rows, lanes] = val
        elif cx == -1 and p == 0:
            self.sxm[X_MINUS.index(j), rows, lanes] = val
        else:
            self.own[p, j, rows, lanes] = val
        if cy == 1 and s == 1 and (j, p) in Y_PLUS:
            k = Y_PLUS.index((j, p))
            self.syp[k : k + 1, lanes] = val[7:8, :]
        if cy == -1 and s == 0 and (j, p) in Y_MINUS:
            k = Y_MINUS.index((j, p))
            self.sym[k : k + 1, lanes] = val[0:1, :]

    def send_half(self, s, near):
        rows = pl.ds(8 * s, 8)
        dy = 1 if s else -1
        plan = [
            (self.sxp.at[1 if s else 2, rows, :], self.rc.at[0 if s else 3], near(1, dy)),
            (self.sxm.at[2 if s else 1, rows, :], self.rc.at[1 if s else 2], near(-1, dy)),
            (self.sxp.at[:, rows, :], self.rxl.at[:, rows, :], near(1, 0)),
            (self.sxm.at[:, rows, :], self.rxr.at[:, rows, :], near(-1, 0)),
            (self.syp, self.ryl, near(0, 1)) if s else (self.sym, self.ryu, near(0, -1)),
        ]
        made = [
            pltpu.make_async_remote_copy(
                src_ref=src, dst_ref=dst, send_sem=self.send.at[5 * s + k],
                recv_sem=self.recv.at[5 * s + k], device_id=dev, device_id_type=MESH,
            )
            for k, (src, dst, dev) in enumerate(plan)
        ]
        for c in made:
            c.start()
        return made

    def get(self, j, p, s, lanes=slice(None)):
        cx, cy, cz = VELOCITY[j]
        q = p - cx
        if q == -1:
            src = self.rxl.at[X_PLUS.index(j)]
        elif q == 2:
            src = self.rxr.at[X_MINUS.index(j)]
        else:
            src = self.own.at[q, j]
        if cy == 0:
            return src[8 * s : 8 * s + 8, lanes]
        if cy == 1:
            if s == 1:
                return src[7:15, lanes]
            if q in (0, 1):
                k = Y_PLUS.index((j, q))
                halo = self.ryl[k : k + 1, lanes]
            else:
                halo = self.rc[CORNERS.index(j), 7:8, lanes]
            main = pltpu.roll(src[0:8, lanes], 1, 0)
            return jnp.where(iota(main.shape, 0) == 0, halo, main)
        if s == 0:
            return src[1:9, lanes]
        if q in (0, 1):
            k = Y_MINUS.index((j, q))
            halo = self.ryu[k : k + 1, lanes]
        else:
            halo = self.rc[CORNERS.index(j), 0:1, lanes]
        main = pltpu.roll(src[8:16, lanes], 7, 0)
        return jnp.where(iota(main.shape, 0) == 7, halo, main)


EX_SCRATCH = [
    pltpu.VMEM((2, Q, 16, LANES), F32),
    pltpu.VMEM((5, 16, LANES), F32),
    pltpu.VMEM((5, 16, LANES), F32),
    pltpu.VMEM((8, LANES), F32),
    pltpu.VMEM((8, LANES), F32),
    pltpu.VMEM((5, 16, LANES), F32),
    pltpu.VMEM((5, 16, LANES), F32),
    pltpu.VMEM((8, LANES), F32),
    pltpu.VMEM((8, LANES), F32),
    pltpu.VMEM((4, 8, LANES), F32),
    pltpu.SemaphoreType.DMA((10,)),
    pltpu.SemaphoreType.DMA((10,)),
]
N_EX = len(EX_SCRATCH)


def dot(a, b, dims=None):
    if dims is None:
        return jnp.dot(a, b, preferred_element_type=F32)
    return lax.dot_general(a, b, dims, preferred_element_type=F32)


def moments(f):
    rho = f[0]
    for a, b in PAIRS:
        rho = rho + (f[a] + f[b])
    mom = []
    for d in range(3):
        acc = None
        for a, b in PAIRS:
            c = VELOCITY[a][d]
            if c == 0:
                continue
            diff = f[a] - f[b] if c == 1 else f[b] - f[a]
            acc = diff if acc is None else acc + diff
        mom.append(acc)
    return rho, mom


def along(i, vec):
    out = None
    for d in range(3):
        c = VELOCITY[i][d]
        if c == 0:
            continue
        if out is None:
            out = vec[d] if c == 1 else -vec[d]
        else:
            out = out + vec[d] if c == 1 else out - vec[d]
    return out


def equilibrium(rho, mom):
    base = rho - 1.5 * (mom[0] * mom[0] + mom[1] * mom[1] + mom[2] * mom[2])
    eq = [base]
    for a, b in PAIRS:
        u = along(a, mom)
        even = base + 4.5 * (u * u)
        odd = 3.0 * u
        eq.append(even + odd)
        eq.append(even - odd)
    return eq


def store_features(dst, lanes, vals):
    for k in range(0, len(vals), 2):
        two = jnp.concatenate([vals[k], vals[k + 1]], axis=0)
        dst[8 * k : 8 * k + 16, lanes] = two.astype(BF)


def one_hot(hit):
    return hit.astype(F32).astype(BF)


def iota(shape, dim):
    return lax.broadcasted_iota(jnp.int32, shape, dim)


def tall(w_t, masked, extra=None):
    expand = one_hot(iota((Q, DEPTH), 0) == iota((Q, DEPTH), 1) // 8)
    wide = dot(w_t, expand, TN)
    lane = iota((UNITS, DEPTH), 1) % 8
    for y in range(8):
        val = jnp.where(lane == y, wide, 0.0)
        if extra is not None:
            val = val + extra
        masked[pl.ds(UNITS * y, UNITS), :] = val.astype(BF)


def flat(w_t, masked):
    expand = one_hot(iota((ROWS, Q), 1) == iota((ROWS, Q), 0) // 8)
    wide = dot(expand, w_t)
    sub = iota((ROWS, UNITS), 0) % 8
    for y in range(8):
        masked[:, pl.ds(UNITS * y, UNITS)] = jnp.where(sub == y, wide, 0.0).astype(BF)


def bias_columns(b_in):
    hi = b_in.astype(BF)
    rest = b_in - hi.astype(F32)
    mid = rest.astype(BF)
    low = (rest - mid.astype(F32)).astype(BF)
    row = iota((8, UNITS), 0)
    parts = jnp.where(
        row == 0, hi.astype(F32),
        jnp.where(row == 1, mid.astype(F32), jnp.where(row == 2, low.astype(F32), 0.0)),
    ).astype(BF)
    place = one_hot(iota((8, DEPTH), 1) == iota((8, DEPTH), 0) + 8 * Q)
    return dot(parts, place, TN)


class Reduction:
    def __init__(self, refs, ag, gx, gy):
        (self.pay, self.rs_in, self.z_own, self.z_in, self.ag_own, self.send, self.recv,
         self.known) = refs
        self.ag = ag
        self.z = lax.rem(gx // 2, DEV_Z)
        core, y = lax.rem(gx, 2), gx // (2 * DEV_Z)
        self.gx, self.gy, self.core, self.y = gx, gy, core, y
        self.me = y * 8 + gy * 2 + core
        cs = [core, 1 - core]
        xs = [gy] + [lax.rem(gy + k, 4) for k in range(1, 4)]
        ys = [y] + [lax.rem(y + k, 4) for k in range(1, 4)]
        self.plane, far = [], []
        for dy in range(4):
            base, mbase = ys[dy] * (2 * DEV_Z) + self.z * 2, ys[dy] * 8
            for dc in range(2):
                for dx in range(4):
                    if dx or dy or dc:
                        dev = (base + cs[dc], xs[dx])
                        far.append((-min(dx, 4 - dx) - min(dy, 4 - dy), len(far)))
                        self.plane.append((mbase + (xs[dx] * 2 + cs[dc]), dev))
        self.plane = [self.plane[k] for _, k in sorted(far)]
        line = gx - 2 * self.z
        self.line = []
        for k in sorted(range(1, DEV_Z), key=lambda k: -min(k, DEV_Z - k)):
            self.line.append((line + 2 * lax.rem(self.z + k, DEV_Z), gy))

    def greet(self, barrier):
        for dev in self.axis("z", 1) + self.axis("y", 1):
            pl.semaphore_signal(barrier, inc=1, device_id=dev, device_id_type=MESH)
        return 4

    def axis(self, name, k):
        if name == "z":
            base = self.gx - 2 * self.z
            return [
                (base + 2 * lax.rem(self.z + d, DEV_Z), self.gy) for d in (k, DEV_Z - k)
            ]
        if name == "y":
            base = self.gx - self.y * (2 * DEV_Z)
            return [
                (base + (2 * DEV_Z) * lax.rem(self.y + d, 4), self.gy) for d in (k, 4 - k)
            ]
        if name == "x":
            return [(self.gx, lax.rem(self.gy + d, 4)) for d in (k, 4 - k)]
        return [(self.gx - self.core + (1 - self.core), self.gy)]

    def tell(self, step):
        peers = self.axis("y", 1) + self.axis("x", 1) + self.axis("core", 1)
        if step < 3:
            peers = self.axis("z", 2**step) + peers
        for dev in peers:
            pl.semaphore_signal(self.known.at[step], inc=1, device_id=dev, device_id_type=MESH)

    def hear(self, step):
        pl.semaphore_wait(self.known.at[step], 7 if step < 3 else 5)

    def remote(self, src, dst, phase, dev):
        return pltpu.make_async_remote_copy(
            src_ref=src, dst_ref=dst, send_sem=self.send.at[phase], recv_sem=self.recv.at[phase],
            device_id=dev, device_id_type=MESH,
        )

    def wait(self, src, dst, phase):
        dev = self.plane[0][1]
        both = self.remote(src, dst, phase, dev)
        both.wait_send()
        both.wait_recv()

    def scatter(self):
        for k, (m, dev) in enumerate(self.plane):
            self.remote(self.pay.at[m], self.rs_in.at[k], 0, dev).start()

    def finish(self):
        self.wait(self.pay.at[0 : PLANE - 1], self.rs_in.at[:], 0)
        part = self.pay[self.me] + jnp.sum(self.rs_in[...], axis=0)
        self.z_own[...] = part
        self.z_in[self.z] = part

        for dev in self.line:
            self.remote(self.z_own.at[:], self.z_in.at[self.z], 1, dev).start()

        sized = self.z_in.at[0 : DEV_Z - 1]
        self.wait(sized, sized, 1)
        total = jnp.sum(self.z_in[...], axis=0)
        self.ag_own[...] = total
        self.ag[self.me] = total

        for _, dev in self.plane:
            self.remote(self.ag_own.at[:], self.ag.at[self.me], 2, dev).start()

        sized = self.ag.at[0 : PLANE - 1]
        self.wait(sized, sized, 2)


RED_SCRATCH = [
    pltpu.VMEM((PLANE, 2, UNITS), F32),
    pltpu.VMEM((PLANE - 1, 2, UNITS), F32),
    pltpu.VMEM((2, UNITS), F32),
    pltpu.VMEM((DEV_Z, 2, UNITS), F32),
    pltpu.VMEM((2, UNITS), F32),
    pltpu.SemaphoreType.DMA((3,)),
    pltpu.SemaphoreType.DMA((3,)),
    pltpu.SemaphoreType.REGULAR((4,)),
]
N_RED = len(RED_SCRATCH)


def kernel(pops_hbm, cot_hbm, *refs):
    small_hbm, (out, ag), scratch = refs[:4], refs[4:6], refs[6:]
    gx, gy = lax.axis_index("gx"), lax.axis_index("gy")
    (w1, w1t, w2, w2t, feat0, feat1, qa, qb, hid0, hid1, ra, rb, t0, gh, grad,
     mom0, mom1, post, tot_ref, pops, cot, flags, w_in_t, b_in, w_out, in_sem) = scratch[N_RED + 3 * N_EX :]
    get_cot = pltpu.make_async_copy(cot_hbm, cot, in_sem.at[0])
    get_pops = pltpu.make_async_copy(pops_hbm, pops, in_sem.at[1])
    gets = [
        pltpu.make_async_copy(src, dst, in_sem.at[2 + k])
        for k, (src, dst) in enumerate(zip(small_hbm, (flags, w_in_t, b_in, w_out)))
    ]
    for c in gets[1:] + [get_cot, get_pops, gets[0]]:
        c.start()
    reduction = Reduction(scratch[:N_RED], ag, gx, gy)
    ex_c, ex_p, ex_d = [
        Exchange(scratch[N_RED + k * N_EX : N_RED + (k + 1) * N_EX]) for k in range(3)
    ]
    step_x = {0: gx, 1: lax.rem(gx + 1, 128), -1: lax.rem(gx + 127, 128)}
    step_y = {0: gy, 1: lax.rem(gy + 1, 4), -1: lax.rem(gy + 3, 4)}

    def near(dx, dy):
        return (step_x[dx], step_y[dy])

    barrier = pltpu.get_barrier_semaphore()
    for dx in (1, 0, -1):
        for dy in (1, 0, -1):
            if dx or dy:
                pl.semaphore_signal(
                    barrier, inc=1, device_id=near(dx, dy), device_id_type=MESH
                )
    greeted = 8 + reduction.greet(barrier)
    for c in gets[1:]:
        c.wait()
    tall(w_in_t[...], w1, bias_columns(b_in[...]))
    flat(w_out[...], w2)
    zero = jnp.zeros((DEPTH - ROWS, GROUPS * LANES), BF)
    for ref in (feat0, feat1, qa, qb):
        ref[ROWS:, :] = zero
    reduction.pay[...] = jnp.zeros((PLANE, 2, UNITS), F32)
    get_cot.wait()
    for p in range(2):
        for i in range(Q):
            wide = cot[p, i].astype(F32)
            for s in range(2):
                ex_c.put(OPPOSITE[i], p, s, wide[8 * s : 8 * s + 8, :])
    one = jnp.ones((8, HALF), F32)
    nil = jnp.zeros((8, HALF), F32)
    get_pops.wait()
    gets[0].wait()

    def lanes_of(p, s, h=None):
        first = (2 * p + s) * LANES
        return pl.ds(first, LANES) if h is None else pl.ds(first + h * HALF, HALF)

    def rows_of(s):
        return pl.ds(8 * s, 8)

    halves = [pl.ds(h * HALF, HALF) for h in range(LANES // HALF)]

    def melt_of(p, s, h):
        return flags[p, rows_of(s), h].astype(F32)

    def front(read, p, s, feat, mom_ref, rest):
        for k, h in enumerate(halves):
            f = [read(i, h) for i in range(Q)]
            rho, mom = moments(f)
            for d in range(3):
                mom_ref[2 * p + s, d, :, h] = mom[d]
            eq = equilibrium(rho, mom)
            store_features(
                feat, lanes_of(p, s, k), [f[i] * INV_W[i] - eq[i] for i in range(Q)] + [one]
            )
            if rest is not None:
                rest(h, f, rho, eq)

    def step_a(p, s):
        g = 2 * p + s

        def rest(h, f, rho, eq):
            melt = melt_of(p, s, h) > 0.5
            excess = rho - 1.0
            for i in range(Q):
                val = -0.25 * f[i] + (1.25 * W[i]) * eq[i]
                cz = VELOCITY[i][2]
                if cz:
                    val = val + (0.15 * W[i] * cz) * excess
                post[g, i, :, h] = jnp.where(melt, val, f[OPPOSITE[i]])

        front(lambda i, h: pops[p, i, rows_of(s), h], p, s, feat0, mom0, rest)
        lanes = lanes_of(p, s)
        for c in range(0, HID, CHUNK):
            block = pl.ds(c, CHUNK)
            t = jnp.tanh(dot(w1[block, :], feat0[:, lanes]))
            t0[block, lanes] = t
            hid0[block, lanes] = t.astype(BF)
        learned = dot(w2[...], hid0[:, lanes])
        melt = melt_of(p, s, slice(None)) > 0.5
        for i in range(Q):
            ex_p.put(i, p, s, post[g, i] + jnp.where(melt, learned[8 * i : 8 * i + 8, :], 0.0))

    copies_c, copies_p, copies_d = [], [], []
    for p in range(2):
        step_a(p, 1)
    pl.semaphore_wait(barrier, greeted)
    copies_c += ex_c.send_half(1, near)
    copies_c += ex_c.send_half(0, near)
    copies_p += ex_p.send_half(1, near)
    for p in range(2):
        step_a(p, 0)
    copies_p += ex_p.send_half(0, near)
    reduction.tell(0)

    tall(w_out[...], w2t)
    flat(w_in_t[...], w1t)
    tot_ref[...] = jnp.zeros((2, ROWS, UNITS), F32)
    for c in copies_c:
        c.wait()

    def take(ex, p, s, q):
        for k, h in enumerate(halves):
            melt = melt_of(p, s, h)
            m = []
            for i in range(Q):
                val = ex.get(OPPOSITE[i], p, s, h)
                grad[2 * p + s, i, :, h] = val
                m.append(val * melt)
            store_features(q, lanes_of(p, s, k), m + [nil])

    for p in range(2):
        for s in range(2):
            take(ex_c, p, s, qb)
            lanes = lanes_of(p, s)
            for c in range(0, HID, CHUNK):
                block = pl.ds(c, CHUNK)
                gh[block, lanes] = dot(w2t[block, :], qb[:, lanes])

    @pl.loop(0, HID // 32)
    def _(k):
        block = pl.ds(pl.multiple_of(32 * k, 32), 32)
        t = t0[block, :]
        t0[block, :] = 1.0 - t * t

    reduction.hear(0)
    reduction.tell(1)
    for c in copies_p:
        c.wait()

    def back(p, s, mom_ref, r, put):
        g = 2 * p + s
        prod = dot(w1t[...], r[:, lanes_of(p, s)])
        for k, h in enumerate(halves):
            melt = melt_of(p, s, h)
            mom = [mom_ref[g, d, :, h] for d in range(3)]
            pr = [prod[8 * i : 8 * i + 8, HALF * k : HALF * (k + 1)] for i in range(Q)]
            m = [grad[g, i, :, h] * melt for i in range(Q)]
            wd = [(1.25 * W[i]) * m[i] - pr[i] for i in range(Q)]
            total = wd[0]
            lift = None
            dj = [None, None, None]
            for a, b in PAIRS:
                both = wd[a] + wd[b]
                total = total + both
                cz = VELOCITY[a][2]
                if cz:
                    term = (0.15 * W[a] * cz) * (m[a] - m[b])
                    lift = term if lift is None else lift + term
                slope = 3.0 * (wd[a] - wd[b]) + 9.0 * along(a, mom) * both
                for d in range(3):
                    c = VELOCITY[a][d]
                    if c == 0:
                        continue
                    if dj[d] is None:
                        dj[d] = slope if c == 1 else -slope
                    else:
                        dj[d] = dj[d] + slope if c == 1 else dj[d] - slope
            drho = total + lift
            dj = [dj[d] - 3.0 * mom[d] * total for d in range(3)]
            put(h, 0, (-0.25) * m[0] + INV_W[0] * pr[0] + drho + (grad[g, 0, :, h] - m[0]))
            for a, b in PAIRS:
                turn = along(a, dj)
                for i, o, base in ((a, b, drho + turn), (b, a, drho - turn)):
                    val = (-0.25) * m[i] + INV_W[i] * pr[i] + base
                    put(h, i, val + (grad[g, o, :, h] - m[o]))

    def step_b(p, s):
        g = 2 * p + s
        front(lambda i, h: ex_p.get(i, p, s, h), p, s, feat1, mom1, None)
        lanes = lanes_of(p, s)
        for c in range(0, HID, CHUNK):
            block = pl.ds(c, CHUNK)
            t = jnp.tanh(dot(w1[block, :], feat1[:, lanes]))
            hid1[block, lanes] = t.astype(BF)
            rb[block, lanes] = (gh[block, lanes] * (1.0 - t * t)).astype(BF)

        def put(h, i, val):
            if VELOCITY[i][2]:
                post[g, i, :, h] = val
            else:
                ex_d.put(OPPOSITE[i], p, s, val, h)

        back(p, s, mom1, rb, put)
        for i in range(Q):
            if VELOCITY[i][2]:
                ex_d.put(OPPOSITE[i], p, s, post[g, i])

    for s in (1, 0):
        for p in range(2):
            step_b(p, s)
        copies_d += ex_d.send_half(s, near)

    sub = iota((ROWS, UNITS), 0) % 8

    reduction.hear(1)
    reduction.tell(2)

    @pl.loop(0, HID // 256)
    def _(c):
        block = pl.ds(pl.multiple_of(256 * c, 256), 256)
        for k, (left, right) in enumerate(((qb, hid1), (feat1, rb))):
            acc = dot(left[:ROWS, :], right[block, :], NT)
            tot_ref[k] += jnp.where(sub == 2 * c, acc[:, :UNITS], 0.0) + jnp.where(
                sub == 2 * c + 1, acc[:, UNITS:], 0.0
            )

    reduction.hear(2)
    reduction.tell(3)
    for c in copies_d:
        c.wait()
    for p in range(2):
        for s in range(2):
            take(ex_d, p, s, qa)
            lanes = lanes_of(p, s)
            for c in range(0, HID, CHUNK):
                block = pl.ds(c, CHUNK)
                ra[block, lanes] = (dot(w2t[block, :], qa[:, lanes]) * t0[block, lanes]).astype(BF)

    for k, (left, right) in enumerate(((qa, hid0), (feat0, ra))):
        tot = tot_ref[k]
        for c in range(HID // 256):
            acc = dot(left[:ROWS, :], right[pl.ds(256 * c, 256), :], NT)
            for y in range(2):
                tot = tot + jnp.where(sub == 2 * c + y, acc[:, UNITS * y : UNITS * (y + 1)], 0.0)
        tot = jnp.sum(tot.reshape(20, 8, UNITS), axis=1)
        for j in range(10):
            reduction.pay[10 * (1 - k) + j] = tot[2 * j : 2 * j + 2, :]
    reduction.hear(3)
    reduction.scatter()

    for p in range(2):
        for s in range(2):

            def put(h, i, val):
                post[2 * p + s, i, :, h] = val

            back(p, s, mom0, ra, put)
        for i in range(Q):
            out[p, i] = jnp.concatenate([post[2 * p, i], post[2 * p + 1, i]], axis=0).astype(BF)
    reduction.finish()


def finish_kernel(d0, ag, d0_ref, gin_ref, gb_ref, gout_ref, sem):
    write = pltpu.make_async_copy(d0, d0_ref, sem)
    write.start()

    def normalized(rows):
        total = jnp.concatenate(rows, axis=0)
        scale = jnp.sum(total * total) / (total.shape[0] * UNITS) + 1e-06
        return total / jnp.sqrt(scale)

    row = [ag[k // 2, k % 2 : k % 2 + 1, :] for k in range(2 * 20)]
    gin_ref[...] = normalized(row[:Q])
    gb_ref[...] = normalized(row[Q : Q + 1])
    gout_ref[...] = normalized(row[Q + 1 : 2 * Q + 1])
    write.wait()


def local_step(populations, cotangent, flags, w_in, b_in, w_out):
    vmem = pl.BlockSpec(memory_space=pltpu.VMEM)
    hbm = pl.BlockSpec(memory_space=pltpu.HBM)
    cells = GROUPS * LANES
    d0, ag = pl.pallas_call(
        kernel,
        out_shape=(
            pltpu.VMEM((2, Q, 16, LANES), BF),
            pltpu.VMEM((PLANE, 2, UNITS), F32),
        ),
        in_specs=[hbm] * 6,
        out_specs=(vmem, vmem),
        scratch_shapes=RED_SCRATCH
        + EX_SCRATCH * 3
        + [
            pltpu.VMEM((HID, DEPTH), BF),
            pltpu.VMEM((ROWS, HID), BF),
            pltpu.VMEM((ROWS, HID), BF),
            pltpu.VMEM((HID, DEPTH), BF),
            pltpu.VMEM((DEPTH, cells), BF),
            pltpu.VMEM((DEPTH, cells), BF),
            pltpu.VMEM((DEPTH, cells), BF),
            pltpu.VMEM((DEPTH, cells), BF),
            pltpu.VMEM((HID, cells), BF),
            pltpu.VMEM((HID, cells), BF),
            pltpu.VMEM((HID, cells), BF),
            pltpu.VMEM((HID, cells), BF),
            pltpu.VMEM((HID, cells), F32),
            pltpu.VMEM((HID, cells), F32),
            pltpu.VMEM((GROUPS, Q, 8, LANES), F32),
            pltpu.VMEM((GROUPS, 3, 8, LANES), F32),
            pltpu.VMEM((GROUPS, 3, 8, LANES), F32),
            pltpu.VMEM((GROUPS, Q, 8, LANES), F32),
            pltpu.VMEM((2, ROWS, UNITS), F32),
            pltpu.VMEM((2, Q, 16, LANES), F32),
            pltpu.VMEM((2, Q, 16, LANES), BF),
            pltpu.VMEM((2, 16, LANES), jnp.int32),
            pltpu.VMEM((Q, UNITS), BF),
            pltpu.VMEM((1, UNITS), F32),
            pltpu.VMEM((Q, UNITS), BF),
            pltpu.SemaphoreType.DMA((6,)),
        ],
        compiler_params=pltpu.CompilerParams(
            collective_id=0, has_side_effects=True, vmem_limit_bytes=66650112
        ),
    )(populations, cotangent, flags, w_in.T, b_in.reshape(1, UNITS), w_out)
    return pl.pallas_call(
        finish_kernel,
        out_shape=(
            jax.ShapeDtypeStruct((2, Q, 16, LANES), BF),
            jax.ShapeDtypeStruct((Q, UNITS), F32),
            jax.ShapeDtypeStruct((1, UNITS), F32),
            jax.ShapeDtypeStruct((Q, UNITS), F32),
        ),
        in_specs=[vmem] * 2,
        out_specs=(hbm, vmem, vmem, vmem),
        scratch_shapes=[pltpu.SemaphoreType.DMA],
        compiler_params=pltpu.CompilerParams(vmem_limit_bytes=1024 * 1024),
    )(d0, ag)


def shards(populations, cotangent, flags, w_in, b_in, w_out):
    d0, grad_in, grad_b, grad_out = local_step(populations, cotangent, flags, w_in, b_in, w_out)
    return d0, grad_in.T, grad_b.reshape(UNITS), grad_out


def solution(mesh):
    placed = (
        P("gx", None, "gy", None),
        P("gx", None, "gy", None),
        P("gx", "gy", None),
        P(),
        P(),
        P(),
    )
    return jax.shard_map(
        shards,
        mesh=mesh,
        in_specs=placed,
        out_specs=(P("gx", None, "gy", None), P(), P(), P()),
        check_vma=False,
    )
```

```python
import functools

import jax
import jax.numpy as jnp
from jax import lax
from jax.experimental import pallas as pl
from jax.experimental.pallas import tpu as pltpu
from jax.sharding import PartitionSpec as P

VELOCITY = [
    (0, 0, 0),
    (1, 0, 0),
    (-1, 0, 0),
    (0, 1, 0),
    (0, -1, 0),
    (0, 0, 1),
    (0, 0, -1),
    (1, 1, 0),
    (-1, -1, 0),
    (1, -1, 0),
    (-1, 1, 0),
    (1, 0, 1),
    (-1, 0, -1),
    (1, 0, -1),
    (-1, 0, 1),
    (0, 1, 1),
    (0, -1, -1),
    (0, 1, -1),
    (0, -1, 1),
]
OPPOSITE = [0, 2, 1, 4, 3, 6, 5, 8, 7, 10, 9, 12, 11, 14, 13, 16, 15, 18, 17]
INV_W = [3.0] + [18.0] * 6 + [36.0] * 12
W = [1.0 / 3.0] + [1.0 / 18.0] * 6 + [1.0 / 36.0] * 12
PAIRS = [(i, i + 1) for i in range(1, 19, 2)]
Q = 19
UNITS = 128
ROWS = 160
DEPTH = 256
HID = 8 * UNITS
LANES = 256
GROUPS = 4

X_PLUS = [1, 7, 9, 11, 13]
X_MINUS = [2, 8, 10, 12, 14]
Y_PLUS = [(3, 0), (3, 1), (15, 0), (15, 1), (17, 0), (17, 1), (7, 0), (10, 1)]
Y_MINUS = [(4, 0), (4, 1), (16, 0), (16, 1), (18, 0), (18, 1), (9, 0), (8, 1)]
CORNERS = [7, 10, 8, 9]
MESH = pl.DeviceIdType.MESH
DEV_Z = 16
PLANE = 32
CHUNK = 256
HALF = 128
BF = jnp.bfloat16
F32 = jnp.float32
NT = (((1,), (1,)), ((), ()))
TN = (((0,), (0,)), ((), ()))


class Exchange:
    def __init__(self, refs):
        (self.own, self.sxp, self.sxm, self.syp, self.sym, self.rxl, self.rxr,
         self.ryl, self.ryu, self.rc, self.send, self.recv) = refs

    def put(self, j, p, s, val, lanes=slice(None)):
        cx, cy, cz = VELOCITY[j]
        if cz:
            val = pltpu.roll(val, cz % LANES, 1)
        rows = pl.ds(8 * s, 8)
        if cx == 1 and p == 1:
            self.sxp[X_PLUS.index(j), rows, lanes] = val
        elif cx == -1 and p == 0:
            self.sxm[X_MINUS.index(j), rows, lanes] = val
        else:
            self.own[p, j, rows, lanes] = val
        if cy == 1 and s == 1 and (j, p) in Y_PLUS:
            k = Y_PLUS.index((j, p))
            self.syp[k : k + 1, lanes] = val[7:8, :]
        if cy == -1 and s == 0 and (j, p) in Y_MINUS:
            k = Y_MINUS.index((j, p))
            self.sym[k : k + 1, lanes] = val[0:1, :]

    def send_half(self, s, near):
        rows = pl.ds(8 * s, 8)
        dy = 1 if s else -1
        plan = [
            (self.sxp.at[1 if s else 2, rows, :], self.rc.at[0 if s else 3], near(1, dy)),
            (self.sxm.at[2 if s else 1, rows, :], self.rc.at[1 if s else 2], near(-1, dy)),
            (self.sxp.at[:, rows, :], self.rxl.at[:, rows, :], near(1, 0)),
            (self.sxm.at[:, rows, :], self.rxr.at[:, rows, :], near(-1, 0)),
            (self.syp, self.ryl, near(0, 1)) if s else (self.sym, self.ryu, near(0, -1)),
        ]
        made = [
            pltpu.make_async_remote_copy(
                src_ref=src, dst_ref=dst, send_sem=self.send.at[5 * s + k],
                recv_sem=self.recv.at[5 * s + k], device_id=dev, device_id_type=MESH,
            )
            for k, (src, dst, dev) in enumerate(plan)
        ]
        for c in made:
            c.start()
        return made

    def get(self, j, p, s, lanes=slice(None)):
        cx, cy, cz = VELOCITY[j]
        q = p - cx
        if q == -1:
            src = self.rxl.at[X_PLUS.index(j)]
        elif q == 2:
            src = self.rxr.at[X_MINUS.index(j)]
        else:
            src = self.own.at[q, j]
        if cy == 0:
            return src[8 * s : 8 * s + 8, lanes]
        if cy == 1:
            if s == 1:
                return src[7:15, lanes]
            if q in (0, 1):
                k = Y_PLUS.index((j, q))
                halo = self.ryl[k : k + 1, lanes]
            else:
                halo = self.rc[CORNERS.index(j), 7:8, lanes]
            main = pltpu.roll(src[0:8, lanes], 1, 0)
            return jnp.where(iota(main.shape, 0) == 0, halo, main)
        if s == 0:
            return src[1:9, lanes]
        if q in (0, 1):
            k = Y_MINUS.index((j, q))
            halo = self.ryu[k : k + 1, lanes]
        else:
            halo = self.rc[CORNERS.index(j), 0:1, lanes]
        main = pltpu.roll(src[8:16, lanes], 7, 0)
        return jnp.where(iota(main.shape, 0) == 7, halo, main)


EX_SCRATCH = [
    pltpu.VMEM((2, Q, 16, LANES), F32),
    pltpu.VMEM((5, 16, LANES), F32),
    pltpu.VMEM((5, 16, LANES), F32),
    pltpu.VMEM((8, LANES), F32),
    pltpu.VMEM((8, LANES), F32),
    pltpu.VMEM((5, 16, LANES), F32),
    pltpu.VMEM((5, 16, LANES), F32),
    pltpu.VMEM((8, LANES), F32),
    pltpu.VMEM((8, LANES), F32),
    pltpu.VMEM((4, 8, LANES), F32),
    pltpu.SemaphoreType.DMA((10,)),
    pltpu.SemaphoreType.DMA((10,)),
]
N_EX = len(EX_SCRATCH)


def dot(a, b, dims=None):
    if dims is None:
        return jnp.dot(a, b, preferred_element_type=F32)
    return lax.dot_general(a, b, dims, preferred_element_type=F32)


def moments(f):
    rho = f[0]
    for a, b in PAIRS:
        rho = rho + (f[a] + f[b])
    mom = []
    for d in range(3):
        acc = None
        for a, b in PAIRS:
            c = VELOCITY[a][d]
            if c == 0:
                continue
            diff = f[a] - f[b] if c == 1 else f[b] - f[a]
            acc = diff if acc is None else acc + diff
        mom.append(acc)
    return rho, mom


def along(i, vec):
    out = None
    for d in range(3):
        c = VELOCITY[i][d]
        if c == 0:
            continue
        if out is None:
            out = vec[d] if c == 1 else -vec[d]
        else:
            out = out + vec[d] if c == 1 else out - vec[d]
    return out


def equilibrium(rho, mom):
    base = rho - 1.5 * (mom[0] * mom[0] + mom[1] * mom[1] + mom[2] * mom[2])
    eq = [base]
    for a, b in PAIRS:
        u = along(a, mom)
        even = base + 4.5 * (u * u)
        odd = 3.0 * u
        eq.append(even + odd)
        eq.append(even - odd)
    return eq


def store_features(dst, lanes, vals):
    for k in range(0, len(vals), 2):
        two = jnp.concatenate([vals[k], vals[k + 1]], axis=0)
        dst[8 * k : 8 * k + 16, lanes] = two.astype(BF)


def one_hot(hit):
    return hit.astype(F32).astype(BF)


def iota(shape, dim):
    return lax.broadcasted_iota(jnp.int32, shape, dim)


def tall(w_t, masked, extra=None):
    expand = one_hot(iota((Q, DEPTH), 0) == iota((Q, DEPTH), 1) // 8)
    wide = dot(w_t, expand, TN)
    lane = iota((UNITS, DEPTH), 1) % 8
    for y in range(8):
        val = jnp.where(lane == y, wide, 0.0)
        if extra is not None:
            val = val + extra
        masked[pl.ds(UNITS * y, UNITS), :] = val.astype(BF)


def flat(w_t, masked):
    expand = one_hot(iota((ROWS, Q), 1) == iota((ROWS, Q), 0) // 8)
    wide = dot(expand, w_t)
    sub = iota((ROWS, UNITS), 0) % 8
    for y in range(8):
        masked[:, pl.ds(UNITS * y, UNITS)] = jnp.where(sub == y, wide, 0.0).astype(BF)


def bias_columns(b_in):
    hi = b_in.astype(BF)
    rest = b_in - hi.astype(F32)
    mid = rest.astype(BF)
    low = (rest - mid.astype(F32)).astype(BF)
    row = iota((8, UNITS), 0)
    parts = jnp.where(
        row == 0, hi.astype(F32),
        jnp.where(row == 1, mid.astype(F32), jnp.where(row == 2, low.astype(F32), 0.0)),
    ).astype(BF)
    place = one_hot(iota((8, DEPTH), 1) == iota((8, DEPTH), 0) + 8 * Q)
    return dot(parts, place, TN)


class Reduction:
    def __init__(self, refs, ag, gx, gy):
        (self.pay, self.rs_in, self.z_own, self.z_in, self.ag_own, self.send, self.recv,
         self.known) = refs
        self.ag = ag
        self.z = lax.rem(gx // 2, DEV_Z)
        core, y = lax.rem(gx, 2), gx // (2 * DEV_Z)
        self.gx, self.gy, self.core, self.y = gx, gy, core, y
        self.me = y * 8 + gy * 2 + core
        cs = [core, 1 - core]
        xs = [gy] + [lax.rem(gy + k, 4) for k in range(1, 4)]
        ys = [y] + [lax.rem(y + k, 4) for k in range(1, 4)]
        self.plane, far = [], []
        for dy in range(4):
            base, mbase = ys[dy] * (2 * DEV_Z) + self.z * 2, ys[dy] * 8
            for dc in range(2):
                for dx in range(4):
                    if dx or dy or dc:
                        dev = (base + cs[dc], xs[dx])
                        far.append((-min(dx, 4 - dx) - min(dy, 4 - dy), len(far)))
                        self.plane.append((mbase + (xs[dx] * 2 + cs[dc]), dev))
        self.plane = [self.plane[k] for _, k in sorted(far)]
        line = gx - 2 * self.z
        self.line = []
        for k in sorted(range(1, DEV_Z), key=lambda k: -min(k, DEV_Z - k)):
            self.line.append((line + 2 * lax.rem(self.z + k, DEV_Z), gy))

    def greet(self, barrier):
        for dev in self.axis("z", 1) + self.axis("y", 1):
            pl.semaphore_signal(barrier, inc=1, device_id=dev, device_id_type=MESH)
        return 4

    def axis(self, name, k):
        if name == "z":
            base = self.gx - 2 * self.z
            return [
                (base + 2 * lax.rem(self.z + d, DEV_Z), self.gy) for d in (k, DEV_Z - k)
            ]
        if name == "y":
            base = self.gx - self.y * (2 * DEV_Z)
            return [
                (base + (2 * DEV_Z) * lax.rem(self.y + d, 4), self.gy) for d in (k, 4 - k)
            ]
        if name == "x":
            return [(self.gx, lax.rem(self.gy + d, 4)) for d in (k, 4 - k)]
        return [(self.gx - self.core + (1 - self.core), self.gy)]

    def tell(self, step):
        peers = self.axis("y", 1) + self.axis("x", 1) + self.axis("core", 1)
        if step < 3:
            peers = self.axis("z", 2**step) + peers
        for dev in peers:
            pl.semaphore_signal(self.known.at[step], inc=1, device_id=dev, device_id_type=MESH)

    def hear(self, step):
        pl.semaphore_wait(self.known.at[step], 7 if step < 3 else 5)

    def remote(self, src, dst, phase, dev):
        return pltpu.make_async_remote_copy(
            src_ref=src, dst_ref=dst, send_sem=self.send.at[phase], recv_sem=self.recv.at[phase],
            device_id=dev, device_id_type=MESH,
        )

    def wait(self, src, dst, phase):
        dev = self.plane[0][1]
        both = self.remote(src, dst, phase, dev)
        both.wait_send()
        both.wait_recv()

    def scatter(self):
        for k, (m, dev) in enumerate(self.plane):
            self.remote(self.pay.at[m], self.rs_in.at[k], 0, dev).start()

    def finish(self):
        self.wait(self.pay.at[0 : PLANE - 1], self.rs_in.at[:], 0)
        part = self.pay[self.me] + jnp.sum(self.rs_in[...], axis=0)
        self.z_own[...] = part
        self.z_in[self.z] = part

        for dev in self.line:
            self.remote(self.z_own.at[:], self.z_in.at[self.z], 1, dev).start()

        sized = self.z_in.at[0 : DEV_Z - 1]
        self.wait(sized, sized, 1)
        total = jnp.sum(self.z_in[...], axis=0)
        self.ag_own[...] = total
        self.ag[self.me] = total

        for _, dev in self.plane:
            self.remote(self.ag_own.at[:], self.ag.at[self.me], 2, dev).start()

        sized = self.ag.at[0 : PLANE - 1]
        self.wait(sized, sized, 2)


RED_SCRATCH = [
    pltpu.VMEM((PLANE, 2, UNITS), F32),
    pltpu.VMEM((PLANE - 1, 2, UNITS), F32),
    pltpu.VMEM((2, UNITS), F32),
    pltpu.VMEM((DEV_Z, 2, UNITS), F32),
    pltpu.VMEM((2, UNITS), F32),
    pltpu.SemaphoreType.DMA((3,)),
    pltpu.SemaphoreType.DMA((3,)),
    pltpu.SemaphoreType.REGULAR((4,)),
]
N_RED = len(RED_SCRATCH)


def kernel(pops_hbm, cot_hbm, *refs):
    small_hbm, (out, ag), scratch = refs[:4], refs[4:6], refs[6:]
    gx, gy = lax.axis_index("gx"), lax.axis_index("gy")
    (w1, w1t, w2, w2t, feat0, feat1, qa, qb, hid0, hid1, ra, rb, t0, gh, grad,
     mom0, mom1, post, tot_ref, pops, cot, flags, w_in_t, b_in, w_out, in_sem) = scratch[N_RED + 3 * N_EX :]
    get_cot = pltpu.make_async_copy(cot_hbm, cot, in_sem.at[0])
    get_pops = pltpu.make_async_copy(pops_hbm, pops, in_sem.at[1])
    gets = [
        pltpu.make_async_copy(src, dst, in_sem.at[2 + k])
        for k, (src, dst) in enumerate(zip(small_hbm, (flags, w_in_t, b_in, w_out)))
    ]
    for c in gets[1:] + [get_cot, get_pops, gets[0]]:
        c.start()
    reduction = Reduction(scratch[:N_RED], ag, gx, gy)
    ex_c, ex_p, ex_d = [
        Exchange(scratch[N_RED + k * N_EX : N_RED + (k + 1) * N_EX]) for k in range(3)
    ]
    step_x = {0: gx, 1: lax.rem(gx + 1, 128), -1: lax.rem(gx + 127, 128)}
    step_y = {0: gy, 1: lax.rem(gy + 1, 4), -1: lax.rem(gy + 3, 4)}

    def near(dx, dy):
        return (step_x[dx], step_y[dy])

    barrier = pltpu.get_barrier_semaphore()
    for dx in (1, 0, -1):
        for dy in (1, 0, -1):
            if dx or dy:
                pl.semaphore_signal(
                    barrier, inc=1, device_id=near(dx, dy), device_id_type=MESH
                )
    greeted = 8 + reduction.greet(barrier)
    for c in gets[1:]:
        c.wait()
    tall(w_in_t[...], w1, bias_columns(b_in[...]))
    zero = jnp.zeros((DEPTH - ROWS, GROUPS * LANES), BF)
    for ref in (feat0, feat1, qa, qb):
        ref[ROWS:, :] = zero
    reduction.pay[...] = jnp.zeros((PLANE, 2, UNITS), F32)
    get_pops.wait()
    gets[0].wait()
    get_cot.wait()

    def lanes_of(p, s, h=None):
        first = (2 * p + s) * LANES
        return pl.ds(first, LANES) if h is None else pl.ds(first + h * HALF, HALF)

    def rows_of(s):
        return pl.ds(8 * s, 8)

    halves = [pl.ds(h * HALF, HALF) for h in range(LANES // HALF)]

    def melt_of(p, s, h):
        return flags[p, rows_of(s), h].astype(F32)

    def front(read, p, s, feat, mom_ref, rest):
        for k, h in enumerate(halves):
            f = [read(i, h) for i in range(Q)]
            rho, mom = moments(f)
            for d in range(3):
                mom_ref[2 * p + s, d, :, h] = mom[d]
            eq = equilibrium(rho, mom)
            store_features(
                feat, lanes_of(p, s, k), [f[i] * INV_W[i] - eq[i] for i in range(Q)] + [one]
            )
            if rest is not None:
                rest(h, f, rho, eq)

    def start_a(p, s):
        g = 2 * p + s

        def rest(h, f, rho, eq):
            melt = melt_of(p, s, h) > 0.5
            excess = rho - 1.0
            for i in range(Q):
                val = -0.25 * f[i] + (1.25 * W[i]) * eq[i]
                cz = VELOCITY[i][2]
                if cz:
                    val = val + (0.15 * W[i] * cz) * excess
                post[g, i, :, h] = jnp.where(melt, val, f[OPPOSITE[i]])

        front(lambda i, h: pops[p, i, rows_of(s), h], p, s, feat0, mom0, rest)

    def net_a(p, s):
        lanes = lanes_of(p, s)
        for c in range(0, HID, CHUNK):
            block = pl.ds(c, CHUNK)
            t = jnp.tanh(dot(w1[block, :], feat0[:, lanes]))
            t0[block, lanes] = t
            hid0[block, lanes] = t.astype(BF)

    def end_a(p, s):
        g = 2 * p + s
        learned = dot(w2[...], hid0[:, lanes_of(p, s)])
        melt = melt_of(p, s, slice(None)) > 0.5
        for i in range(Q):
            ex_p.put(i, p, s, post[g, i] + jnp.where(melt, learned[8 * i : 8 * i + 8, :], 0.0))

    def pair_a(s):
        for stage in (start_a, net_a, end_a):
            for p in range(2):
                stage(p, s)

    copies_c, copies_p, copies_d = [], [], []
    flat(w_out[...], w2)
    for p in range(2):
        for i in range(Q):
            wide = cot[p, i].astype(F32)
            for s in range(2):
                ex_c.put(OPPOSITE[i], p, s, wide[8 * s : 8 * s + 8, :])
    one = jnp.ones((8, HALF), F32)
    nil = jnp.zeros((8, HALF), F32)
    pair_a(1)
    pl.semaphore_wait(barrier, greeted)
    copies_c += ex_c.send_half(1, near)
    copies_c += ex_c.send_half(0, near)
    copies_p += ex_p.send_half(1, near)
    pair_a(0)
    copies_p += ex_p.send_half(0, near)
    reduction.tell(0)

    tall(w_out[...], w2t)
    flat(w_in_t[...], w1t)
    tot_ref[...] = jnp.zeros((2, ROWS, UNITS), F32)
    for c in copies_c:
        c.wait()

    def take(ex, p, s, q):
        for k, h in enumerate(halves):
            melt = melt_of(p, s, h)
            m = []
            for i in range(Q):
                val = ex.get(OPPOSITE[i], p, s, h)
                grad[2 * p + s, i, :, h] = val
                m.append(val * melt)
            store_features(q, lanes_of(p, s, k), m + [nil])

    for p in range(2):
        for s in range(2):
            take(ex_c, p, s, qb)
            lanes = lanes_of(p, s)
            for c in range(0, HID, CHUNK):
                block = pl.ds(c, CHUNK)
                gh[block, lanes] = dot(w2t[block, :], qb[:, lanes])

    @pl.loop(0, HID // 32)
    def _(k):
        block = pl.ds(pl.multiple_of(32 * k, 32), 32)
        t = t0[block, :]
        t0[block, :] = 1.0 - t * t

    reduction.hear(0)
    reduction.tell(1)
    for c in copies_p:
        c.wait()

    def back(p, s, mom_ref, r, put):
        g = 2 * p + s
        prod = dot(w1t[...], r[:, lanes_of(p, s)])
        for k, h in enumerate(halves):
            melt = melt_of(p, s, h)
            mom = [mom_ref[g, d, :, h] for d in range(3)]
            pr = [prod[8 * i : 8 * i + 8, HALF * k : HALF * (k + 1)] for i in range(Q)]
            m = [grad[g, i, :, h] * melt for i in range(Q)]
            wd = [(1.25 * W[i]) * m[i] - pr[i] for i in range(Q)]
            total = wd[0]
            lift = None
            dj = [None, None, None]
            for a, b in PAIRS:
                both = wd[a] + wd[b]
                total = total + both
                cz = VELOCITY[a][2]
                if cz:
                    term = (0.15 * W[a] * cz) * (m[a] - m[b])
                    lift = term if lift is None else lift + term
                slope = 3.0 * (wd[a] - wd[b]) + 9.0 * along(a, mom) * both
                for d in range(3):
                    c = VELOCITY[a][d]
                    if c == 0:
                        continue
                    if dj[d] is None:
                        dj[d] = slope if c == 1 else -slope
                    else:
                        dj[d] = dj[d] + slope if c == 1 else dj[d] - slope
            drho = total + lift
            dj = [dj[d] - 3.0 * mom[d] * total for d in range(3)]
            put(h, 0, (-0.25) * m[0] + INV_W[0] * pr[0] + drho + (grad[g, 0, :, h] - m[0]))
            for a, b in PAIRS:
                turn = along(a, dj)
                for i, o, base in ((a, b, drho + turn), (b, a, drho - turn)):
                    val = (-0.25) * m[i] + INV_W[i] * pr[i] + base
                    put(h, i, val + (grad[g, o, :, h] - m[o]))

    def start_b(p, s):
        front(lambda i, h: ex_p.get(i, p, s, h), p, s, feat1, mom1, None)

    def net_b(p, s):
        lanes = lanes_of(p, s)
        for c in range(0, HID, CHUNK):
            block = pl.ds(c, CHUNK)
            t = jnp.tanh(dot(w1[block, :], feat1[:, lanes]))
            hid1[block, lanes] = t.astype(BF)
            rb[block, lanes] = (gh[block, lanes] * (1.0 - t * t)).astype(BF)

    def end_b(p, s):
        g = 2 * p + s

        def put(h, i, val):
            if VELOCITY[i][2]:
                post[g, i, :, h] = val
            else:
                ex_d.put(OPPOSITE[i], p, s, val, h)

        back(p, s, mom1, rb, put)
        for i in range(Q):
            if VELOCITY[i][2]:
                ex_d.put(OPPOSITE[i], p, s, post[g, i])

    for s in (1, 0):
        for stage in (start_b, net_b, end_b):
            for p in range(2):
                stage(p, s)
        copies_d += ex_d.send_half(s, near)

    sub = iota((ROWS, UNITS), 0) % 8

    reduction.hear(1)
    reduction.tell(2)

    @pl.loop(0, HID // 256)
    def _(c):
        block = pl.ds(pl.multiple_of(256 * c, 256), 256)
        for k, (left, right) in enumerate(((qb, hid1), (feat1, rb))):
            acc = dot(left[:ROWS, :], right[block, :], NT)
            tot_ref[k] += jnp.where(sub == 2 * c, acc[:, :UNITS], 0.0) + jnp.where(
                sub == 2 * c + 1, acc[:, UNITS:], 0.0
            )

    reduction.hear(2)
    reduction.tell(3)
    for c in copies_d:
        c.wait()
    for p in range(2):
        for s in range(2):
            take(ex_d, p, s, qa)
            lanes = lanes_of(p, s)
            for c in range(0, HID, CHUNK):
                block = pl.ds(c, CHUNK)
                ra[block, lanes] = (dot(w2t[block, :], qa[:, lanes]) * t0[block, lanes]).astype(BF)

    for k, (left, right) in enumerate(((qa, hid0), (feat0, ra))):
        tot = tot_ref[k]
        for c in range(HID // 256):
            acc = dot(left[:ROWS, :], right[pl.ds(256 * c, 256), :], NT)
            for y in range(2):
                tot = tot + jnp.where(sub == 2 * c + y, acc[:, UNITS * y : UNITS * (y + 1)], 0.0)
        tot = jnp.sum(tot.reshape(20, 8, UNITS), axis=1)
        for j in range(10):
            reduction.pay[10 * (1 - k) + j] = tot[2 * j : 2 * j + 2, :]
    reduction.hear(3)
    reduction.scatter()

    for p in range(2):
        for s in range(2):

            def put(h, i, val):
                post[2 * p + s, i, :, h] = val

            back(p, s, mom0, ra, put)
        for i in range(Q):
            out[p, i] = jnp.concatenate([post[2 * p, i], post[2 * p + 1, i]], axis=0).astype(BF)
    reduction.finish()


def finish_kernel(d0, ag, d0_ref, gin_ref, gb_ref, gout_ref, gin, gb, gout, sem):
    write = pltpu.make_async_copy(d0, d0_ref, sem.at[0])
    write.start()

    def normalized(rows):
        total = jnp.concatenate(rows, axis=0)
        scale = jnp.sum(total * total) / (total.shape[0] * UNITS) + 1e-06
        return total / jnp.sqrt(scale)

    row = [ag[k // 2, k % 2 : k % 2 + 1, :] for k in range(2 * 20)]
    gin[...] = normalized(row[:Q])
    gb[...] = normalized(row[Q : Q + 1])
    gout[...] = normalized(row[Q + 1 : 2 * Q + 1])
    small = [
        pltpu.make_async_copy(src, dst, sem.at[1 + k])
        for k, (src, dst) in enumerate(((gin, gin_ref), (gb, gb_ref), (gout, gout_ref)))
    ]
    for c in small:
        c.start()
    for c in small:
        c.wait()
    write.wait()


def local_step(populations, cotangent, flags, w_in, b_in, w_out):
    vmem = pl.BlockSpec(memory_space=pltpu.VMEM)
    hbm = pl.BlockSpec(memory_space=pltpu.HBM)
    cells = GROUPS * LANES
    d0, ag = pl.pallas_call(
        kernel,
        out_shape=(
            pltpu.VMEM((2, Q, 16, LANES), BF),
            pltpu.VMEM((PLANE, 2, UNITS), F32),
        ),
        in_specs=[hbm] * 6,
        out_specs=(vmem, vmem),
        scratch_shapes=RED_SCRATCH
        + EX_SCRATCH * 3
        + [
            pltpu.VMEM((HID, DEPTH), BF),
            pltpu.VMEM((ROWS, HID), BF),
            pltpu.VMEM((ROWS, HID), BF),
            pltpu.VMEM((HID, DEPTH), BF),
            pltpu.VMEM((DEPTH, cells), BF),
            pltpu.VMEM((DEPTH, cells), BF),
            pltpu.VMEM((DEPTH, cells), BF),
            pltpu.VMEM((DEPTH, cells), BF),
            pltpu.VMEM((HID, cells), BF),
            pltpu.VMEM((HID, cells), BF),
            pltpu.VMEM((HID, cells), BF),
            pltpu.VMEM((HID, cells), BF),
            pltpu.VMEM((HID, cells), F32),
            pltpu.VMEM((HID, cells), F32),
            pltpu.VMEM((GROUPS, Q, 8, LANES), F32),
            pltpu.VMEM((GROUPS, 3, 8, LANES), F32),
            pltpu.VMEM((GROUPS, 3, 8, LANES), F32),
            pltpu.VMEM((GROUPS, Q, 8, LANES), F32),
            pltpu.VMEM((2, ROWS, UNITS), F32),
            pltpu.VMEM((2, Q, 16, LANES), F32),
            pltpu.VMEM((2, Q, 16, LANES), BF),
            pltpu.VMEM((2, 16, LANES), jnp.int32),
            pltpu.VMEM((Q, UNITS), BF),
            pltpu.VMEM((1, UNITS), F32),
            pltpu.VMEM((Q, UNITS), BF),
            pltpu.SemaphoreType.DMA((6,)),
        ],
        compiler_params=pltpu.CompilerParams(
            collective_id=0, has_side_effects=True, vmem_limit_bytes=66650112
        ),
    )(populations, cotangent, flags, w_in.T, b_in.reshape(1, UNITS), w_out)
    return pl.pallas_call(
        finish_kernel,
        out_shape=(
            jax.ShapeDtypeStruct((2, Q, 16, LANES), BF),
            jax.ShapeDtypeStruct((Q, UNITS), F32),
            jax.ShapeDtypeStruct((1, UNITS), F32),
            jax.ShapeDtypeStruct((Q, UNITS), F32),
        ),
        in_specs=[vmem] * 2,
        out_specs=(hbm,) * 4,
        scratch_shapes=[
            pltpu.VMEM((Q, UNITS), F32),
            pltpu.VMEM((1, UNITS), F32),
            pltpu.VMEM((Q, UNITS), F32),
            pltpu.SemaphoreType.DMA((4,)),
        ],
        compiler_params=pltpu.CompilerParams(vmem_limit_bytes=1024 * 1024),
    )(d0, ag)


def shards(populations, cotangent, flags, w_in, b_in, w_out):
    d0, grad_in, grad_b, grad_out = local_step(populations, cotangent, flags, w_in, b_in, w_out)
    return d0, grad_in.T, grad_b.reshape(UNITS), grad_out


def solution(mesh):
    placed = (
        P("gx", None, "gy", None),
        P("gx", None, "gy", None),
        P("gx", "gy", None),
        P(),
        P(),
        P(),
    )
    return jax.shard_map(
        shards,
        mesh=mesh,
        in_specs=placed,
        out_specs=(P("gx", None, "gy", None), P(), P(), P()),
        check_vma=False,
    )
```

```python
import functools

import jax
import jax.numpy as jnp
from jax import lax
from jax.experimental import pallas as pl
from jax.experimental.pallas import tpu as pltpu
from jax.sharding import PartitionSpec as P

VELOCITY = [
    (0, 0, 0),
    (1, 0, 0),
    (-1, 0, 0),
    (0, 1, 0),
    (0, -1, 0),
    (0, 0, 1),
    (0, 0, -1),
    (1, 1, 0),
    (-1, -1, 0),
    (1, -1, 0),
    (-1, 1, 0),
    (1, 0, 1),
    (-1, 0, -1),
    (1, 0, -1),
    (-1, 0, 1),
    (0, 1, 1),
    (0, -1, -1),
    (0, 1, -1),
    (0, -1, 1),
]
OPPOSITE = [0, 2, 1, 4, 3, 6, 5, 8, 7, 10, 9, 12, 11, 14, 13, 16, 15, 18, 17]
INV_W = [3.0] + [18.0] * 6 + [36.0] * 12
W = [1.0 / 3.0] + [1.0 / 18.0] * 6 + [1.0 / 36.0] * 12
PAIRS = [(i, i + 1) for i in range(1, 19, 2)]
Q = 19
UNITS = 128
ROWS = 160
DEPTH = 256
HID = 8 * UNITS
LANES = 256
GROUPS = 4

X_PLUS = [1, 7, 9, 11, 13]
X_MINUS = [2, 8, 10, 12, 14]
Y_PLUS = [(3, 0), (3, 1), (15, 0), (15, 1), (17, 0), (17, 1), (7, 0), (10, 1)]
Y_MINUS = [(4, 0), (4, 1), (16, 0), (16, 1), (18, 0), (18, 1), (9, 0), (8, 1)]
CORNERS = [7, 10, 8, 9]
MESH = pl.DeviceIdType.MESH
DEV_Z = 16
PLANE = 32
CHUNK = 256
HALF = 128
BF = jnp.bfloat16
F32 = jnp.float32
NT = (((1,), (1,)), ((), ()))
TN = (((0,), (0,)), ((), ()))


class Exchange:
    def __init__(self, refs):
        (self.own, self.sxp, self.sxm, self.syp, self.sym, self.rxl, self.rxr,
         self.ryl, self.ryu, self.rc, self.send, self.recv) = refs

    def put(self, j, p, s, val, lanes=slice(None)):
        cx, cy, cz = VELOCITY[j]
        if cz:
            val = pltpu.roll(val, cz % LANES, 1)
        rows = pl.ds(8 * s, 8)
        if cx == 1 and p == 1:
            self.sxp[X_PLUS.index(j), rows, lanes] = val
        elif cx == -1 and p == 0:
            self.sxm[X_MINUS.index(j), rows, lanes] = val
        else:
            self.own[p, j, rows, lanes] = val
        if cy == 1 and s == 1 and (j, p) in Y_PLUS:
            k = Y_PLUS.index((j, p))
            self.syp[k : k + 1, lanes] = val[7:8, :]
        if cy == -1 and s == 0 and (j, p) in Y_MINUS:
            k = Y_MINUS.index((j, p))
            self.sym[k : k + 1, lanes] = val[0:1, :]

    def send_half(self, s, near):
        rows = pl.ds(8 * s, 8)
        dy = 1 if s else -1
        plan = [
            (self.sxp.at[1 if s else 2, rows, :], self.rc.at[0 if s else 3], near(1, dy)),
            (self.sxm.at[2 if s else 1, rows, :], self.rc.at[1 if s else 2], near(-1, dy)),
            (self.sxp.at[:, rows, :], self.rxl.at[:, rows, :], near(1, 0)),
            (self.sxm.at[:, rows, :], self.rxr.at[:, rows, :], near(-1, 0)),
            (self.syp, self.ryl, near(0, 1)) if s else (self.sym, self.ryu, near(0, -1)),
        ]
        made = [
            pltpu.make_async_remote_copy(
                src_ref=src, dst_ref=dst, send_sem=self.send.at[5 * s + k],
                recv_sem=self.recv.at[5 * s + k], device_id=dev, device_id_type=MESH,
            )
            for k, (src, dst, dev) in enumerate(plan)
        ]
        for c in made:
            c.start()
        return made

    def get(self, j, p, s, lanes=slice(None)):
        cx, cy, cz = VELOCITY[j]
        q = p - cx
        if q == -1:
            src = self.rxl.at[X_PLUS.index(j)]
        elif q == 2:
            src = self.rxr.at[X_MINUS.index(j)]
        else:
            src = self.own.at[q, j]
        if cy == 0:
            return src[8 * s : 8 * s + 8, lanes]
        if cy == 1:
            if s == 1:
                return src[7:15, lanes]
            if q in (0, 1):
                k = Y_PLUS.index((j, q))
                halo = self.ryl[k : k + 1, lanes]
            else:
                halo = self.rc[CORNERS.index(j), 7:8, lanes]
            main = pltpu.roll(src[0:8, lanes], 1, 0)
            return jnp.where(iota(main.shape, 0) == 0, halo, main)
        if s == 0:
            return src[1:9, lanes]
        if q in (0, 1):
            k = Y_MINUS.index((j, q))
            halo = self.ryu[k : k + 1, lanes]
        else:
            halo = self.rc[CORNERS.index(j), 0:1, lanes]
        main = pltpu.roll(src[8:16, lanes], 7, 0)
        return jnp.where(iota(main.shape, 0) == 7, halo, main)


EX_SCRATCH = [
    pltpu.VMEM((2, Q, 16, LANES), F32),
    pltpu.VMEM((5, 16, LANES), F32),
    pltpu.VMEM((5, 16, LANES), F32),
    pltpu.VMEM((8, LANES), F32),
    pltpu.VMEM((8, LANES), F32),
    pltpu.VMEM((5, 16, LANES), F32),
    pltpu.VMEM((5, 16, LANES), F32),
    pltpu.VMEM((8, LANES), F32),
    pltpu.VMEM((8, LANES), F32),
    pltpu.VMEM((4, 8, LANES), F32),
    pltpu.SemaphoreType.DMA((10,)),
    pltpu.SemaphoreType.DMA((10,)),
]
N_EX = len(EX_SCRATCH)


def dot(a, b, dims=None):
    if dims is None:
        return jnp.dot(a, b, preferred_element_type=F32)
    return lax.dot_general(a, b, dims, preferred_element_type=F32)


def moments(f):
    rho = f[0]
    for a, b in PAIRS:
        rho = rho + (f[a] + f[b])
    mom = []
    for d in range(3):
        acc = None
        for a, b in PAIRS:
            c = VELOCITY[a][d]
            if c == 0:
                continue
            diff = f[a] - f[b] if c == 1 else f[b] - f[a]
            acc = diff if acc is None else acc + diff
        mom.append(acc)
    return rho, mom


def along(i, vec):
    out = None
    for d in range(3):
        c = VELOCITY[i][d]
        if c == 0:
            continue
        if out is None:
            out = vec[d] if c == 1 else -vec[d]
        else:
            out = out + vec[d] if c == 1 else out - vec[d]
    return out


def equilibrium(rho, mom):
    base = rho - 1.5 * (mom[0] * mom[0] + mom[1] * mom[1] + mom[2] * mom[2])
    eq = [base]
    for a, b in PAIRS:
        u = along(a, mom)
        even = base + 4.5 * (u * u)
        odd = 3.0 * u
        eq.append(even + odd)
        eq.append(even - odd)
    return eq


def store_features(dst, lanes, vals):
    for k in range(0, len(vals), 2):
        two = jnp.concatenate([vals[k], vals[k + 1]], axis=0)
        dst[8 * k : 8 * k + 16, lanes] = two.astype(BF)


def one_hot(hit):
    return hit.astype(F32).astype(BF)


def iota(shape, dim):
    return lax.broadcasted_iota(jnp.int32, shape, dim)


def tall(w_t, masked, extra=None):
    expand = one_hot(iota((Q, DEPTH), 0) == iota((Q, DEPTH), 1) // 8)
    wide = dot(w_t, expand, TN)
    lane = iota((UNITS, DEPTH), 1) % 8
    for y in range(8):
        val = jnp.where(lane == y, wide, 0.0)
        if extra is not None:
            val = val + extra
        masked[pl.ds(UNITS * y, UNITS), :] = val.astype(BF)


def flat(w_t, masked):
    expand = one_hot(iota((ROWS, Q), 1) == iota((ROWS, Q), 0) // 8)
    wide = dot(expand, w_t)
    sub = iota((ROWS, UNITS), 0) % 8
    for y in range(8):
        masked[:, pl.ds(UNITS * y, UNITS)] = jnp.where(sub == y, wide, 0.0).astype(BF)


def bias_columns(b_in):
    hi = b_in.astype(BF)
    rest = b_in - hi.astype(F32)
    mid = rest.astype(BF)
    low = (rest - mid.astype(F32)).astype(BF)
    row = iota((8, UNITS), 0)
    parts = jnp.where(
        row == 0, hi.astype(F32),
        jnp.where(row == 1, mid.astype(F32), jnp.where(row == 2, low.astype(F32), 0.0)),
    ).astype(BF)
    place = one_hot(iota((8, DEPTH), 1) == iota((8, DEPTH), 0) + 8 * Q)
    return dot(parts, place, TN)


class Reduction:
    def __init__(self, refs, ag, gx, gy):
        (self.pay, self.rs_in, self.z_own, self.z_in, self.ag_own, self.send, self.recv,
         self.known) = refs
        self.ag = ag
        self.z = lax.rem(gx // 2, DEV_Z)
        core, y = lax.rem(gx, 2), gx // (2 * DEV_Z)
        self.gx, self.gy, self.core, self.y = gx, gy, core, y
        self.me = y * 8 + gy * 2 + core
        cs = [core, 1 - core]
        xs = [gy] + [lax.rem(gy + k, 4) for k in range(1, 4)]
        ys = [y] + [lax.rem(y + k, 4) for k in range(1, 4)]
        self.plane, far = [], []
        for dy in range(4):
            base, mbase = ys[dy] * (2 * DEV_Z) + self.z * 2, ys[dy] * 8
            for dc in range(2):
                for dx in range(4):
                    if dx or dy or dc:
                        dev = (base + cs[dc], xs[dx])
                        far.append((-min(dx, 4 - dx) - min(dy, 4 - dy), len(far)))
                        self.plane.append((mbase + (xs[dx] * 2 + cs[dc]), dev))
        self.plane = [self.plane[k] for _, k in sorted(far)]
        line = gx - 2 * self.z
        self.line = []
        for k in sorted(range(1, DEV_Z), key=lambda k: -min(k, DEV_Z - k)):
            self.line.append((line + 2 * lax.rem(self.z + k, DEV_Z), gy))

    def greet(self, barrier):
        for dev in self.axis("z", 1) + self.axis("y", 1):
            pl.semaphore_signal(barrier, inc=1, device_id=dev, device_id_type=MESH)
        return 4

    def axis(self, name, k):
        if name == "z":
            base = self.gx - 2 * self.z
            return [
                (base + 2 * lax.rem(self.z + d, DEV_Z), self.gy) for d in (k, DEV_Z - k)
            ]
        if name == "y":
            base = self.gx - self.y * (2 * DEV_Z)
            return [
                (base + (2 * DEV_Z) * lax.rem(self.y + d, 4), self.gy) for d in (k, 4 - k)
            ]
        if name == "x":
            return [(self.gx, lax.rem(self.gy + d, 4)) for d in (k, 4 - k)]
        return [(self.gx - self.core + (1 - self.core), self.gy)]

    def tell(self, step):
        peers = self.axis("y", 1) + self.axis("x", 1) + self.axis("core", 1)
        if step < 3:
            peers = self.axis("z", 2**step) + peers
        for dev in peers:
            pl.semaphore_signal(self.known.at[step], inc=1, device_id=dev, device_id_type=MESH)

    def hear(self, step):
        pl.semaphore_wait(self.known.at[step], 7 if step < 3 else 5)

    def remote(self, src, dst, phase, dev):
        return pltpu.make_async_remote_copy(
            src_ref=src, dst_ref=dst, send_sem=self.send.at[phase], recv_sem=self.recv.at[phase],
            device_id=dev, device_id_type=MESH,
        )

    def wait(self, src, dst, phase):
        dev = self.plane[0][1]
        both = self.remote(src, dst, phase, dev)
        both.wait_send()
        both.wait_recv()

    def scatter(self):
        for k, (m, dev) in enumerate(self.plane):
            self.remote(self.pay.at[m], self.rs_in.at[k], 0, dev).start()

    def finish(self):
        self.wait(self.pay.at[0 : PLANE - 1], self.rs_in.at[:], 0)
        part = self.pay[self.me] + jnp.sum(self.rs_in[...], axis=0)
        self.z_own[...] = part
        self.z_in[self.z] = part

        for dev in self.line:
            self.remote(self.z_own.at[:], self.z_in.at[self.z], 1, dev).start()

        sized = self.z_in.at[0 : DEV_Z - 1]
        self.wait(sized, sized, 1)
        total = jnp.sum(self.z_in[...], axis=0)
        self.ag_own[...] = total
        self.ag[self.me] = total

        for _, dev in self.plane:
            self.remote(self.ag_own.at[:], self.ag.at[self.me], 2, dev).start()

        sized = self.ag.at[0 : PLANE - 1]
        self.wait(sized, sized, 2)


RED_SCRATCH = [
    pltpu.VMEM((PLANE, 2, UNITS), F32),
    pltpu.VMEM((PLANE - 1, 2, UNITS), F32),
    pltpu.VMEM((2, UNITS), F32),
    pltpu.VMEM((DEV_Z, 2, UNITS), F32),
    pltpu.VMEM((2, UNITS), F32),
    pltpu.SemaphoreType.DMA((3,)),
    pltpu.SemaphoreType.DMA((3,)),
    pltpu.SemaphoreType.REGULAR((4,)),
]
N_RED = len(RED_SCRATCH)


def kernel(pops_hbm, cot_hbm, *refs):
    small_hbm, (out, ag), scratch = refs[:4], refs[4:6], refs[6:]
    gx, gy = lax.axis_index("gx"), lax.axis_index("gy")
    (w1, w1t, w2, w2t, feat0, feat1, qa, qb, hid0, hid1, ra, rb, t0, gh, grad,
     mom0, mom1, post, tot_ref, pops, cot, flags, w_in_t, b_in, w_out, in_sem) = scratch[N_RED + 3 * N_EX :]
    get_cot = pltpu.make_async_copy(cot_hbm, cot, in_sem.at[0])
    get_pops = pltpu.make_async_copy(pops_hbm, pops, in_sem.at[1])
    gets = [
        pltpu.make_async_copy(src, dst, in_sem.at[2 + k])
        for k, (src, dst) in enumerate(zip(small_hbm, (flags, w_in_t, b_in, w_out)))
    ]
    for c in gets[1:] + [get_cot, get_pops, gets[0]]:
        c.start()
    reduction = Reduction(scratch[:N_RED], ag, gx, gy)
    ex_c, ex_p, ex_d = [
        Exchange(scratch[N_RED + k * N_EX : N_RED + (k + 1) * N_EX]) for k in range(3)
    ]
    step_x = {0: gx, 1: lax.rem(gx + 1, 128), -1: lax.rem(gx + 127, 128)}
    step_y = {0: gy, 1: lax.rem(gy + 1, 4), -1: lax.rem(gy + 3, 4)}

    def near(dx, dy):
        return (step_x[dx], step_y[dy])

    barrier = pltpu.get_barrier_semaphore()
    for dx in (1, 0, -1):
        for dy in (1, 0, -1):
            if dx or dy:
                pl.semaphore_signal(
                    barrier, inc=1, device_id=near(dx, dy), device_id_type=MESH
                )
    greeted = 8 + reduction.greet(barrier)
    for c in gets[1:]:
        c.wait()
    tall(w_in_t[...], w1, bias_columns(b_in[...]))
    zero = jnp.zeros((DEPTH - ROWS, GROUPS * LANES), BF)
    for ref in (feat0, feat1, qa, qb):
        ref[ROWS:, :] = zero
    reduction.pay[...] = jnp.zeros((PLANE, 2, UNITS), F32)
    get_pops.wait()
    gets[0].wait()
    get_cot.wait()

    def lanes_of(p, s, h=None):
        first = (2 * p + s) * LANES
        return pl.ds(first, LANES) if h is None else pl.ds(first + h * HALF, HALF)

    def rows_of(s):
        return pl.ds(8 * s, 8)

    halves = [pl.ds(h * HALF, HALF) for h in range(LANES // HALF)]

    def melt_of(p, s, h):
        return flags[p, rows_of(s), h].astype(F32)

    def front(read, p, s, feat, mom_ref, rest):
        for k, h in enumerate(halves):
            f = [read(i, h) for i in range(Q)]
            rho, mom = moments(f)
            for d in range(3):
                mom_ref[2 * p + s, d, :, h] = mom[d]
            eq = equilibrium(rho, mom)
            store_features(
                feat, lanes_of(p, s, k), [f[i] * INV_W[i] - eq[i] for i in range(Q)] + [one]
            )
            if rest is not None:
                rest(h, f, rho, eq)

    def start_a(p, s):
        g = 2 * p + s

        def rest(h, f, rho, eq):
            melt = melt_of(p, s, h) > 0.5
            excess = rho - 1.0
            for i in range(Q):
                val = -0.25 * f[i] + (1.25 * W[i]) * eq[i]
                cz = VELOCITY[i][2]
                if cz:
                    val = val + (0.15 * W[i] * cz) * excess
                post[g, i, :, h] = jnp.where(melt, val, f[OPPOSITE[i]])

        front(lambda i, h: pops[p, i, rows_of(s), h], p, s, feat0, mom0, rest)

    def net_a(p, s):
        lanes = lanes_of(p, s)
        for c in range(0, HID, CHUNK):
            block = pl.ds(c, CHUNK)
            t = jnp.tanh(dot(w1[block, :], feat0[:, lanes]))
            t0[block, lanes] = t
            hid0[block, lanes] = t.astype(BF)

    def end_a(p, s):
        g = 2 * p + s
        learned = dot(w2[...], hid0[:, lanes_of(p, s)])
        melt = melt_of(p, s, slice(None)) > 0.5
        for i in range(Q):
            ex_p.put(i, p, s, post[g, i] + jnp.where(melt, learned[8 * i : 8 * i + 8, :], 0.0))

    def pair_a(s):
        for stage in (start_a, net_a, end_a):
            for p in range(2):
                stage(p, s)

    copies_c, copies_p, copies_d = [], [], []
    flat(w_out[...], w2)
    for p in range(2):
        for i in range(Q):
            wide = cot[p, i].astype(F32)
            for s in range(2):
                ex_c.put(OPPOSITE[i], p, s, wide[8 * s : 8 * s + 8, :])
    one = jnp.ones((8, HALF), F32)
    nil = jnp.zeros((8, HALF), F32)
    for p in range(2):
        start_a(p, 1)
    for p in range(2):
        net_a(p, 1)
    pl.semaphore_wait(barrier, greeted)
    copies_c += ex_c.send_half(1, near)
    copies_c += ex_c.send_half(0, near)
    for p in range(2):
        end_a(p, 1)
    copies_p += ex_p.send_half(1, near)
    pair_a(0)
    copies_p += ex_p.send_half(0, near)
    reduction.tell(0)

    tall(w_out[...], w2t)
    flat(w_in_t[...], w1t)
    tot_ref[...] = jnp.zeros((2, ROWS, UNITS), F32)
    for c in copies_c:
        c.wait()

    def take(ex, p, s, q):
        for k, h in enumerate(halves):
            melt = melt_of(p, s, h)
            m = []
            for i in range(Q):
                val = ex.get(OPPOSITE[i], p, s, h)
                grad[2 * p + s, i, :, h] = val
                m.append(val * melt)
            store_features(q, lanes_of(p, s, k), m + [nil])

    for p in range(2):
        for s in range(2):
            take(ex_c, p, s, qb)
            lanes = lanes_of(p, s)
            for c in range(0, HID, CHUNK):
                block = pl.ds(c, CHUNK)
                gh[block, lanes] = dot(w2t[block, :], qb[:, lanes])

    @pl.loop(0, HID // 32)
    def _(k):
        block = pl.ds(pl.multiple_of(32 * k, 32), 32)
        t = t0[block, :]
        t0[block, :] = 1.0 - t * t

    reduction.hear(0)
    reduction.tell(1)
    for c in copies_p:
        c.wait()

    def back(p, s, mom_ref, r, put):
        g = 2 * p + s
        prod = dot(w1t[...], r[:, lanes_of(p, s)])
        for k, h in enumerate(halves):
            melt = melt_of(p, s, h)
            mom = [mom_ref[g, d, :, h] for d in range(3)]
            pr = [prod[8 * i : 8 * i + 8, HALF * k : HALF * (k + 1)] for i in range(Q)]
            m = [grad[g, i, :, h] * melt for i in range(Q)]
            wd = [(1.25 * W[i]) * m[i] - pr[i] for i in range(Q)]
            total = wd[0]
            lift = None
            dj = [None, None, None]
            for a, b in PAIRS:
                both = wd[a] + wd[b]
                total = total + both
                cz = VELOCITY[a][2]
                if cz:
                    term = (0.15 * W[a] * cz) * (m[a] - m[b])
                    lift = term if lift is None else lift + term
                slope = 3.0 * (wd[a] - wd[b]) + 9.0 * along(a, mom) * both
                for d in range(3):
                    c = VELOCITY[a][d]
                    if c == 0:
                        continue
                    if dj[d] is None:
                        dj[d] = slope if c == 1 else -slope
                    else:
                        dj[d] = dj[d] + slope if c == 1 else dj[d] - slope
            drho = total + lift
            dj = [dj[d] - 3.0 * mom[d] * total for d in range(3)]
            put(h, 0, (-0.25) * m[0] + INV_W[0] * pr[0] + drho + (grad[g, 0, :, h] - m[0]))
            for a, b in PAIRS:
                turn = along(a, dj)
                for i, o, base in ((a, b, drho + turn), (b, a, drho - turn)):
                    val = (-0.25) * m[i] + INV_W[i] * pr[i] + base
                    put(h, i, val + (grad[g, o, :, h] - m[o]))

    def start_b(p, s):
        front(lambda i, h: ex_p.get(i, p, s, h), p, s, feat1, mom1, None)

    def net_b(p, s):
        lanes = lanes_of(p, s)
        for c in range(0, HID, CHUNK):
            block = pl.ds(c, CHUNK)
            t = jnp.tanh(dot(w1[block, :], feat1[:, lanes]))
            hid1[block, lanes] = t.astype(BF)
            rb[block, lanes] = (gh[block, lanes] * (1.0 - t * t)).astype(BF)

    def end_b(p, s):
        g = 2 * p + s

        def put(h, i, val):
            if VELOCITY[i][2]:
                post[g, i, :, h] = val
            else:
                ex_d.put(OPPOSITE[i], p, s, val, h)

        back(p, s, mom1, rb, put)
        for i in range(Q):
            if VELOCITY[i][2]:
                ex_d.put(OPPOSITE[i], p, s, post[g, i])

    for s in (1, 0):
        for stage in (start_b, net_b, end_b):
            for p in range(2):
                stage(p, s)
        copies_d += ex_d.send_half(s, near)

    sub = iota((ROWS, UNITS), 0) % 8

    reduction.hear(1)
    reduction.tell(2)

    @pl.loop(0, HID // 256)
    def _(c):
        block = pl.ds(pl.multiple_of(256 * c, 256), 256)
        for k, (left, right) in enumerate(((qb, hid1), (feat1, rb))):
            acc = dot(left[:ROWS, :], right[block, :], NT)
            tot_ref[k] += jnp.where(sub == 2 * c, acc[:, :UNITS], 0.0) + jnp.where(
                sub == 2 * c + 1, acc[:, UNITS:], 0.0
            )

    reduction.hear(2)
    reduction.tell(3)
    corner_pair = {(0, 0): 8, (1, 0): 8, (1, 1): 6, (0, 1): 10}

    def take_pairs(p, s, late):
        for k, h in enumerate(halves):
            melt = melt_of(p, s, h)
            for i in range(0, Q, 2):
                if (corner_pair[p, s] == i) != late:
                    continue
                both = []
                for n in (i, i + 1):
                    if n < Q:
                        val = ex_d.get(OPPOSITE[n], p, s, h)
                        grad[2 * p + s, n, :, h] = val
                        both.append(val * melt)
                    else:
                        both.append(nil)
                two = jnp.concatenate(both, axis=0)
                qa[8 * i : 8 * i + 16, lanes_of(p, s, k)] = two.astype(BF)

    for half in (copies_d[:5], copies_d[5:]):
        for c in half[2:]:
            c.wait()
    for p in range(2):
        for s in range(2):
            take_pairs(p, s, False)
    for half in (copies_d[:5], copies_d[5:]):
        for c in half[:2]:
            c.wait()
    for p in range(2):
        for s in range(2):
            take_pairs(p, s, True)
            lanes = lanes_of(p, s)
            for c in range(0, HID, CHUNK):
                block = pl.ds(c, CHUNK)
                ra[block, lanes] = (dot(w2t[block, :], qa[:, lanes]) * t0[block, lanes]).astype(BF)

    for k, (left, right) in enumerate(((qa, hid0), (feat0, ra))):
        tot = tot_ref[k]
        for c in range(HID // 256):
            acc = dot(left[:ROWS, :], right[pl.ds(256 * c, 256), :], NT)
            for y in range(2):
                tot = tot + jnp.where(sub == 2 * c + y, acc[:, UNITS * y : UNITS * (y + 1)], 0.0)
        tot = jnp.sum(tot.reshape(20, 8, UNITS), axis=1)
        for j in range(10):
            reduction.pay[10 * (1 - k) + j] = tot[2 * j : 2 * j + 2, :]
    reduction.hear(3)
    reduction.scatter()

    for p in range(2):
        for s in range(2):

            def put(h, i, val):
                post[2 * p + s, i, :, h] = val

            back(p, s, mom0, ra, put)
        for i in range(Q):
            out[p, i] = jnp.concatenate([post[2 * p, i], post[2 * p + 1, i]], axis=0).astype(BF)
    reduction.finish()


def finish_kernel(d0, ag, d0_ref, gin_ref, gb_ref, gout_ref, gin, gb, gout, sem):
    write = pltpu.make_async_copy(d0, d0_ref, sem.at[0])
    write.start()

    def normalized(rows):
        total = jnp.concatenate(rows, axis=0)
        scale = jnp.sum(total * total) / (total.shape[0] * UNITS) + 1e-06
        return total / jnp.sqrt(scale)

    row = [ag[k // 2, k % 2 : k % 2 + 1, :] for k in range(2 * 20)]
    gin[...] = normalized(row[:Q])
    gb[...] = normalized(row[Q : Q + 1])
    gout[...] = normalized(row[Q + 1 : 2 * Q + 1])
    small = [
        pltpu.make_async_copy(src, dst, sem.at[1 + k])
        for k, (src, dst) in enumerate(((gin, gin_ref), (gb, gb_ref), (gout, gout_ref)))
    ]
    for c in small:
        c.start()
    for c in small:
        c.wait()
    write.wait()


def local_step(populations, cotangent, flags, w_in, b_in, w_out):
    vmem = pl.BlockSpec(memory_space=pltpu.VMEM)
    hbm = pl.BlockSpec(memory_space=pltpu.HBM)
    cells = GROUPS * LANES
    d0, ag = pl.pallas_call(
        kernel,
        out_shape=(
            pltpu.VMEM((2, Q, 16, LANES), BF),
            pltpu.VMEM((PLANE, 2, UNITS), F32),
        ),
        in_specs=[hbm] * 6,
        out_specs=(vmem, vmem),
        scratch_shapes=RED_SCRATCH
        + EX_SCRATCH * 3
        + [
            pltpu.VMEM((HID, DEPTH), BF),
            pltpu.VMEM((ROWS, HID), BF),
            pltpu.VMEM((ROWS, HID), BF),
            pltpu.VMEM((HID, DEPTH), BF),
            pltpu.VMEM((DEPTH, cells), BF),
            pltpu.VMEM((DEPTH, cells), BF),
            pltpu.VMEM((DEPTH, cells), BF),
            pltpu.VMEM((DEPTH, cells), BF),
            pltpu.VMEM((HID, cells), BF),
            pltpu.VMEM((HID, cells), BF),
            pltpu.VMEM((HID, cells), BF),
            pltpu.VMEM((HID, cells), BF),
            pltpu.VMEM((HID, cells), F32),
            pltpu.VMEM((HID, cells), F32),
            pltpu.VMEM((GROUPS, Q, 8, LANES), F32),
            pltpu.VMEM((GROUPS, 3, 8, LANES), F32),
            pltpu.VMEM((GROUPS, 3, 8, LANES), F32),
            pltpu.VMEM((GROUPS, Q, 8, LANES), F32),
            pltpu.VMEM((2, ROWS, UNITS), F32),
            pltpu.VMEM((2, Q, 16, LANES), F32),
            pltpu.VMEM((2, Q, 16, LANES), BF),
            pltpu.VMEM((2, 16, LANES), jnp.int32),
            pltpu.VMEM((Q, UNITS), BF),
            pltpu.VMEM((1, UNITS), F32),
            pltpu.VMEM((Q, UNITS), BF),
            pltpu.SemaphoreType.DMA((6,)),
        ],
        compiler_params=pltpu.CompilerParams(
            collective_id=0, has_side_effects=True, vmem_limit_bytes=66650112
        ),
    )(populations, cotangent, flags, w_in.T, b_in.reshape(1, UNITS), w_out)
    return pl.pallas_call(
        finish_kernel,
        out_shape=(
            jax.ShapeDtypeStruct((2, Q, 16, LANES), BF),
            jax.ShapeDtypeStruct((Q, UNITS), F32),
            jax.ShapeDtypeStruct((1, UNITS), F32),
            jax.ShapeDtypeStruct((Q, UNITS), F32),
        ),
        in_specs=[vmem] * 2,
        out_specs=(hbm,) * 4,
        scratch_shapes=[
            pltpu.VMEM((Q, UNITS), F32),
            pltpu.VMEM((1, UNITS), F32),
            pltpu.VMEM((Q, UNITS), F32),
            pltpu.SemaphoreType.DMA((4,)),
        ],
        compiler_params=pltpu.CompilerParams(vmem_limit_bytes=1024 * 1024),
    )(d0, ag)


def shards(populations, cotangent, flags, w_in, b_in, w_out):
    d0, grad_in, grad_b, grad_out = local_step(populations, cotangent, flags, w_in, b_in, w_out)
    return d0, grad_in.T, grad_b.reshape(UNITS), grad_out


def solution(mesh):
    placed = (
        P("gx", None, "gy", None),
        P("gx", None, "gy", None),
        P("gx", "gy", None),
        P(),
        P(),
        P(),
    )
    return jax.shard_map(
        shards,
        mesh=mesh,
        in_specs=placed,
        out_specs=(P("gx", None, "gy", None), P(), P(), P()),
        check_vma=False,
    )
```

```python
import functools

import jax
import jax.numpy as jnp
from jax import lax
from jax.experimental import pallas as pl
from jax.experimental.pallas import tpu as pltpu
from jax.sharding import PartitionSpec as P

VELOCITY = [
    (0, 0, 0),
    (1, 0, 0),
    (-1, 0, 0),
    (0, 1, 0),
    (0, -1, 0),
    (0, 0, 1),
    (0, 0, -1),
    (1, 1, 0),
    (-1, -1, 0),
    (1, -1, 0),
    (-1, 1, 0),
    (1, 0, 1),
    (-1, 0, -1),
    (1, 0, -1),
    (-1, 0, 1),
    (0, 1, 1),
    (0, -1, -1),
    (0, 1, -1),
    (0, -1, 1),
]
OPPOSITE = [0, 2, 1, 4, 3, 6, 5, 8, 7, 10, 9, 12, 11, 14, 13, 16, 15, 18, 17]
INV_W = [3.0] + [18.0] * 6 + [36.0] * 12
W = [1.0 / 3.0] + [1.0 / 18.0] * 6 + [1.0 / 36.0] * 12
PAIRS = [(i, i + 1) for i in range(1, 19, 2)]
Q = 19
UNITS = 128
ROWS = 160
DEPTH = 256
HID = 8 * UNITS
LANES = 256
GROUPS = 4

X_PLUS = [1, 7, 9, 11, 13]
X_MINUS = [2, 8, 10, 12, 14]
Y_PLUS = [(3, 0), (3, 1), (15, 0), (15, 1), (17, 0), (17, 1), (7, 0), (10, 1)]
Y_MINUS = [(4, 0), (4, 1), (16, 0), (16, 1), (18, 0), (18, 1), (9, 0), (8, 1)]
CORNERS = [7, 10, 8, 9]
MESH = pl.DeviceIdType.MESH
DEV_Z = 16
PLANE = 32
CHUNK = 256
HALF = 128
BF = jnp.bfloat16
F32 = jnp.float32
NT = (((1,), (1,)), ((), ()))
TN = (((0,), (0,)), ((), ()))


class Exchange:
    def __init__(self, refs, span):
        self.span = span
        (self.own, self.sxp, self.sxm, self.syp, self.sym, self.rxl, self.rxr,
         self.ryl, self.ryu, self.rc, self.send, self.recv) = refs

    def put(self, j, p, s, val, lanes=slice(None)):
        cx, cy, cz = VELOCITY[j]
        if cz:
            val = pltpu.roll(val, cz % LANES, 1)
        rows = pl.ds(8 * s, 8)
        if cx == 1 and p == 1:
            self.sxp[X_PLUS.index(j), rows, lanes] = val
        elif cx == -1 and p == 0:
            self.sxm[X_MINUS.index(j), rows, lanes] = val
        else:
            self.own[p, j, rows, lanes] = val
        if cy == 1 and s == 1 and (j, p) in Y_PLUS:
            k = Y_PLUS.index((j, p))
            self.syp[k : k + 1, lanes] = val[7:8, :]
        if cy == -1 and s == 0 and (j, p) in Y_MINUS:
            k = Y_MINUS.index((j, p))
            self.sym[k : k + 1, lanes] = val[0:1, :]

    def send_half(self, s, near):
        rows = pl.ds(8 * s, 8)
        dy = 1 if s else -1
        plan = [
            (self.sxp.at[1 if s else 2, rows, :], self.rc.at[0 if s else 3], near(1, dy)),
            (self.sxm.at[2 if s else 1, rows, :], self.rc.at[1 if s else 2], near(-1, dy)),
            (self.sxp.at[:, rows, :], self.rxl.at[:, rows, :], near(1, 0)),
            (self.sxm.at[:, rows, :], self.rxr.at[:, rows, :], near(-1, 0)),
            (self.syp, self.ryl, near(0, 1)) if s else (self.sym, self.ryu, near(0, -1)),
        ]
        made = [
            pltpu.make_async_remote_copy(
                src_ref=src, dst_ref=dst, send_sem=self.send,
                recv_sem=self.recv, device_id=dev, device_id_type=MESH,
            )
            for k, (src, dst, dev) in enumerate(plan)
        ]
        for c in made:
            c.start()
        return made

    def finish(self, near):
        every = pltpu.make_async_remote_copy(
            src_ref=self.span, dst_ref=self.span, send_sem=self.send, recv_sem=self.recv,
            device_id=near(1, 0), device_id_type=MESH,
        )
        every.wait_send()
        every.wait_recv()

    def get(self, j, p, s, lanes=slice(None)):
        cx, cy, cz = VELOCITY[j]
        q = p - cx
        if q == -1:
            src = self.rxl.at[X_PLUS.index(j)]
        elif q == 2:
            src = self.rxr.at[X_MINUS.index(j)]
        else:
            src = self.own.at[q, j]
        if cy == 0:
            return src[8 * s : 8 * s + 8, lanes]
        if cy == 1:
            if s == 1:
                return src[7:15, lanes]
            if q in (0, 1):
                k = Y_PLUS.index((j, q))
                halo = self.ryl[k : k + 1, lanes]
            else:
                halo = self.rc[CORNERS.index(j), 7:8, lanes]
            main = pltpu.roll(src[0:8, lanes], 1, 0)
            return jnp.where(iota(main.shape, 0) == 0, halo, main)
        if s == 0:
            return src[1:9, lanes]
        if q in (0, 1):
            k = Y_MINUS.index((j, q))
            halo = self.ryu[k : k + 1, lanes]
        else:
            halo = self.rc[CORNERS.index(j), 0:1, lanes]
        main = pltpu.roll(src[8:16, lanes], 7, 0)
        return jnp.where(iota(main.shape, 0) == 7, halo, main)


EX_SCRATCH = [
    pltpu.VMEM((2, Q, 16, LANES), F32),
    pltpu.VMEM((5, 16, LANES), F32),
    pltpu.VMEM((5, 16, LANES), F32),
    pltpu.VMEM((8, LANES), F32),
    pltpu.VMEM((8, LANES), F32),
    pltpu.VMEM((5, 16, LANES), F32),
    pltpu.VMEM((5, 16, LANES), F32),
    pltpu.VMEM((8, LANES), F32),
    pltpu.VMEM((8, LANES), F32),
    pltpu.VMEM((4, 8, LANES), F32),
    pltpu.SemaphoreType.DMA,
    pltpu.SemaphoreType.DMA,
]
N_EX = len(EX_SCRATCH)


def dot(a, b, dims=None):
    if dims is None:
        return jnp.dot(a, b, preferred_element_type=F32)
    return lax.dot_general(a, b, dims, preferred_element_type=F32)


def moments(f):
    rho = f[0]
    for a, b in PAIRS:
        rho = rho + (f[a] + f[b])
    mom = []
    for d in range(3):
        acc = None
        for a, b in PAIRS:
            c = VELOCITY[a][d]
            if c == 0:
                continue
            diff = f[a] - f[b] if c == 1 else f[b] - f[a]
            acc = diff if acc is None else acc + diff
        mom.append(acc)
    return rho, mom


def along(i, vec):
    out = None
    for d in range(3):
        c = VELOCITY[i][d]
        if c == 0:
            continue
        if out is None:
            out = vec[d] if c == 1 else -vec[d]
        else:
            out = out + vec[d] if c == 1 else out - vec[d]
    return out


def equilibrium(rho, mom):
    base = rho - 1.5 * (mom[0] * mom[0] + mom[1] * mom[1] + mom[2] * mom[2])
    eq = [base]
    for a, b in PAIRS:
        u = along(a, mom)
        even = base + 4.5 * (u * u)
        odd = 3.0 * u
        eq.append(even + odd)
        eq.append(even - odd)
    return eq


def store_features(dst, lanes, vals):
    for k in range(0, len(vals), 2):
        two = jnp.concatenate([vals[k], vals[k + 1]], axis=0)
        dst[8 * k : 8 * k + 16, lanes] = two.astype(BF)


def one_hot(hit):
    return hit.astype(F32).astype(BF)


def iota(shape, dim):
    return lax.broadcasted_iota(jnp.int32, shape, dim)


def tall(w_t, masked, extra=None):
    expand = one_hot(iota((Q, DEPTH), 0) == iota((Q, DEPTH), 1) // 8)
    wide = dot(w_t, expand, TN)
    lane = iota((UNITS, DEPTH), 1) % 8
    for y in range(8):
        val = jnp.where(lane == y, wide, 0.0)
        if extra is not None:
            val = val + extra
        masked[pl.ds(UNITS * y, UNITS), :] = val.astype(BF)


def flat(w_t, masked):
    expand = one_hot(iota((ROWS, Q), 1) == iota((ROWS, Q), 0) // 8)
    wide = dot(expand, w_t)
    sub = iota((ROWS, UNITS), 0) % 8
    for y in range(8):
        masked[:, pl.ds(UNITS * y, UNITS)] = jnp.where(sub == y, wide, 0.0).astype(BF)


def bias_columns(b_in):
    hi = b_in.astype(BF)
    rest = b_in - hi.astype(F32)
    mid = rest.astype(BF)
    low = (rest - mid.astype(F32)).astype(BF)
    row = iota((8, UNITS), 0)
    parts = jnp.where(
        row == 0, hi.astype(F32),
        jnp.where(row == 1, mid.astype(F32), jnp.where(row == 2, low.astype(F32), 0.0)),
    ).astype(BF)
    place = one_hot(iota((8, DEPTH), 1) == iota((8, DEPTH), 0) + 8 * Q)
    return dot(parts, place, TN)


class Reduction:
    def __init__(self, refs, ag, gx, gy):
        (self.pay, self.rs_in, self.z_own, self.z_in, self.ag_own, self.send, self.recv,
         self.known) = refs
        self.ag = ag
        self.z = lax.rem(gx // 2, DEV_Z)
        core, y = lax.rem(gx, 2), gx // (2 * DEV_Z)
        self.gx, self.gy, self.core, self.y = gx, gy, core, y
        self.me = y * 8 + gy * 2 + core
        cs = [core, 1 - core]
        xs = [gy] + [lax.rem(gy + k, 4) for k in range(1, 4)]
        ys = [y] + [lax.rem(y + k, 4) for k in range(1, 4)]
        self.plane, far = [], []
        for dy in range(4):
            base, mbase = ys[dy] * (2 * DEV_Z) + self.z * 2, ys[dy] * 8
            for dc in range(2):
                for dx in range(4):
                    if dx or dy or dc:
                        dev = (base + cs[dc], xs[dx])
                        far.append((-min(dx, 4 - dx) - min(dy, 4 - dy), len(far)))
                        self.plane.append((mbase + (xs[dx] * 2 + cs[dc]), dev))
        self.plane = [self.plane[k] for _, k in sorted(far)]
        line = gx - 2 * self.z
        self.line = []
        for k in sorted(range(1, DEV_Z), key=lambda k: -min(k, DEV_Z - k)):
            self.line.append((line + 2 * lax.rem(self.z + k, DEV_Z), gy))

    def greet(self, barrier):
        for dev in self.axis("z", 1) + self.axis("y", 1):
            pl.semaphore_signal(barrier, inc=1, device_id=dev, device_id_type=MESH)
        return 4

    def axis(self, name, k):
        if name == "z":
            base = self.gx - 2 * self.z
            return [
                (base + 2 * lax.rem(self.z + d, DEV_Z), self.gy) for d in (k, DEV_Z - k)
            ]
        if name == "y":
            base = self.gx - self.y * (2 * DEV_Z)
            return [
                (base + (2 * DEV_Z) * lax.rem(self.y + d, 4), self.gy) for d in (k, 4 - k)
            ]
        if name == "x":
            return [(self.gx, lax.rem(self.gy + d, 4)) for d in (k, 4 - k)]
        return [(self.gx - self.core + (1 - self.core), self.gy)]

    def tell(self, step):
        peers = self.axis("y", 1) + self.axis("x", 1) + self.axis("core", 1)
        if step < 3:
            peers = self.axis("z", 2**step) + peers
        for dev in peers:
            pl.semaphore_signal(self.known.at[step], inc=1, device_id=dev, device_id_type=MESH)

    def hear(self, step):
        pl.semaphore_wait(self.known.at[step], 7 if step < 3 else 5)

    def remote(self, src, dst, phase, dev):
        return pltpu.make_async_remote_copy(
            src_ref=src, dst_ref=dst, send_sem=self.send.at[phase], recv_sem=self.recv.at[phase],
            device_id=dev, device_id_type=MESH,
        )

    def wait(self, src, dst, phase):
        dev = self.plane[0][1]
        both = self.remote(src, dst, phase, dev)
        both.wait_send()
        both.wait_recv()

    def scatter(self):
        for k, (m, dev) in enumerate(self.plane):
            self.remote(self.pay.at[m], self.rs_in.at[k], 0, dev).start()

    def finish(self):
        self.wait(self.pay.at[0 : PLANE - 1], self.rs_in.at[:], 0)
        part = self.pay[self.me] + jnp.sum(self.rs_in[...], axis=0)
        self.z_own[...] = part
        self.z_in[self.z] = part

        for dev in self.line:
            self.remote(self.z_own.at[:], self.z_in.at[self.z], 1, dev).start()

        sized = self.z_in.at[0 : DEV_Z - 1]
        self.wait(sized, sized, 1)
        total = jnp.sum(self.z_in[...], axis=0)
        self.ag_own[...] = total
        self.ag[self.me] = total

        for _, dev in self.plane:
            self.remote(self.ag_own.at[:], self.ag.at[self.me], 2, dev).start()

        sized = self.ag.at[0 : PLANE - 1]
        self.wait(sized, sized, 2)


RED_SCRATCH = [
    pltpu.VMEM((PLANE, 2, UNITS), F32),
    pltpu.VMEM((PLANE - 1, 2, UNITS), F32),
    pltpu.VMEM((2, UNITS), F32),
    pltpu.VMEM((DEV_Z, 2, UNITS), F32),
    pltpu.VMEM((2, UNITS), F32),
    pltpu.SemaphoreType.DMA((3,)),
    pltpu.SemaphoreType.DMA((3,)),
    pltpu.SemaphoreType.REGULAR((4,)),
]
N_RED = len(RED_SCRATCH)


def kernel(pops_hbm, cot_hbm, *refs):
    small_hbm, (out, ag), scratch = refs[:4], refs[4:6], refs[6:]
    gx, gy = lax.axis_index("gx"), lax.axis_index("gy")
    (w1, w1t, w2, w2t, feat0, feat1, qa, qb, hid0, hid1, ra, rb, t0, gh, grad,
     mom0, mom1, post, tot_ref, pops, cot, flags, w_in_t, b_in, w_out, span, in_sem) = scratch[N_RED + 3 * N_EX :]
    get_cot = pltpu.make_async_copy(cot_hbm, cot, in_sem.at[0])
    get_pops = pltpu.make_async_copy(pops_hbm, pops, in_sem.at[1])
    gets = [
        pltpu.make_async_copy(src, dst, in_sem.at[2 + k])
        for k, (src, dst) in enumerate(zip(small_hbm, (flags, w_in_t, b_in, w_out)))
    ]
    for c in gets[1:] + [get_cot, get_pops, gets[0]]:
        c.start()
    reduction = Reduction(scratch[:N_RED], ag, gx, gy)
    ex_c, ex_p, ex_d = [
        Exchange(scratch[N_RED + k * N_EX : N_RED + (k + 1) * N_EX], span) for k in range(3)
    ]
    step_x = {0: gx, 1: lax.rem(gx + 1, 128), -1: lax.rem(gx + 127, 128)}
    step_y = {0: gy, 1: lax.rem(gy + 1, 4), -1: lax.rem(gy + 3, 4)}

    def near(dx, dy):
        return (step_x[dx], step_y[dy])

    barrier = pltpu.get_barrier_semaphore()
    for dx in (1, 0, -1):
        for dy in (1, 0, -1):
            if dx or dy:
                pl.semaphore_signal(
                    barrier, inc=1, device_id=near(dx, dy), device_id_type=MESH
                )
    greeted = 8 + reduction.greet(barrier)
    for c in gets[1:]:
        c.wait()
    tall(w_in_t[...], w1, bias_columns(b_in[...]))
    zero = jnp.zeros((DEPTH - ROWS, GROUPS * LANES), BF)
    for ref in (feat0, feat1, qa, qb):
        ref[ROWS:, :] = zero
    reduction.pay[...] = jnp.zeros((PLANE, 2, UNITS), F32)
    get_pops.wait()
    gets[0].wait()
    get_cot.wait()

    def lanes_of(p, s, h=None):
        first = (2 * p + s) * LANES
        return pl.ds(first, LANES) if h is None else pl.ds(first + h * HALF, HALF)

    def rows_of(s):
        return pl.ds(8 * s, 8)

    halves = [pl.ds(h * HALF, HALF) for h in range(LANES // HALF)]

    def melt_of(p, s, h):
        return flags[p, rows_of(s), h].astype(F32)

    def front(read, p, s, feat, mom_ref, rest):
        for k, h in enumerate(halves):
            f = [read(i, h) for i in range(Q)]
            rho, mom = moments(f)
            for d in range(3):
                mom_ref[2 * p + s, d, :, h] = mom[d]
            eq = equilibrium(rho, mom)
            store_features(
                feat, lanes_of(p, s, k), [f[i] * INV_W[i] - eq[i] for i in range(Q)] + [one]
            )
            if rest is not None:
                rest(h, f, rho, eq)

    def start_a(p, s):
        g = 2 * p + s

        def rest(h, f, rho, eq):
            melt = melt_of(p, s, h) > 0.5
            excess = rho - 1.0
            for i in range(Q):
                val = -0.25 * f[i] + (1.25 * W[i]) * eq[i]
                cz = VELOCITY[i][2]
                if cz:
                    val = val + (0.15 * W[i] * cz) * excess
                post[g, i, :, h] = jnp.where(melt, val, f[OPPOSITE[i]])

        front(lambda i, h: pops[p, i, rows_of(s), h], p, s, feat0, mom0, rest)

    def net_a(p, s):
        lanes = lanes_of(p, s)
        for c in range(0, HID, CHUNK):
            block = pl.ds(c, CHUNK)
            t = jnp.tanh(dot(w1[block, :], feat0[:, lanes]))
            t0[block, lanes] = t
            hid0[block, lanes] = t.astype(BF)

    def end_a(p, s):
        g = 2 * p + s
        learned = dot(w2[...], hid0[:, lanes_of(p, s)])
        melt = melt_of(p, s, slice(None)) > 0.5
        for i in range(Q):
            ex_p.put(i, p, s, post[g, i] + jnp.where(melt, learned[8 * i : 8 * i + 8, :], 0.0))

    def pair_a(s):
        for stage in (start_a, net_a, end_a):
            for p in range(2):
                stage(p, s)

    copies_c, copies_p, copies_d = [], [], []
    flat(w_out[...], w2)
    for p in range(2):
        for i in range(Q):
            wide = cot[p, i].astype(F32)
            for s in range(2):
                ex_c.put(OPPOSITE[i], p, s, wide[8 * s : 8 * s + 8, :])
    one = jnp.ones((8, HALF), F32)
    nil = jnp.zeros((8, HALF), F32)
    pair_a(1)
    pl.semaphore_wait(barrier, greeted)
    copies_c += ex_c.send_half(1, near)
    copies_c += ex_c.send_half(0, near)
    copies_p += ex_p.send_half(1, near)
    pair_a(0)
    copies_p += ex_p.send_half(0, near)
    reduction.tell(0)

    tall(w_out[...], w2t)
    flat(w_in_t[...], w1t)
    tot_ref[...] = jnp.zeros((2, ROWS, UNITS), F32)
    ex_c.finish(near)

    def take(ex, p, s, q):
        for k, h in enumerate(halves):
            melt = melt_of(p, s, h)
            m = []
            for i in range(Q):
                val = ex.get(OPPOSITE[i], p, s, h)
                grad[2 * p + s, i, :, h] = val
                m.append(val * melt)
            store_features(q, lanes_of(p, s, k), m + [nil])

    for p in range(2):
        for s in range(2):
            take(ex_c, p, s, qb)
            lanes = lanes_of(p, s)
            for c in range(0, HID, CHUNK):
                block = pl.ds(c, CHUNK)
                gh[block, lanes] = dot(w2t[block, :], qb[:, lanes])

    @pl.loop(0, HID // 32)
    def _(k):
        block = pl.ds(pl.multiple_of(32 * k, 32), 32)
        t = t0[block, :]
        t0[block, :] = 1.0 - t * t

    reduction.hear(0)
    reduction.tell(1)
    ex_p.finish(near)

    def back(p, s, mom_ref, r, put):
        g = 2 * p + s
        prod = dot(w1t[...], r[:, lanes_of(p, s)])
        for k, h in enumerate(halves):
            melt = melt_of(p, s, h)
            mom = [mom_ref[g, d, :, h] for d in range(3)]
            pr = [prod[8 * i : 8 * i + 8, HALF * k : HALF * (k + 1)] for i in range(Q)]
            m = [grad[g, i, :, h] * melt for i in range(Q)]
            wd = [(1.25 * W[i]) * m[i] - pr[i] for i in range(Q)]
            total = wd[0]
            lift = None
            dj = [None, None, None]
            for a, b in PAIRS:
                both = wd[a] + wd[b]
                total = total + both
                cz = VELOCITY[a][2]
                if cz:
                    term = (0.15 * W[a] * cz) * (m[a] - m[b])
                    lift = term if lift is None else lift + term
                slope = 3.0 * (wd[a] - wd[b]) + 9.0 * along(a, mom) * both
                for d in range(3):
                    c = VELOCITY[a][d]
                    if c == 0:
                        continue
                    if dj[d] is None:
                        dj[d] = slope if c == 1 else -slope
                    else:
                        dj[d] = dj[d] + slope if c == 1 else dj[d] - slope
            drho = total + lift
            dj = [dj[d] - 3.0 * mom[d] * total for d in range(3)]
            put(h, 0, (-0.25) * m[0] + INV_W[0] * pr[0] + drho + (grad[g, 0, :, h] - m[0]))
            for a, b in PAIRS:
                turn = along(a, dj)
                for i, o, base in ((a, b, drho + turn), (b, a, drho - turn)):
                    val = (-0.25) * m[i] + INV_W[i] * pr[i] + base
                    put(h, i, val + (grad[g, o, :, h] - m[o]))

    def start_b(p, s):
        front(lambda i, h: ex_p.get(i, p, s, h), p, s, feat1, mom1, None)

    def net_b(p, s):
        lanes = lanes_of(p, s)
        for c in range(0, HID, CHUNK):
            block = pl.ds(c, CHUNK)
            t = jnp.tanh(dot(w1[block, :], feat1[:, lanes]))
            hid1[block, lanes] = t.astype(BF)
            rb[block, lanes] = (gh[block, lanes] * (1.0 - t * t)).astype(BF)

    def end_b(p, s):
        g = 2 * p + s

        def put(h, i, val):
            if VELOCITY[i][2]:
                post[g, i, :, h] = val
            else:
                ex_d.put(OPPOSITE[i], p, s, val, h)

        back(p, s, mom1, rb, put)
        for i in range(Q):
            if VELOCITY[i][2]:
                ex_d.put(OPPOSITE[i], p, s, post[g, i])

    for s in (1, 0):
        for stage in (start_b, net_b, end_b):
            for p in range(2):
                stage(p, s)
        copies_d += ex_d.send_half(s, near)

    sub = iota((ROWS, UNITS), 0) % 8

    reduction.hear(1)
    reduction.tell(2)

    @pl.loop(0, HID // 256)
    def _(c):
        block = pl.ds(pl.multiple_of(256 * c, 256), 256)
        for k, (left, right) in enumerate(((qb, hid1), (feat1, rb))):
            acc = dot(left[:ROWS, :], right[block, :], NT)
            tot_ref[k] += jnp.where(sub == 2 * c, acc[:, :UNITS], 0.0) + jnp.where(
                sub == 2 * c + 1, acc[:, UNITS:], 0.0
            )

    reduction.hear(2)
    reduction.tell(3)
    ex_d.finish(near)
    for p in range(2):
        for s in range(2):
            take(ex_d, p, s, qa)
            lanes = lanes_of(p, s)
            for c in range(0, HID, CHUNK):
                block = pl.ds(c, CHUNK)
                ra[block, lanes] = (dot(w2t[block, :], qa[:, lanes]) * t0[block, lanes]).astype(BF)

    for k, (left, right) in enumerate(((qa, hid0), (feat0, ra))):
        tot = tot_ref[k]
        for c in range(HID // 256):
            acc = dot(left[:ROWS, :], right[pl.ds(256 * c, 256), :], NT)
            for y in range(2):
                tot = tot + jnp.where(sub == 2 * c + y, acc[:, UNITS * y : UNITS * (y + 1)], 0.0)
        tot = jnp.sum(tot.reshape(20, 8, UNITS), axis=1)
        for j in range(10):
            reduction.pay[10 * (1 - k) + j] = tot[2 * j : 2 * j + 2, :]
    reduction.hear(3)
    reduction.scatter()

    for p in range(2):
        for s in range(2):

            def put(h, i, val):
                post[2 * p + s, i, :, h] = val

            back(p, s, mom0, ra, put)
        for i in range(Q):
            out[p, i] = jnp.concatenate([post[2 * p, i], post[2 * p + 1, i]], axis=0).astype(BF)
    reduction.finish()


def finish_kernel(d0, ag, d0_ref, gin_ref, gb_ref, gout_ref, gin, gb, gout, sem):
    write = pltpu.make_async_copy(d0, d0_ref, sem.at[0])
    write.start()

    def normalized(rows):
        total = jnp.concatenate(rows, axis=0)
        scale = jnp.sum(total * total) / (total.shape[0] * UNITS) + 1e-06
        return total / jnp.sqrt(scale)

    row = [ag[k // 2, k % 2 : k % 2 + 1, :] for k in range(2 * 20)]
    gin[...] = normalized(row[:Q])
    gb[...] = normalized(row[Q : Q + 1])
    gout[...] = normalized(row[Q + 1 : 2 * Q + 1])
    small = [
        pltpu.make_async_copy(src, dst, sem.at[1 + k])
        for k, (src, dst) in enumerate(((gin, gin_ref), (gb, gb_ref), (gout, gout_ref)))
    ]
    for c in small:
        c.start()
    for c in small:
        c.wait()
    write.wait()


def local_step(populations, cotangent, flags, w_in, b_in, w_out):
    vmem = pl.BlockSpec(memory_space=pltpu.VMEM)
    hbm = pl.BlockSpec(memory_space=pltpu.HBM)
    cells = GROUPS * LANES
    d0, ag = pl.pallas_call(
        kernel,
        out_shape=(
            pltpu.VMEM((2, Q, 16, LANES), BF),
            pltpu.VMEM((PLANE, 2, UNITS), F32),
        ),
        in_specs=[hbm] * 6,
        out_specs=(vmem, vmem),
        scratch_shapes=RED_SCRATCH
        + EX_SCRATCH * 3
        + [
            pltpu.VMEM((HID, DEPTH), BF),
            pltpu.VMEM((ROWS, HID), BF),
            pltpu.VMEM((ROWS, HID), BF),
            pltpu.VMEM((HID, DEPTH), BF),
            pltpu.VMEM((DEPTH, cells), BF),
            pltpu.VMEM((DEPTH, cells), BF),
            pltpu.VMEM((DEPTH, cells), BF),
            pltpu.VMEM((DEPTH, cells), BF),
            pltpu.VMEM((HID, cells), BF),
            pltpu.VMEM((HID, cells), BF),
            pltpu.VMEM((HID, cells), BF),
            pltpu.VMEM((HID, cells), BF),
            pltpu.VMEM((HID, cells), F32),
            pltpu.VMEM((HID, cells), F32),
            pltpu.VMEM((GROUPS, Q, 8, LANES), F32),
            pltpu.VMEM((GROUPS, 3, 8, LANES), F32),
            pltpu.VMEM((GROUPS, 3, 8, LANES), F32),
            pltpu.VMEM((GROUPS, Q, 8, LANES), F32),
            pltpu.VMEM((2, ROWS, UNITS), F32),
            pltpu.VMEM((2, Q, 16, LANES), F32),
            pltpu.VMEM((2, Q, 16, LANES), BF),
            pltpu.VMEM((2, 16, LANES), jnp.int32),
            pltpu.VMEM((Q, UNITS), BF),
            pltpu.VMEM((1, UNITS), F32),
            pltpu.VMEM((Q, UNITS), BF),
            pltpu.VMEM((208, LANES), F32),
            pltpu.SemaphoreType.DMA((6,)),
        ],
        compiler_params=pltpu.CompilerParams(
            collective_id=0, has_side_effects=True, vmem_limit_bytes=66650112
        ),
    )(populations, cotangent, flags, w_in.T, b_in.reshape(1, UNITS), w_out)
    return pl.pallas_call(
        finish_kernel,
        out_shape=(
            jax.ShapeDtypeStruct((2, Q, 16, LANES), BF),
            jax.ShapeDtypeStruct((Q, UNITS), F32),
            jax.ShapeDtypeStruct((1, UNITS), F32),
            jax.ShapeDtypeStruct((Q, UNITS), F32),
        ),
        in_specs=[vmem] * 2,
        out_specs=(hbm,) * 4,
        scratch_shapes=[
            pltpu.VMEM((Q, UNITS), F32),
            pltpu.VMEM((1, UNITS), F32),
            pltpu.VMEM((Q, UNITS), F32),
            pltpu.SemaphoreType.DMA((4,)),
        ],
        compiler_params=pltpu.CompilerParams(vmem_limit_bytes=1024 * 1024),
    )(d0, ag)


def shards(populations, cotangent, flags, w_in, b_in, w_out):
    d0, grad_in, grad_b, grad_out = local_step(populations, cotangent, flags, w_in, b_in, w_out)
    return d0, grad_in.T, grad_b.reshape(UNITS), grad_out


def solution(mesh):
    placed = (
        P("gx", None, "gy", None),
        P("gx", None, "gy", None),
        P("gx", "gy", None),
        P(),
        P(),
        P(),
    )
    return jax.shard_map(
        shards,
        mesh=mesh,
        in_specs=placed,
        out_specs=(P("gx", None, "gy", None), P(), P(), P()),
        check_vma=False,
    )
```
